128 devices in a mesh: dom: 16 (over x, y), blk: 8 (over z, core).
Axes of the slice: x: 4, y: 4, z: 4, core: 2. Of those that a mesh axis runs over, the one named last changes fastest.
Arguments:
- node_features: bfloat16 [32768, 512], P(('dom', 'blk')), may hold values from -6 to 6
- norm_gain: float32 [512], replicated, may hold values from 0.25 to 1.75
- w_query: bfloat16 [512, 512], replicated, may hold values from -0.25 to 0.25
- w_key: bfloat16 [512, 512], replicated, may hold values from -0.25 to 0.25
- w_value: bfloat16 [512, 512], replicated, may hold values from -0.25 to 0.25
- w_out: bfloat16 [512, 512], replicated, may hold values from -1.5 to 1.5
- w_message: bfloat16 [512, 512], replicated, may hold values from -1 to 1
- node_cluster: int32 [32768], P(('dom', 'blk')), may hold values from 0 to 15
- block_pattern: int32 [128, 8], P(('dom', 'blk')), may hold values from 0 to 1, as said below
- send_rows: int32 [2048, 128], P(('dom', 'blk')), may hold values from 0 to 255
- send_counts: int32 [2048], P(('dom', 'blk')), may hold values from 32 to 128, as said below
- edge_src: int32 [524288], P(('dom', 'blk')), may hold values from 0 to 2047
- edge_dst: int32 [524288], P(('dom', 'blk')), may hold values from 0 to 255
- out_grad: bfloat16 [32768, 512], P(('dom', 'blk')), may hold values from -6 to 6
Outputs:
- layer_out: bfloat16 [32768, 512], P(('dom', 'blk'))
- feature_grad: bfloat16 [32768, 512], P(('dom', 'blk'))
- weight_grads: float32 [5, 512, 512], replicated
- gain_grad: float32 [512], replicated
The draws below stay inside these ranges and needn't reach their ends.
Inputs may be any that keep to these rules, and one draw needn't show every extreme that they name: `block_pattern`: row g has a 1 at column (g mod 8); other entries are 0 or 1. `send_counts`: entry g * 16 + p is how many leading slots of device g's block to dom peer p are live; every device has one peer whose block has all 128 slots live.
All inputs are finite; a program needn't handle non-finite values.
Results may differ from the reference program's by a relative error of at most 0.013.
Values may be sent and summed in bfloat16 or wider, within the bound.
No kernel may reach another device: no remote copies, remote signals or barrier semaphores. Data moves between devices by JAX's collectives and lax.ppermute only.
A program may use at most 128 MiB of HBM per device.

```python
import math
import jax
import jax.numpy as jnp
import numpy as np
from jax import lax

D = 512
HEADS = 8
HEAD_DIM = 64
ROWS = 256
CLUSTERS = 16
CAP = 128
EDGES = 4096
NODES = 32768
N_DOM = 16
N_BLK = 8


def draw_block_pattern(key, part):
    random_bits = jax.random.randint(key, (N_DOM * N_BLK, N_BLK), 0, 2)
    own_column = (jnp.arange(N_DOM * N_BLK) % N_BLK)[:, None] == jnp.arange(N_BLK)[None, :]
    return jnp.where(own_column, 1, random_bits).astype(jnp.int32)


def draw_send_counts(key, part):
    first_key, second_key = jax.random.split(key)
    drawn = jax.random.randint(first_key, (N_DOM * N_BLK, N_DOM), CAP // 4, CAP + 1)
    full_peer = jax.random.randint(second_key, (N_DOM * N_BLK, 1), 0, N_DOM)
    drawn = jnp.where(jnp.arange(N_DOM)[None, :] == full_peer, CAP, drawn)
    return drawn.reshape(-1).astype(jnp.int32)


def set_ends(result, key, least, high):
    longest = result.shape.index(max(result.shape))
    spots = []
    for shift in (0, 1):
        where = [jax.random.randint(jax.random.fold_in(key, axis), (), 0, length) for axis, length in enumerate(result.shape)]
        where[longest] = (where[longest] + shift) % result.shape[longest]
        spots.append(tuple(where))
    return result.at[spots[0]].set(least).at[spots[1]].set(high)


def block_levels(stream_key, dims, cuts, low, largest):
    def one(dim, shards_of):
        draws = jax.random.uniform(jax.random.fold_in(jax.random.fold_in(stream_key, 6), dim), (shards_of,), jnp.float32, low / len(cuts), largest / len(cuts))
        return jnp.repeat(jnp.exp(draws), dims[dim] // shards_of).reshape((-1,) + (1,) * (len(dims) - dim - 1))

    level = one(*cuts[0])
    for cut in cuts[1:]:
        level = level * one(*cut)
    return level


def rank_bounds(number_of, lean):
    portions = [(1 << 20) // math.isqrt(standing ** lean) + 1 for standing in range(1, number_of + 1)]
    width = 1 + sum(portions) // (1 << 30)
    return np.cumsum(np.array([max(1, weight // width) for weight in portions]))


def ranked(rng, dims, number_of, slope):
    grid = rank_bounds(number_of, slope)
    pick = jax.random.randint(jax.random.fold_in(rng, 1), dims, 0, int(grid[number_of - 1]))
    grade = jnp.searchsorted(jnp.asarray(grid, jnp.int32), pick, side="right")
    return jax.random.permutation(jax.random.fold_in(rng, 2), number_of)[grade].astype(jnp.int32)


def gaussian(own_key, dims, width, bound, shards=(), held_as=jnp.bfloat16):
    level = block_levels(own_key, dims, shards, -0.22, 0.18) if shards else 1.0
    result = jax.random.normal(own_key, dims, jnp.float32) * width * level
    return jnp.minimum(jnp.maximum(result, -bound), bound).astype(held_as)


def setup_inputs(seed: int = 0) -> dict:
    streams_of = jax.random.split(jax.random.key(seed), 15)
    return {
        "node_features": gaussian(streams_of[0], (NODES, D), 1.0, 6.0, ((0, 128),)),
        "norm_gain": jnp.clip(1.0 + 0.15 * jax.random.normal(streams_of[1], (D,), jnp.float32), 0.25, 1.75),
        "w_query": gaussian(streams_of[2], (D, D), D ** -0.5, 0.25),
        "w_key": gaussian(streams_of[3], (D, D), D ** -0.5, 0.25),
        "w_value": gaussian(streams_of[4], (D, D), D ** -0.5, 0.25),
        "w_out": gaussian(streams_of[5], (D, D), (D // 32) ** -0.5, 1.5),
        "w_message": gaussian(streams_of[6], (D, D), (D // 16) ** -0.5, 1.0),
        "node_cluster": set_ends(jax.random.randint(streams_of[7], (NODES,), 0, CLUSTERS), jax.random.fold_in(streams_of[7], 1), 0, CLUSTERS - 1).astype(jnp.int32),
        "block_pattern": draw_block_pattern(jax.random.fold_in(streams_of[14], 71), 0),
        "send_rows": set_ends(jax.random.randint(streams_of[9], (N_DOM * N_BLK * N_DOM, CAP), 0, ROWS), jax.random.fold_in(streams_of[9], 1), 0, ROWS - 1).astype(jnp.int32),
        "send_counts": draw_send_counts(jax.random.fold_in(streams_of[14], 71), 0),
        "edge_src": set_ends(jax.random.randint(streams_of[11], (N_DOM * N_BLK * EDGES,), 0, N_DOM * CAP), jax.random.fold_in(streams_of[11], 1), 0, (N_DOM * CAP) - 1).astype(jnp.int32),
        "edge_dst": set_ends(ranked(streams_of[12], (N_DOM * N_BLK * EDGES,), ROWS, 2), jax.random.fold_in(streams_of[12], 3), 0, ROWS - 1).astype(jnp.int32),
        "out_grad": gaussian(streams_of[13], (NODES, D), 1.0, 6.0, ((0, 128),)),
    }


epsilon = 1e-06
score_shift = 8.0

def rounded(array):
    return lax.optimization_barrier(array.astype(jnp.bfloat16))

def rms_norm(features, norm_gain):
    scaling = lax.rsqrt(lax.optimization_barrier(jnp.mean(features * features, axis=-1, keepdims=True)) + epsilon)
    return features * scaling * norm_gain

def head_norm(projected):
    head_view = projected.reshape(projected.shape[0], HEADS, HEAD_DIM)
    scaling = lax.rsqrt(lax.optimization_barrier(jnp.mean(head_view * head_view, axis=-1, keepdims=True)) + epsilon)
    return (head_view * scaling).reshape(projected.shape)

def masked_weights(query_heads, query_labels, key_heads, key_labels, pattern_row):
    owners = jnp.arange(N_BLK * ROWS, dtype=jnp.int32) // ROWS
    block_flags = pattern_row[owners]
    allowed = (query_labels[:, None] == key_labels[None, :]) & (block_flags[None, :] == 1)
    scaling = score_shift / HEAD_DIM
    scores = jnp.einsum('rhe,khe->hrk', query_heads.astype(jnp.float32), key_heads.astype(jnp.float32)) * scaling
    return jnp.where(allowed[None], jnp.exp(scores - score_shift), 0.0)

def group_forward(group):
    query_all, key_all, value_all, label_all, pattern = group

    def one_device(position):
        query_part = lax.dynamic_slice_in_dim(query_all, position * ROWS, ROWS, 0)
        label_part = lax.dynamic_slice_in_dim(label_all, position * ROWS, ROWS, 0)
        weights = masked_weights(query_part, label_part, key_all, label_all, pattern[position])
        denom = lax.optimization_barrier(jnp.sum(weights, axis=2)).T
        numer = jnp.einsum('hrk,khe->rhe', rounded(weights).astype(jnp.float32), value_all.astype(jnp.float32))
        return (numer, denom)
    return lax.map(one_device, jnp.arange(N_BLK, dtype=jnp.int32))

def group_backward(group):
    query_all, key_all, value_all, grad_all, correction_all, label_all, pattern = group
    scaling = score_shift / HEAD_DIM

    def one_device(running, position):
        key_total, value_total = running
        query_part = lax.dynamic_slice_in_dim(query_all, position * ROWS, ROWS, 0)
        grad_part = lax.dynamic_slice_in_dim(grad_all, position * ROWS, ROWS, 0)
        correction_part = lax.dynamic_slice_in_dim(correction_all, position * ROWS, ROWS, 0)
        label_part = lax.dynamic_slice_in_dim(label_all, position * ROWS, ROWS, 0)
        weights = masked_weights(query_part, label_part, key_all, label_all, pattern[position])
        grad_dots = jnp.einsum('rhe,khe->hrk', grad_part.astype(jnp.float32), value_all.astype(jnp.float32))
        slopes = rounded(weights * (grad_dots - correction_part.T[:, :, None])).astype(jnp.float32)
        slope_blocks = slopes.reshape(HEADS, ROWS, N_BLK, ROWS)
        key_blocks = key_all.astype(jnp.float32).reshape(N_BLK, ROWS, HEADS, HEAD_DIM)
        dq_blocks = jnp.einsum('hrbk,bkhe->brhe', slope_blocks, key_blocks) * scaling
        dq_part = lax.optimization_barrier(jnp.sum(rounded(dq_blocks).astype(jnp.float32), axis=0))
        dk_part = jnp.einsum('hrk,rhe->khe', slopes, query_part.astype(jnp.float32)) * scaling
        dv_part = jnp.einsum('hrk,rhe->khe', rounded(weights).astype(jnp.float32), grad_part.astype(jnp.float32))
        key_total = key_total + rounded(dk_part).astype(jnp.float32)
        value_total = value_total + rounded(dv_part).astype(jnp.float32)
        return ((key_total, value_total), dq_part)
    zero_block = jnp.zeros((N_BLK * ROWS, HEADS, HEAD_DIM), jnp.float32)
    (key_total, value_total), dq_parts = lax.scan(one_device, (zero_block, zero_block), jnp.arange(N_BLK, dtype=jnp.int32))
    return (dq_parts.reshape(N_BLK * ROWS, HEADS, HEAD_DIM), key_total, value_total)

def reference(node_features, norm_gain, w_query, w_key, w_value, w_out, w_message, node_cluster, block_pattern, send_rows, send_counts, edge_src, edge_dst, out_grad):
    features = node_features.astype(jnp.float32)
    normed_f, norm_pull = jax.vjp(rms_norm, features, norm_gain)
    normed = rounded(normed_f)
    node_blocks = normed.reshape(N_DOM, N_BLK, ROWS, D)
    row_table = send_rows.reshape(N_DOM, N_BLK, N_DOM, CAP)
    live_table = jnp.arange(CAP, dtype=jnp.int32)[None, None, None, :] < send_counts.reshape(N_DOM, N_BLK, N_DOM)[..., None]
    source_table = edge_src.reshape(N_DOM, N_BLK, EDGES)
    target_table = edge_dst.reshape(N_DOM, N_BLK, EDGES)

    def count_edges(targets):
        return jax.ops.segment_sum(jnp.ones(targets.shape, jnp.float32), targets, ROWS)
    degree = jnp.maximum(jax.vmap(jax.vmap(count_edges))(target_table), 1.0)

    def pick_rows(node_rows, chosen):
        return node_rows[chosen]

    def receive(target):
        chosen = row_table[:, :, target]
        live_now = live_table[:, :, target]
        sent = jax.vmap(jax.vmap(pick_rows))(node_blocks, chosen)
        sent = jnp.where(live_now[..., None], sent, jnp.zeros((), sent.dtype))
        slot_table = jnp.transpose(sent, (1, 0, 2, 3)).reshape(N_BLK, N_DOM * CAP, D)

        def average(table_rows, sources, targets, counts):
            picked = table_rows[sources].astype(jnp.float32)
            return rounded(jax.ops.segment_sum(picked, targets, ROWS) / counts[:, None])
        return jax.vmap(average)(slot_table, source_table[target], target_table[target], degree[target])
    mean_rows = lax.map(receive, jnp.arange(N_DOM, dtype=jnp.int32)).reshape(NODES, D)
    local_term = jnp.dot(mean_rows, w_message, preferred_element_type=jnp.float32)
    query_f, query_pull = jax.vjp(head_norm, jnp.dot(normed, w_query, preferred_element_type=jnp.float32))
    key_f, key_pull = jax.vjp(head_norm, jnp.dot(normed, w_key, preferred_element_type=jnp.float32))
    queries = rounded(query_f)
    keys = rounded(key_f)
    values = rounded(jnp.dot(normed, w_value, preferred_element_type=jnp.float32))

    def grouped(array):
        return array.reshape(N_DOM, N_BLK * ROWS, HEADS, HEAD_DIM)
    labels = node_cluster.reshape(N_DOM, N_BLK * ROWS)
    pattern = block_pattern.reshape(N_DOM, N_BLK, N_BLK)
    numer, denom = lax.map(group_forward, (grouped(queries), grouped(keys), grouped(values), labels, pattern))
    numer = numer.reshape(NODES, HEADS, HEAD_DIM)
    denom = denom.reshape(NODES, HEADS)
    attn_heads = rounded(numer / denom[..., None])
    attn_rows = attn_heads.reshape(NODES, D)
    attn_proj = jnp.dot(attn_rows, w_out, preferred_element_type=jnp.float32)
    layer_out = (features + local_term + attn_proj).astype(jnp.bfloat16)
    grad_attn = jnp.dot(out_grad, w_out.T, preferred_element_type=jnp.float32).reshape(NODES, HEADS, HEAD_DIM)
    grad_heads = rounded(grad_attn / denom[..., None])
    correction = lax.optimization_barrier(jnp.sum(grad_attn * attn_heads.astype(jnp.float32), axis=-1)) / denom
    dq_heads, dk_heads, dv_heads = lax.map(group_backward, (grouped(queries), grouped(keys), grouped(values), grouped(grad_heads), correction.reshape(N_DOM, N_BLK * ROWS, HEADS), labels, pattern))
    dquery = rounded(query_pull(dq_heads.reshape(NODES, D))[0])
    dkey = rounded(key_pull(dk_heads.reshape(NODES, D))[0])
    dvalue = rounded(dv_heads.reshape(NODES, D))
    dmessage = rounded(jnp.dot(out_grad, w_message.T, preferred_element_type=jnp.float32) / degree.reshape(NODES)[:, None])
    message_blocks = dmessage.reshape(N_DOM, N_BLK, ROWS, D)

    def give_back(running, target):

        def per_device(message_rows, sources, targets):
            return rounded(jax.ops.segment_sum(message_rows[targets].astype(jnp.float32), sources, N_DOM * CAP)).astype(jnp.float32)
        slot_grads = jax.vmap(per_device)(message_blocks[target], source_table[target], target_table[target])
        returned = jnp.transpose(slot_grads.reshape(N_BLK, N_DOM, CAP, D), (1, 0, 2, 3))
        returned = jnp.where(live_table[:, :, target][..., None], returned, 0.0)

        def scatter_rows(grad_rows, chosen):
            return jax.ops.segment_sum(grad_rows, chosen, ROWS)
        return (running + jax.vmap(jax.vmap(scatter_rows))(returned, row_table[:, :, target]), None)
    halo_grad, unused = lax.scan(give_back, jnp.zeros((N_DOM, N_BLK, ROWS, D), jnp.float32), jnp.arange(N_DOM, dtype=jnp.int32))
    dnormed = jnp.dot(dquery, w_query.T, preferred_element_type=jnp.float32)
    dnormed = dnormed + jnp.dot(dkey, w_key.T, preferred_element_type=jnp.float32)
    dnormed = dnormed + jnp.dot(dvalue, w_value.T, preferred_element_type=jnp.float32)
    dnormed = dnormed + halo_grad.reshape(NODES, D)
    dfeatures, gain_grad = norm_pull(dnormed)
    feature_grad = (out_grad.astype(jnp.float32) + dfeatures).astype(jnp.bfloat16)
    weight_grads = jnp.stack([jnp.dot(normed.T, dquery, preferred_element_type=jnp.float32), jnp.dot(normed.T, dkey, preferred_element_type=jnp.float32), jnp.dot(normed.T, dvalue, preferred_element_type=jnp.float32), jnp.dot(attn_rows.T, out_grad, preferred_element_type=jnp.float32), jnp.dot(mean_rows.T, out_grad, preferred_element_type=jnp.float32)])
    return (layer_out, feature_grad, weight_grads, gain_grad)
```

```python
import math

import jax
import jax.numpy as jnp
from jax import lax
from jax.experimental import pallas as pl
from jax.experimental.pallas import tpu as pltpu
from jax.sharding import PartitionSpec as P

F32 = jnp.float32
BF16 = jnp.bfloat16
EPS = 1e-06
D = 512
ROWS = 256
HEAD = 64
BLK = 8
DOM = 16
CAP = 128
SLOTS = DOM * CAP
EDGES = 4096
PAY = ROWS + 16
LOG2E = math.log2(math.e)
SCORE_MUL = LOG2E / 8.0
SCORE_SUB = (8.0 + 128.0) * LOG2E

NT = (((1,), (1,)), ((), ()))
NN = (((1,), (0,)), ((), ()))


def dot(a, b, dims=NN):
    return lax.dot_general(a, b, dims, preferred_element_type=F32)


def call(body, out_shape, scratch=(), smem=0, n_in=0):
    specs = [pl.BlockSpec(memory_space=pltpu.SMEM)] * smem + [pl.BlockSpec(memory_space=pltpu.VMEM)] * n_in
    return pl.pallas_call(
        body,
        out_shape=out_shape,
        in_specs=specs,
        out_specs=jax.tree.map(lambda _: pl.BlockSpec(memory_space=pltpu.VMEM), out_shape),
        scratch_shapes=list(scratch),
    )


def shape(dims, dtype):
    return jax.ShapeDtypeStruct(dims, dtype)


def norm_body(x_ref, gain_ref, label_ref, pattern_ref, out_ref):
    x = x_ref[...].astype(F32)
    scale = lax.rsqrt(jnp.mean(x * x, axis=-1, keepdims=True) + EPS)
    out_ref[0:ROWS, :] = (x * scale * gain_ref[...]).astype(BF16)
    row = lax.broadcasted_iota(jnp.int32, (16, ROWS), 0)
    labels = jnp.broadcast_to(label_ref[...].astype(F32), (16, ROWS))
    pattern = jnp.broadcast_to(pattern_ref[...].astype(F32), (16, ROWS))
    tail = jnp.where(row == 0, labels, jnp.where(row == 1, pattern, 0.0))
    out_ref[ROWS:PAY, 0:ROWS] = tail.astype(BF16)
    out_ref[ROWS:PAY, ROWS:D] = jnp.zeros((16, D - ROWS), BF16)


def outgoing_body(counts_ref, pay_ref, rows_ref, out_ref):
    normed = pay_ref[0:ROWS, :]
    columns = jnp.transpose(rows_ref[...].astype(F32))
    lane = lax.broadcasted_iota(jnp.int32, (CAP, ROWS), 1).astype(F32)
    slot = lax.broadcasted_iota(jnp.int32, (CAP, ROWS), 0)
    for p in range(DOM):
        hit = (lane == columns[:, p : p + 1]) & (slot < counts_ref[p])
        out_ref[p] = dot(jnp.where(hit, 1.0, 0.0).astype(BF16), normed).astype(BF16)


E_STEP = 512


def edges_body(src_ref, dst_ref, grad_ref, w_ref, counts_t_ref, degree_ref, slots_ref, acc_ref):
    low_row = lax.broadcasted_iota(jnp.int32, (512, E_STEP), 0)
    high_row = lax.broadcasted_iota(jnp.int32, (1024, E_STEP), 0)
    for step in range(EDGES // E_STEP):
        src = src_ref[step : step + 1, :]
        dst = dst_ref[step : step + 1, :]
        low = jnp.where(low_row == (src & 511), 1.0, 0.0).astype(BF16)
        high = jnp.where(high_row == ((src >> 9) * 256 + dst), 1.0, 0.0).astype(BF16)
        part = dot(low, high, NT)
        if step == 0:
            acc_ref[...] = part
        else:
            acc_ref[...] += part
    counts = acc_ref[...]
    per_row = jnp.sum(counts, axis=0, keepdims=True)
    per_row = per_row[:, 0:256] + per_row[:, 256:512] + per_row[:, 512:768] + per_row[:, 768:1024]
    degree = jnp.transpose(jnp.broadcast_to(jnp.maximum(per_row, 1.0), (128, ROWS)))
    degree_ref[...] = degree
    counts_t_ref[...] = jnp.transpose(counts).astype(BF16)
    counts = counts.astype(BF16)
    inverse = 1.0 / degree[:, 0:1]
    message = (dot(grad_ref[...], w_ref[...], NT) * inverse).astype(BF16)
    for high in range(4):
        part = dot(counts[:, high * 256 : (high + 1) * 256], message).astype(BF16)
        for k in range(4):
            slots_ref[high * 4 + k] = part[k * CAP : (k + 1) * CAP, :]


def mean_body(own_ref, counts_t_ref, degree_ref, table_ref, x_ref, w_ref, mine_ref, other_ref, base_ref, means_ref):
    total = jnp.zeros((ROWS, D), F32)
    for high in range(4):
        table = jnp.concatenate([table_ref[high * 4 + k] for k in range(4)], axis=0)
        total = total + dot(counts_t_ref[high * 256 : (high + 1) * 256, :], table)
    mean = total / degree_ref[:, 0:1]
    mean_rows = mean.astype(BF16)
    base_ref[...] = x_ref[...].astype(F32) + dot(mean_rows, w_ref[...])
    turned = jnp.transpose(mean_rows.astype(F32)).astype(BF16)
    for h in range(BLK):
        means_ref[h] = turned[h * HEAD : (h + 1) * HEAD, :]
    z, core = own_ref[0], own_ref[1]
    for dz in range(4):
        chip = ((z + dz) & 3) * 2
        mine_ref[dz] = means_ref[chip + core]
        other_ref[dz] = means_ref[chip + (1 - core)]


def attention_body(
    source_ref, na_ref, nb_ref, ga_ref, gb_ref, wqkv_ref, wo_ref,
    paya_ref, payb_ref, dw_ref,
    y_ref, s_ref, qaug_ref, kaug_ref, vaug_ref, kt_ref, vt_ref, w_ref, num_ref, dqt_ref, dq_ref, dk_ref, dv_ref, at_ref, gat_ref,
):
    lane = lax.broadcasted_iota(jnp.int32, (ROWS, 128), 1)
    left = lane < HEAD
    bits = []

    for r in range(BLK):
        n_ref, g_ref = (na_ref, ga_ref) if r < 4 else (nb_ref, gb_ref)
        part = n_ref[r % 4]
        normed = part[0:ROWS, :]
        tail = part[ROWS:PAY, :].astype(F32)
        projected = dot(normed, wqkv_ref[...])
        qk = projected[:, 0:128]
        square = qk * qk
        scale_q = lax.rsqrt(jnp.sum(jnp.where(left, square, 0.0), axis=-1, keepdims=True) * (1.0 / HEAD) + EPS)
        scale_k = lax.rsqrt(jnp.sum(jnp.where(left, 0.0, square), axis=-1, keepdims=True) * (1.0 / HEAD) + EPS)
        scale = jnp.where(left, scale_q, scale_k)
        y = qk * scale
        y_ref[r] = y
        s_ref[r] = scale
        label = jnp.transpose(jnp.broadcast_to(tail[0:1, 0:ROWS], (8, ROWS)))[:, 0:1]
        one_hot = jnp.where((lane - HEAD).astype(F32) == label, 32.0, 0.0)
        qaug_ref[r] = jnp.where(left, y, one_hot).astype(BF16)
        turned = pltpu.roll(y, HEAD, 1)
        kaug_ref[r] = jnp.where(left, turned, one_hot).astype(BF16)
        kt_ref[r] = jnp.transpose(turned)[0:HEAD, :].astype(BF16)
        value = jnp.where(left, projected[:, 128:256], jnp.where(lane < HEAD + 2, 1.0, 0.0))
        vaug_ref[r] = value.astype(BF16)
        vt_ref[r] = jnp.transpose(value).astype(BF16)
        gat_ref[r] = dot(wo_ref[...], g_ref[r % 4], NT)
        flags = jnp.where(tail[1:2, 0:128] == 1.0, 1 << jnp.minimum(lane[0:1, :], 8), 0)
        bits.append(jnp.sum(flags.astype(F32)).astype(jnp.int32))
        dk_ref[r] = jnp.zeros((ROWS, 128), F32)
        dv_ref[r] = jnp.zeros((ROWS, 128), F32)

    def query_block(i, bits_i):
        num_ref[...] = jnp.zeros((128, ROWS), F32)
        dqt_ref[...] = jnp.zeros((HEAD, ROWS), F32)

        def forward(j, carry):
            @pl.when(((bits_i >> source_ref[j]) & 1) == 1)
            def _():
                scores = dot(kaug_ref[j], qaug_ref[i], NT)
                weights = jnp.exp2(scores * SCORE_MUL - SCORE_SUB).astype(BF16)
                w_ref[j] = weights
                num_ref[...] += dot(vt_ref[j], weights)
            return carry

        lax.fori_loop(0, BLK, forward, 0)
        inverse = 1.0 / num_ref[HEAD : HEAD + 1, :]
        attn = (num_ref[0:HEAD, :] * inverse).astype(BF16)
        at_ref[i] = attn
        grad_attn = gat_ref[i]
        grad = grad_attn * inverse
        minus = jnp.sum(grad_attn * attn.astype(F32), axis=0, keepdims=True) * (-inverse)
        coarse = minus.astype(BF16).astype(F32)
        row = lax.broadcasted_iota(jnp.int32, (HEAD, ROWS), 0)
        extra = jnp.where(row == 0, coarse, jnp.where(row == 1, minus - coarse, 0.0))
        grad_aug = jnp.concatenate([grad, extra], axis=0)
        grad_rows = jnp.transpose(grad_aug).astype(BF16)
        grad_aug = grad_aug.astype(BF16)

        def backward(j, carry):
            @pl.when(((bits_i >> source_ref[j]) & 1) == 1)
            def _():
                weights = w_ref[j]
                slopes = (weights.astype(F32) * dot(vaug_ref[j], grad_aug)).astype(BF16)
                dqt_ref[...] += dot(kt_ref[j], slopes)
                dk_ref[j] += dot(slopes, qaug_ref[i])
                dv_ref[j] += dot(weights, grad_rows)
            return carry

        lax.fori_loop(0, BLK, backward, 0)
        dq_ref[i] = jnp.transpose(jnp.concatenate([dqt_ref[...], dqt_ref[...]], axis=0))

    for i in range(BLK):
        query_block(i, bits[i])

    dw = jnp.zeros((192, D), F32)
    dwo = jnp.zeros((HEAD, D), F32)
    for r in range(BLK):
        n_ref, g_ref = (na_ref, ga_ref) if r < 4 else (nb_ref, gb_ref)
        pay_ref = paya_ref if r < 4 else payb_ref
        y = y_ref[r]
        grad = jnp.where(left, dq_ref[r], pltpu.roll(dk_ref[r], HEAD, 1)) * (8.0 / HEAD)
        product = y * grad
        mean_q = jnp.sum(jnp.where(left, product, 0.0), axis=-1, keepdims=True) * (1.0 / HEAD)
        mean_k = jnp.sum(jnp.where(left, 0.0, product), axis=-1, keepdims=True) * (1.0 / HEAD)
        first = (s_ref[r] * (grad - y * jnp.where(left, mean_q, mean_k))).astype(BF16)
        attn = at_ref[r].astype(F32)
        attn = jnp.transpose(jnp.concatenate([attn, attn], axis=0))
        second = jnp.where(left, dv_ref[r], attn).astype(BF16)
        pay_ref[r % 4, :, 0:128] = first
        pay_ref[r % 4, :, 128:256] = second
        first_t = jnp.transpose(first.astype(F32)).astype(BF16)
        second_t = jnp.transpose(second.astype(F32)).astype(BF16)
        dw = dw + dot(jnp.concatenate([first_t, second_t[0:HEAD]], axis=0), n_ref[r % 4, 0:ROWS, :])
        dwo = dwo + dot(second_t[HEAD:128], g_ref[r % 4])
    dw_ref[0:192, :] = dw
    dw_ref[192:256, :] = dwo


def chunks_body(m0_ref, m1_ref, m2_ref, m3_ref, ga_ref, gb_ref, dw_ref, out_ref):
    total = jnp.zeros((HEAD, D), F32)
    for dz, m_ref in enumerate((m0_ref, m1_ref, m2_ref, m3_ref)):
        total = total + dot(m_ref[0], ga_ref[dz]) + dot(m_ref[1], gb_ref[dz])
    for a in range(4):
        for b in range(4):
            out_ref[a * 4 + b, 0:64, :] = dw_ref[a * 64 : (a + 1) * 64, b * 128 : (b + 1) * 128].astype(BF16)
            out_ref[a * 4 + b, 64:80, :] = total[a * 16 : (a + 1) * 16, b * 128 : (b + 1) * 128].astype(BF16)


def chunk_sum_body(in_ref, out_ref):
    total = in_ref[0].astype(F32)
    for p in range(1, DOM):
        total = total + in_ref[p].astype(F32)
    total = total.astype(BF16)
    for p in range(DOM):
        out_ref[p] = total


def rows_body(
    own_ref, counts_ref, r0_ref, r1_ref, r2_ref, r3_ref, back_ref, rows_ref, base_ref, x_ref, gain_ref, grad_ref,
    wq_ref, wk_ref, wv_ref, wo_ref, out_ref, feature_ref, gain_grad_ref, dq_ref, dk_ref, dv_ref, at_ref,
):
    left = lax.broadcasted_iota(jnp.int32, (ROWS, 128), 1) < HEAD
    z, core = own_ref[0], own_ref[1]
    even = core == 0
    for dz, r_ref in enumerate((r0_ref, r1_ref, r2_ref, r3_ref)):
        chip = (z + dz) & 3
        one, two = r_ref[0].astype(F32), r_ref[1].astype(F32)
        low, high = jnp.where(even, one, two), jnp.where(even, two, one)
        low0, low1 = low[:, 0:128], low[:, 128:256]
        high0, high1 = high[:, 0:128], high[:, 128:256]
        dq_ref[chip] = jnp.where(left, low0, pltpu.roll(high0, HEAD, 1)).astype(BF16)
        dk_ref[chip] = jnp.where(left, pltpu.roll(low0, HEAD, 1), high0).astype(BF16)
        dv_ref[chip] = jnp.where(left, low1, pltpu.roll(high1, HEAD, 1)).astype(BF16)
        at_ref[chip] = jnp.where(left, pltpu.roll(low1, HEAD, 1), high1).astype(BF16)

    def whole(ref):
        return jnp.concatenate([ref[m] for m in range(4)], axis=1)

    out_ref[...] = (base_ref[...] + dot(whole(at_ref), wo_ref[...])).astype(BF16)
    dnormed = dot(whole(dq_ref), wq_ref[...], NT) + dot(whole(dk_ref), wk_ref[...], NT)
    dnormed = dnormed + dot(whole(dv_ref), wv_ref[...], NT)
    row = lax.broadcasted_iota(jnp.int32, (ROWS, CAP), 0)
    slot = lax.broadcasted_iota(jnp.int32, (ROWS, CAP), 1)
    for k in range(4):
        hits = []
        for p in range(4 * k, 4 * k + 4):
            hit = (row == rows_ref[p : p + 1, :]) & (slot < counts_ref[p])
            hits.append(jnp.where(hit, 1.0, 0.0).astype(BF16))
        part = jnp.concatenate([back_ref[p] for p in range(4 * k, 4 * k + 4)], axis=0)
        dnormed = dnormed + dot(jnp.concatenate(hits, axis=1), part)
    x = x_ref[...].astype(F32)
    scale = lax.rsqrt(jnp.mean(x * x, axis=-1, keepdims=True) + EPS)
    gain_grad_ref[...] = jnp.sum(dnormed * (x * scale), axis=0, keepdims=True)
    scaled = dnormed * gain_ref[...]
    inner = jnp.mean(scaled * x, axis=-1, keepdims=True)
    dx = scale * scaled - x * (scale * scale * scale * inner)
    feature_ref[...] = (grad_ref[...].astype(F32) + dx).astype(BF16)


def weights_body(in_ref, out_ref):
    which = pl.program_id(0)
    for t in range(3):
        @pl.when(which == t)
        def _():
            for b in range(4):
                part = jnp.concatenate([in_ref[h, t * 4 + b, 0:64, :].astype(F32) for h in range(BLK)], axis=0)
                out_ref[0, b * 128 : (b + 1) * 128, :] = jnp.transpose(part)

    @pl.when(which == 3)
    def _():
        for h in range(BLK):
            for b in range(4):
                out_ref[0, h * 64 : (h + 1) * 64, b * 128 : (b + 1) * 128] = in_ref[h, 12 + b, 0:64, :].astype(F32)

    @pl.when(which == 4)
    def _():
        for h in range(BLK):
            for a in range(4):
                for b in range(4):
                    top = h * 64 + a * 16
                    out_ref[0, top : top + 16, b * 128 : (b + 1) * 128] = in_ref[h, a * 4 + b, 64:80, :].astype(F32)


def chip_shift(step, swap):
    return [(z * 2 + c, ((z + step) % 4) * 2 + (c ^ swap)) for z in range(4) for c in range(2)]


def along_chips(array, step):
    return lax.ppermute(array, "blk", chip_shift(step, 0))


def other_core(array):
    return lax.ppermute(array, "blk", chip_shift(0, 1))


def gather_blocks(block):
    mine = jnp.stack([block] + [along_chips(block, step) for step in (1, 2, 3)])
    return mine, other_core(mine)


def local(
    x, gain, wq, wk, wv, wo, wm, cluster, pattern, send_rows, send_counts, edge_src, edge_dst, out_grad
):
    me = lax.axis_index("blk").astype(jnp.int32)
    z, core = me // 2, me % 2
    own = jnp.stack([z, core])
    r = jnp.arange(BLK, dtype=jnp.int32)
    source = ((z - r % 4) % 4) * 2 + (core ^ (r // 4))
    gain_row = gain.reshape(1, D)

    ga, gb = gather_blocks(out_grad)

    pattern_row = jnp.pad(pattern, ((0, 0), (0, ROWS - BLK)))
    pay = call(norm_body, shape((PAY, D), BF16), n_in=4)(x, gain_row, cluster.reshape(1, ROWS), pattern_row)
    na, nb = gather_blocks(pay)
    outgoing = call(outgoing_body, shape((DOM, CAP, D), BF16), smem=1, n_in=2)(send_counts, pay, send_rows)
    incoming = lax.all_to_all(outgoing, "dom", split_axis=0, concat_axis=0, tiled=True)

    counts_t, degree, slot_grads = call(
        edges_body,
        (shape((1024, 512), BF16), shape((ROWS, 128), F32), shape((DOM, CAP, D), BF16)),
        scratch=[pltpu.VMEM((512, 1024), F32)],
        n_in=4,
    )(edge_src.reshape(EDGES // E_STEP, E_STEP), edge_dst.reshape(EDGES // E_STEP, E_STEP), out_grad, wm)

    mine, other, base = call(
        mean_body,
        (shape((4, HEAD, ROWS), BF16), shape((4, HEAD, ROWS), BF16), shape((ROWS, D), F32)),
        scratch=[pltpu.VMEM((BLK, HEAD, ROWS), BF16)],
        smem=1,
        n_in=5,
    )(own, counts_t, degree, incoming, x, wm)
    back = lax.all_to_all(slot_grads, "dom", split_axis=0, concat_axis=0, tiled=True)
    other = other_core(other)
    means = [jnp.stack([mine[dz], other[dz]]) for dz in range(4)]
    means = [means[0]] + [along_chips(means[dz], dz) for dz in (1, 2, 3)]

    def head_columns(w):
        return lax.dynamic_slice(w, (0, me * HEAD), (D, HEAD))

    wqkv = jnp.concatenate(
        [head_columns(wq), head_columns(wk), head_columns(wv), jnp.zeros((D, HEAD), BF16)], axis=1
    )
    wo_head = lax.dynamic_slice(wo, (me * HEAD, 0), (HEAD, D))
    pay_a, pay_b, dw = call(
        attention_body,
        (shape((4, ROWS, 256), BF16), shape((4, ROWS, 256), BF16), shape((256, D), F32)),
        scratch=[
            pltpu.VMEM((BLK, ROWS, 128), F32),
            pltpu.VMEM((BLK, ROWS, 128), F32),
            pltpu.VMEM((BLK, ROWS, 128), BF16),
            pltpu.VMEM((BLK, ROWS, 128), BF16),
            pltpu.VMEM((BLK, ROWS, 128), BF16),
            pltpu.VMEM((BLK, HEAD, ROWS), BF16),
            pltpu.VMEM((BLK, 128, ROWS), BF16),
            pltpu.VMEM((BLK, ROWS, ROWS), BF16),
            pltpu.VMEM((128, ROWS), F32),
            pltpu.VMEM((HEAD, ROWS), F32),
            pltpu.VMEM((BLK, ROWS, 128), F32),
            pltpu.VMEM((BLK, ROWS, 128), F32),
            pltpu.VMEM((BLK, ROWS, 128), F32),
            pltpu.VMEM((BLK, HEAD, ROWS), BF16),
            pltpu.VMEM((BLK, HEAD, ROWS), F32),
        ],
        smem=1,
        n_in=6,
    )(source, na, nb, ga, gb, wqkv, wo_head)

    chunks = call(chunks_body, shape((DOM, 80, 128), BF16), n_in=7)(*means, ga, gb, dw)
    chunks = lax.all_to_all(chunks, "dom", split_axis=0, concat_axis=0, tiled=True)
    chunks = call(chunk_sum_body, shape((DOM, 80, 128), BF16), n_in=1)(chunks)
    chunks = lax.all_to_all(chunks, "dom", split_axis=0, concat_axis=0, tiled=True)
    chunks = lax.all_gather(chunks.reshape(DOM * 80, 128), "blk", axis=0, tiled=True)
    weight_grads = pl.pallas_call(
        weights_body,
        grid=(5,),
        out_shape=shape((5, D, D), F32),
        in_specs=[pl.BlockSpec((BLK, DOM, 80, 128), lambda t: (0, 0, 0, 0))],
        out_specs=pl.BlockSpec((1, D, D), lambda t: (t, 0, 0)),
    )(chunks.reshape(BLK, DOM, 80, 128))

    pay_b = other_core(pay_b)
    results = [jnp.stack([pay_a[dz], pay_b[dz]]) for dz in range(4)]
    results = [results[0]] + [along_chips(results[dz], -dz) for dz in (1, 2, 3)]
    layer_out, feature_grad, gain_part = call(
        rows_body,
        (shape((ROWS, D), BF16), shape((ROWS, D), BF16), shape((1, D), F32)),
        scratch=[pltpu.VMEM((4, ROWS, 128), BF16)] * 4,
        smem=2,
        n_in=14,
    )(own, send_counts, *results, back, send_rows, base, x, gain_row, out_grad, wq, wk, wv, wo)
    gain_parts = jnp.broadcast_to(gain_part.reshape(1, 4, 128), (DOM * BLK, 4, 128))
    gain_parts = lax.all_to_all(gain_parts, ("dom", "blk"), split_axis=0, concat_axis=0, tiled=True)
    gain_grad = jnp.sum(gain_parts, axis=0).reshape(D)
    return layer_out, feature_grad, weight_grads, gain_grad


def solution(mesh):
    both = ("dom", "blk")
    placed = (
        P(both, None), P(), P(), P(), P(), P(), P(), P(both), P(both, None), P(both, None), P(both), P(both), P(both),
        P(both, None),
    )
    return jax.shard_map(
        local,
        mesh=mesh,
        in_specs=placed,
        out_specs=(P(both, None), P(both, None), P(), P()),
        check_vma=False,
    )
```

```python
import math

import jax
import jax.numpy as jnp
from jax import lax
from jax.experimental import pallas as pl
from jax.experimental.pallas import tpu as pltpu
from jax.sharding import PartitionSpec as P

F32 = jnp.float32
BF16 = jnp.bfloat16
EPS = 1e-06
D = 512
ROWS = 256
HEAD = 64
BLK = 8
DOM = 16
CAP = 128
EDGES = 4096
PAY = 2 * ROWS + 16
LOG2E = math.log2(math.e)
SCORE_MUL = LOG2E / 8.0
SCORE_SUB = (8.0 + 256.0) * LOG2E
CHUNK = 80
SPREAD = 4 * CHUNK + 16

NT = (((1,), (1,)), ((), ()))
NN = (((1,), (0,)), ((), ()))


def dot(a, b, dims=NN):
    return lax.dot_general(a, b, dims, preferred_element_type=F32)


def call(body, out_shape, operands, scratch=(), scalars=0, micros=2):
    specs = [pl.BlockSpec(memory_space=pltpu.SMEM)] * scalars
    specs += [pl.BlockSpec(memory_space=pltpu.VMEM)] * (len(operands) - scalars)
    return pl.pallas_call(
        body,
        out_shape=out_shape,
        in_specs=specs,
        out_specs=jax.tree.map(lambda _: pl.BlockSpec(memory_space=pltpu.VMEM), out_shape),
        scratch_shapes=list(scratch),
        cost_estimate=pl.CostEstimate(flops=int(micros * 1e9), transcendentals=0, bytes_accessed=1 << 20),
    )(*operands)


def shape(dims, dtype):
    return jax.ShapeDtypeStruct(dims, dtype)


def position():
    me = lax.axis_index("blk").astype(jnp.int32)
    return lax.shift_right_logical(me, 1), me & 1


def norm_body(pattern_ref, x_ref, gain_ref, label_ref, grad_ref, out_ref):
    x = x_ref[...].astype(F32)
    scale = lax.rsqrt(jnp.mean(x * x, axis=-1, keepdims=True) + EPS)
    out_ref[0:ROWS, :] = (x * scale * gain_ref[...]).astype(BF16)
    out_ref[ROWS : 2 * ROWS, :] = grad_ref[...]
    row = lax.broadcasted_iota(jnp.int32, (16, ROWS), 0)
    lane = lax.broadcasted_iota(jnp.int32, (16, ROWS), 1)
    tail = jnp.where(row == 0, label_ref[...].astype(F32), 0.0)
    for b in range(BLK):
        flag = jnp.where(pattern_ref[0, b] == 1, 1.0, 0.0)
        tail = jnp.where((row == 1 + b) & (lane >= 0), flag, tail)
    out_ref[2 * ROWS : PAY, 0:ROWS] = tail.astype(BF16)
    out_ref[2 * ROWS : PAY, ROWS:D] = jnp.zeros((16, D - ROWS), BF16)


def outgoing_body(counts_ref, pay_ref, rows_ref, out_ref):
    normed = pay_ref[0:ROWS, :]
    columns = jnp.transpose(rows_ref[...].astype(F32))
    lane = lax.broadcasted_iota(jnp.int32, (CAP, ROWS), 1).astype(F32)
    slot = lax.broadcasted_iota(jnp.int32, (CAP, ROWS), 0)
    for p in range(DOM):
        hit = (lane == columns[:, p : p + 1]) & (slot < counts_ref[p])
        out_ref[p] = dot(jnp.where(hit, 1.0, 0.0).astype(BF16), normed).astype(BF16)


E_ROWS = 4


def edges_body(
    src_ref, dst_ref, grad_ref, w_ref, wq_ref, wk_ref, wv_ref, wo_ref,
    counts_t_ref, degree_ref, slots_ref, wqkv_ref, wo_head_ref, acc_ref,
):
    z, core = position()
    for m in range(4):
        @pl.when(z == m)
        def _():
            for k, ref in enumerate((wq_ref, wk_ref, wv_ref)):
                pair = jnp.transpose(ref[:, m * 128 : (m + 1) * 128].astype(F32))
                picked = jnp.where(core == 0, pair[0:HEAD], pair[HEAD:128])
                wqkv_ref[k * HEAD : (k + 1) * HEAD, :] = picked.astype(BF16)
            for c in range(2):
                @pl.when(core == c)
                def _():
                    wo_head_ref[...] = wo_ref[m * 128 + c * HEAD : m * 128 + (c + 1) * HEAD, :]

    low_row = lax.broadcasted_iota(jnp.int32, (512, E_ROWS * 128), 0)
    high_row = lax.broadcasted_iota(jnp.int32, (1024, E_ROWS * 128), 0)
    for step in range(EDGES // (E_ROWS * 128)):
        rows = [step * E_ROWS + k for k in range(E_ROWS)]
        src = jnp.concatenate([src_ref[k : k + 1, :] for k in rows], axis=1)
        dst = jnp.concatenate([dst_ref[k : k + 1, :] for k in rows], axis=1)
        low = jnp.where(low_row == (src & 511), 1.0, 0.0).astype(BF16)
        high = jnp.where(high_row == ((src >> 9) * 256 + dst), 1.0, 0.0).astype(BF16)
        part = dot(low, high, NT)
        if step == 0:
            acc_ref[...] = part
        else:
            acc_ref[...] += part
    counts = acc_ref[...]
    per_row = jnp.sum(counts, axis=0, keepdims=True)
    per_row = per_row[:, 0:256] + per_row[:, 256:512] + per_row[:, 512:768] + per_row[:, 768:1024]
    degree = jnp.transpose(jnp.broadcast_to(jnp.maximum(per_row, 1.0), (128, ROWS)))
    degree_ref[...] = degree
    counts_t_ref[...] = jnp.transpose(counts).astype(BF16)
    counts = counts.astype(BF16)
    inverse = 1.0 / degree[:, 0:1]
    message = (dot(grad_ref[...], w_ref[...], NT) * inverse).astype(BF16)
    for high in range(4):
        part = dot(counts[:, high * 256 : (high + 1) * 256], message).astype(BF16)
        for k in range(4):
            slots_ref[high * 4 + k] = part[k * CAP : (k + 1) * CAP, :]


def mean_body(counts_t_ref, degree_ref, table_ref, x_ref, w_ref, mine_ref, other_ref, base_ref, means_ref):
    total = jnp.zeros((ROWS, D), F32)
    for high in range(4):
        table = jnp.concatenate([table_ref[high * 4 + k] for k in range(4)], axis=0)
        total = total + dot(counts_t_ref[high * 256 : (high + 1) * 256, :], table)
    mean_rows = (total / degree_ref[:, 0:1]).astype(BF16)
    base_ref[...] = x_ref[...].astype(F32) + dot(mean_rows, w_ref[...])
    turned = jnp.transpose(mean_rows.astype(F32)).astype(BF16)
    for h in range(BLK):
        means_ref[h] = turned[h * HEAD : (h + 1) * HEAD, :]
    z, core = position()
    for dz in range(4):
        chip = ((z + dz) & 3) * 2
        mine_ref[dz] = means_ref[chip + core]
        other_ref[dz] = means_ref[chip + (1 - core)]


def attention_body(
    p0_ref, p1_ref, p2_ref, p3_ref, p4_ref, p5_ref, p6_ref, p7_ref, wqkv_ref, wo_ref,
    r0_ref, r1_ref, r2_ref, r3_ref, dw_ref,
    y_ref, s_ref, qt_ref, kt_ref, k_ref, v_ref, vt_ref, w_ref, dq_ref, dk_ref, dv_ref, at_ref, ga_ref,
):
    pays = (p0_ref, p1_ref, p2_ref, p3_ref, p4_ref, p5_ref, p6_ref, p7_ref)
    outs = (r0_ref, r1_ref, r2_ref, r3_ref)
    z, core = position()
    row = lax.broadcasted_iota(jnp.int32, (HEAD, ROWS), 0)
    number = row.astype(F32)

    def head_scale(part):
        return lax.rsqrt(jnp.sum(part * part, axis=0, keepdims=True) * (1.0 / HEAD) + EPS)

    for r in range(BLK):
        pay = pays[r]
        projected = dot(wqkv_ref[...], pay[0:ROWS, :], NT)
        query, key, value = projected[0:HEAD], projected[HEAD:128], projected[128:192]
        scale_q, scale_k = head_scale(query), head_scale(key)
        query, key = query * scale_q, key * scale_k
        y_ref[r, 0:HEAD] = query
        y_ref[r, HEAD:128] = key
        s_ref[r, 0:1] = scale_q
        s_ref[r, 1:2] = scale_k
        tail = pay[2 * ROWS : PAY, 0:ROWS].astype(F32)
        same = jnp.where(number == tail[0:1], 32.0, 0.0)
        sender = ((z - (r & 3)) & 3) * 2 + (core ^ (r >> 2))
        wanted = jnp.concatenate([jnp.zeros((16, ROWS), F32), tail[1:9] * 32.0, jnp.zeros((40, ROWS), F32)], axis=0)
        owner = jnp.where(row == 16 + sender, 32.0, 0.0)
        qt_ref[r] = jnp.concatenate([query, same + wanted], axis=0).astype(BF16)
        key = jnp.concatenate([key, same + owner], axis=0)
        kt_ref[r] = key[0:HEAD].astype(BF16)
        k_ref[r] = jnp.transpose(key).astype(BF16)
        value = jnp.concatenate([value, jnp.where(row < 2, 1.0, 0.0)], axis=0)
        vt_ref[r] = value[0:80].astype(BF16)
        v_ref[r] = jnp.transpose(value).astype(BF16)
        ga_ref[r] = dot(wo_ref[...], pay[ROWS : 2 * ROWS, :], NT)
        dk_ref[r] = jnp.zeros((HEAD, ROWS), F32)
        dv_ref[r] = jnp.zeros((HEAD, ROWS), F32)

    keys_t = jnp.concatenate([kt_ref[j] for j in range(BLK)], axis=1)
    values_t = jnp.concatenate([vt_ref[j] for j in range(BLK)], axis=1)

    def query_block(i, carry):
        query = qt_ref[i]
        for j in range(BLK):
            scores = dot(k_ref[j], query)
            w_ref[j] = jnp.exp2(scores * SCORE_MUL - SCORE_SUB).astype(BF16)
        numer = dot(values_t, w_ref[...].reshape(BLK * ROWS, ROWS))
        inverse = 1.0 / numer[HEAD : HEAD + 1]
        attn = (numer[0:HEAD] * inverse).astype(BF16)
        at_ref[i] = attn
        grad_attn = ga_ref[i]
        minus = jnp.sum(grad_attn * attn.astype(F32), axis=0, keepdims=True) * (-inverse)
        coarse = minus.astype(BF16).astype(F32)
        extra = jnp.where(row == 0, coarse, jnp.where(row == 1, minus - coarse, 0.0))
        grad = jnp.concatenate([grad_attn * inverse, extra], axis=0).astype(BF16)
        dq = jnp.zeros((HEAD, ROWS), F32)
        for j in range(BLK):
            weights = w_ref[j]
            slopes = (weights.astype(F32) * dot(v_ref[j], grad)).astype(BF16)
            dq = dq + dot(kt_ref[j], slopes)
            dk_ref[j] += dot(query[0:HEAD], slopes, NT)
            dv_ref[j] += dot(grad[0:HEAD], weights, NT)
        dq_ref[i] = dq
        return carry

    lax.fori_loop(0, BLK, query_block, 0)

    dw = jnp.zeros((192, D), F32)
    dwo = jnp.zeros((HEAD, D), F32)
    for r in range(BLK):
        pay = pays[r]

        def pull(grad, y, scale):
            grad = grad * (8.0 / HEAD)
            return scale * (grad - y * (jnp.sum(y * grad, axis=0, keepdims=True) * (1.0 / HEAD)))

        dquery = pull(dq_ref[r], y_ref[r, 0:HEAD], s_ref[r, 0:1])
        dkey = pull(dk_ref[r], y_ref[r, HEAD:128], s_ref[r, 1:2])
        first = jnp.concatenate([dquery, dkey], axis=0)
        second = jnp.concatenate([dv_ref[r], at_ref[r].astype(F32)], axis=0)
        outs[r & 3][r >> 2, :, 0:128] = jnp.transpose(first).astype(BF16)
        outs[r & 3][r >> 2, :, 128:256] = jnp.transpose(second).astype(BF16)
        left = jnp.concatenate([first, second[0:HEAD]], axis=0).astype(BF16)
        dw = dw + dot(left, pay[0:ROWS, :])
        dwo = dwo + dot(at_ref[r], pay[ROWS : 2 * ROWS, :])
    dw_ref[0:192, :] = dw
    dw_ref[192:256, :] = dwo


def chunks_body(
    p0_ref, p1_ref, p2_ref, p3_ref, p4_ref, p5_ref, p6_ref, p7_ref, m0_ref, m1_ref, m2_ref, m3_ref, dw_ref, out_ref
):
    pays = (p0_ref, p1_ref, p2_ref, p3_ref, p4_ref, p5_ref, p6_ref, p7_ref)
    total = jnp.zeros((HEAD, D), F32)
    for dz, m_ref in enumerate((m0_ref, m1_ref, m2_ref, m3_ref)):
        for c in range(2):
            total = total + dot(m_ref[c], pays[4 * c + dz][ROWS : 2 * ROWS, :])
    for a in range(4):
        for b in range(4):
            out_ref[a * 4 + b, 0:64, :] = dw_ref[a * 64 : (a + 1) * 64, b * 128 : (b + 1) * 128].astype(BF16)
            out_ref[a * 4 + b, 64:80, :] = total[a * 16 : (a + 1) * 16, b * 128 : (b + 1) * 128].astype(BF16)


def chunk_sum_body(in_ref, out_ref):
    total = in_ref[0].astype(F32)
    for p in range(1, DOM):
        total = total + in_ref[p].astype(F32)
    out_ref[...] = total.astype(BF16)


def spread_body(c0_ref, c1_ref, c2_ref, c3_ref, g0_ref, g1_ref, g2_ref, g3_ref, out_ref, gains_ref):
    z, core = position()
    for dz, g_ref in enumerate((g0_ref, g1_ref, g2_ref, g3_ref)):
        gains_ref[dz] = g_ref[...]
    gain = jnp.zeros((8, 128), F32)
    for b in range(BLK):
        gain = gain + gains_ref[(z - (b >> 1)) & 3, core ^ (b & 1)]
    coarse = gain.astype(BF16).astype(F32)
    fine = (gain - coarse).astype(BF16).astype(F32)
    tail = jnp.concatenate([coarse, fine], axis=0).astype(BF16)
    for p in range(DOM):
        for dz, c_ref in enumerate((c0_ref, c1_ref, c2_ref, c3_ref)):
            out_ref[p, dz * CHUNK : (dz + 1) * CHUNK, :] = c_ref[...]
        out_ref[p, 4 * CHUNK : SPREAD, :] = tail


def rows_body(
    counts_ref, r0_ref, r1_ref, r2_ref, r3_ref, t0_ref, t1_ref, t2_ref, t3_ref, back_ref, rows_ref, base_ref, x_ref,
    gain_ref, grad_ref, wq_ref, wk_ref, wv_ref, wo_ref,
    out_ref, feature_ref, gain_grad_ref, dq_ref, dk_ref, dv_ref, at_ref,
):
    left = lax.broadcasted_iota(jnp.int32, (ROWS, 128), 1) < HEAD
    z, core = position()
    even = core == 0
    for dz, (r_ref, t_ref) in enumerate(zip((r0_ref, r1_ref, r2_ref, r3_ref), (t0_ref, t1_ref, t2_ref, t3_ref))):
        chip = (z + dz) & 3
        one, two = r_ref[0].astype(F32), t_ref[...].astype(F32)
        low, high = jnp.where(even, one, two), jnp.where(even, two, one)
        low0, low1 = low[:, 0:128], low[:, 128:256]
        high0, high1 = high[:, 0:128], high[:, 128:256]
        dq_ref[chip] = jnp.where(left, low0, pltpu.roll(high0, HEAD, 1)).astype(BF16)
        dk_ref[chip] = jnp.where(left, pltpu.roll(low0, HEAD, 1), high0).astype(BF16)
        dv_ref[chip] = jnp.where(left, low1, pltpu.roll(high1, HEAD, 1)).astype(BF16)
        at_ref[chip] = jnp.where(left, pltpu.roll(low1, HEAD, 1), high1).astype(BF16)

    def whole(ref):
        return jnp.concatenate([ref[m] for m in range(4)], axis=1)

    out_ref[...] = (base_ref[...] + dot(whole(at_ref), wo_ref[...])).astype(BF16)
    dnormed = dot(whole(dq_ref), wq_ref[...], NT) + dot(whole(dk_ref), wk_ref[...], NT)
    dnormed = dnormed + dot(whole(dv_ref), wv_ref[...], NT)
    row = lax.broadcasted_iota(jnp.int32, (ROWS, CAP), 0)
    slot = lax.broadcasted_iota(jnp.int32, (ROWS, CAP), 1)
    for k in range(4):
        hits = []
        for p in range(4 * k, 4 * k + 4):
            hit = (row == rows_ref[p : p + 1, :]) & (slot < counts_ref[p])
            hits.append(jnp.where(hit, 1.0, 0.0).astype(BF16))
        part = jnp.concatenate([back_ref[p] for p in range(4 * k, 4 * k + 4)], axis=0)
        dnormed = dnormed + dot(jnp.concatenate(hits, axis=1), part)
    x = x_ref[...].astype(F32)
    scale = lax.rsqrt(jnp.mean(x * x, axis=-1, keepdims=True) + EPS)
    gain_grad = jnp.sum(dnormed * (x * scale), axis=0, keepdims=True)
    gain_grad_ref[...] = jnp.zeros((8, 128), F32)
    for k in range(4):
        gain_grad_ref[k : k + 1, :] = gain_grad[:, k * 128 : (k + 1) * 128]
    scaled = dnormed * gain_ref[...]
    inner = jnp.mean(scaled * x, axis=-1, keepdims=True)
    dx = scale * scaled - x * (scale * scale * scale * inner)
    feature_ref[...] = (grad_ref[...].astype(F32) + dx).astype(BF16)


def weights_body(mine_ref, other_ref, out_ref, gain_ref):
    which = pl.program_id(0)
    z, core = position()

    @pl.when(which == 0)
    def _():
        gain = jnp.zeros((8, 128), F32)
        for p in range(DOM):
            tail = mine_ref[p, 4 * CHUNK : SPREAD, :].astype(F32)
            gain = gain + (tail[0:8] + tail[8:16])
        gain_ref[...] = gain

    for c in range(2):
        @pl.when(core == c)
        def _():
            def piece(h, p, top, size):
                start = ((z - (h >> 1)) & 3) * CHUNK + top
                ref = mine_ref if h & 1 == c else other_ref
                return ref[p, pl.ds(pl.multiple_of(start, 16), size), :].astype(F32)

            @pl.when(which < 3)
            def _():
                for b in range(4):
                    part = jnp.concatenate([piece(h, which * 4 + b, 0, 64) for h in range(BLK)], axis=0)
                    out_ref[0, b * 128 : (b + 1) * 128, :] = jnp.transpose(part)

            @pl.when(which == 3)
            def _():
                for h in range(BLK):
                    for b in range(4):
                        out_ref[0, h * 64 : (h + 1) * 64, b * 128 : (b + 1) * 128] = piece(h, 12 + b, 0, 64)

            @pl.when(which == 4)
            def _():
                for h in range(BLK):
                    for a in range(4):
                        for b in range(4):
                            top = h * 64 + a * 16
                            out_ref[0, top : top + 16, b * 128 : (b + 1) * 128] = piece(h, a * 4 + b, 64, 16)


def chip_shift(step, swap):
    return [(z * 2 + c, ((z + step) % 4) * 2 + (c ^ swap)) for z in range(4) for c in range(2)]


def along_chips(array, step):
    return lax.ppermute(array, "blk", chip_shift(step, 0))


def other_core(array):
    return lax.ppermute(array, "blk", chip_shift(0, 1))


def to_dom_peers(array):
    return lax.all_to_all(array, "dom", split_axis=0, concat_axis=0, tiled=True)


def local(
    x, gain, wq, wk, wv, wo, wm, cluster, pattern, send_rows, send_counts, edge_src, edge_dst, out_grad
):
    gain_row = gain.reshape(1, D)
    pay = call(norm_body, shape((PAY, D), BF16), (pattern, x, gain_row, cluster.reshape(1, ROWS), out_grad), scalars=1)
    pays = [pay] + [along_chips(pay, step) for step in (1, 2, 3)]
    pays = pays + [other_core(part) for part in pays]
    outgoing = call(outgoing_body, shape((DOM, CAP, D), BF16), (send_counts, pay, send_rows), scalars=1, micros=3)
    incoming = to_dom_peers(outgoing)

    counts_t, degree, slot_grads, wqkv, wo_head = call(
        edges_body,
        (
            shape((1024, 512), BF16), shape((ROWS, 128), F32), shape((DOM, CAP, D), BF16),
            shape((192, D), BF16), shape((HEAD, D), BF16),
        ),
        (edge_src.reshape(32, 128), edge_dst.reshape(32, 128), out_grad, wm, wq, wk, wv, wo),
        scratch=[pltpu.VMEM((512, 1024), F32)],
        micros=10,
    )
    incoming, slot_grads = lax.optimization_barrier((incoming, slot_grads))
    back = to_dom_peers(slot_grads)

    mine, other, base = call(
        mean_body,
        (shape((4, HEAD, ROWS), BF16), shape((4, HEAD, ROWS), BF16), shape((ROWS, D), F32)),
        (counts_t, degree, incoming, x, wm),
        scratch=[pltpu.VMEM((BLK, HEAD, ROWS), BF16)],
        micros=4,
    )
    other = other_core(other)
    means = [jnp.stack([mine[dz], other[dz]]) for dz in range(4)]
    means = [means[0]] + [along_chips(means[dz], dz) for dz in (1, 2, 3)]

    *results, dw = call(
        attention_body,
        (*[shape((2, ROWS, 256), BF16)] * 4, shape((256, D), F32)),
        (*pays, wqkv, wo_head),
        scratch=[
            pltpu.VMEM((BLK, 128, ROWS), F32),
            pltpu.VMEM((BLK, 8, ROWS), F32),
            pltpu.VMEM((BLK, 128, ROWS), BF16),
            pltpu.VMEM((BLK, HEAD, ROWS), BF16),
            pltpu.VMEM((BLK, ROWS, 128), BF16),
            pltpu.VMEM((BLK, ROWS, 128), BF16),
            pltpu.VMEM((BLK, 80, ROWS), BF16),
            pltpu.VMEM((BLK, ROWS, ROWS), BF16),
            pltpu.VMEM((BLK, HEAD, ROWS), F32),
            pltpu.VMEM((BLK, HEAD, ROWS), F32),
            pltpu.VMEM((BLK, HEAD, ROWS), F32),
            pltpu.VMEM((BLK, HEAD, ROWS), BF16),
            pltpu.VMEM((BLK, HEAD, ROWS), F32),
        ],
        micros=30,
    )

    chunks = call(chunks_body, shape((DOM, CHUNK, 128), BF16), (*pays, *means, dw), micros=3)
    chunks, back = lax.optimization_barrier((chunks, back))
    chunk = call(chunk_sum_body, shape((CHUNK, 128), BF16), (to_dom_peers(chunks),), micros=1)
    chunk_parts = [chunk] + [along_chips(chunk, step) for step in (1, 2, 3)]

    results = [results[0]] + [along_chips(results[dz], -dz) for dz in (1, 2, 3)]
    swapped = [other_core(part[1]) for part in results]
    layer_out, feature_grad, gain_part = call(
        rows_body,
        (shape((ROWS, D), BF16), shape((ROWS, D), BF16), shape((8, 128), F32)),
        (send_counts, *results, *swapped, back, send_rows, base, x, gain_row, out_grad, wq, wk, wv, wo),
        scratch=[pltpu.VMEM((4, ROWS, 128), BF16)] * 4,
        scalars=1,
        micros=5,
    )
    gain_part = jnp.stack([gain_part, other_core(gain_part)])
    gain_parts = [gain_part] + [along_chips(gain_part, step) for step in (1, 2, 3)]
    spread = call(
        spread_body,
        shape((DOM, SPREAD, 128), BF16),
        (*chunk_parts, *gain_parts),
        scratch=[pltpu.VMEM((4, 2, 8, 128), F32)],
    )
    gathered = to_dom_peers(spread)
    whole = pl.BlockSpec((DOM, SPREAD, 128), lambda t: (0, 0, 0))
    weight_grads, gain_grad = pl.pallas_call(
        weights_body,
        grid=(5,),
        out_shape=(shape((5, D, D), F32), shape((8, 128), F32)),
        in_specs=[whole, whole],
        out_specs=(pl.BlockSpec((1, D, D), lambda t: (t, 0, 0)), pl.BlockSpec((8, 128), lambda t: (0, 0))),
    )(gathered, other_core(gathered))
    return layer_out, feature_grad, weight_grads, gain_grad[0:4].reshape(D)


def solution(mesh):
    both = ("dom", "blk")
    placed = (
        P(both, None), P(), P(), P(), P(), P(), P(), P(both), P(both, None), P(both, None), P(both), P(both), P(both),
        P(both, None),
    )
    return jax.shard_map(
        local,
        mesh=mesh,
        in_specs=placed,
        out_specs=(P(both, None), P(both, None), P(), P()),
        check_vma=False,
    )
```

```python
import math

import jax
import jax.numpy as jnp
from jax import lax
from jax.experimental import pallas as pl
from jax.experimental.pallas import tpu as pltpu
from jax.sharding import PartitionSpec as P

F32 = jnp.float32
BF16 = jnp.bfloat16
EPS = 1e-06
D = 512
ROWS = 256
HEAD = 64
BLK = 8
DOM = 16
CAP = 128
EDGES = 4096
PAY = 2 * ROWS + 16
LOG2E = math.log2(math.e)
SCORE_MUL = LOG2E / 8.0
SCORE_SUB = (8.0 + 256.0) * LOG2E
CHUNK = 80
SPREAD = 4 * CHUNK + 16

NT = (((1,), (1,)), ((), ()))
NN = (((1,), (0,)), ((), ()))


def dot(a, b, dims=NN):
    return lax.dot_general(a, b, dims, preferred_element_type=F32)


def call(body, out_shape, operands, scratch=(), scalars=0, micros=2):
    specs = [pl.BlockSpec(memory_space=pltpu.SMEM)] * scalars
    specs += [pl.BlockSpec(memory_space=pltpu.VMEM)] * (len(operands) - scalars)
    return pl.pallas_call(
        body,
        out_shape=out_shape,
        in_specs=specs,
        out_specs=jax.tree.map(lambda _: pl.BlockSpec(memory_space=pltpu.VMEM), out_shape),
        scratch_shapes=list(scratch),
        cost_estimate=pl.CostEstimate(flops=int(micros * 1e9), transcendentals=0, bytes_accessed=1 << 20),
    )(*operands)


def shape(dims, dtype):
    return jax.ShapeDtypeStruct(dims, dtype)


def position():
    me = lax.axis_index("blk").astype(jnp.int32)
    return lax.shift_right_logical(me, 1), me & 1


def norm_body(pattern_ref, counts_ref, x_ref, gain_ref, label_ref, grad_ref, rows_ref, out_ref, slots_ref):
    x = x_ref[...].astype(F32)
    scale = lax.rsqrt(jnp.mean(x * x, axis=-1, keepdims=True) + EPS)
    normed = (x * scale * gain_ref[...]).astype(BF16)
    out_ref[0:ROWS, :] = normed
    out_ref[ROWS : 2 * ROWS, :] = grad_ref[...]
    row = lax.broadcasted_iota(jnp.int32, (16, ROWS), 0)
    lane = lax.broadcasted_iota(jnp.int32, (16, ROWS), 1)
    tail = jnp.where(row == 0, label_ref[...].astype(F32), 0.0)
    for b in range(BLK):
        flag = jnp.where(pattern_ref[0, b] == 1, 1.0, 0.0)
        tail = jnp.where((row == 1 + b) & (lane >= 0), flag, tail)
    out_ref[2 * ROWS : PAY, 0:ROWS] = tail.astype(BF16)
    out_ref[2 * ROWS : PAY, ROWS:D] = jnp.zeros((16, D - ROWS), BF16)
    columns = jnp.transpose(rows_ref[...].astype(F32))
    lane = lax.broadcasted_iota(jnp.int32, (CAP, ROWS), 1).astype(F32)
    slot = lax.broadcasted_iota(jnp.int32, (CAP, ROWS), 0)
    for p in range(DOM):
        hit = (lane == columns[:, p : p + 1]) & (slot < counts_ref[p])
        slots_ref[p] = dot(jnp.where(hit, 1.0, 0.0).astype(BF16), normed).astype(BF16)


E_ROWS = 4


def edges_body(
    src_ref, dst_ref, grad_ref, w_ref, wq_ref, wk_ref, wv_ref, wo_ref,
    counts_t_ref, degree_ref, slots_ref, wqkv_ref, wo_head_ref, acc_ref,
):
    z, core = position()
    for m in range(4):
        @pl.when(z == m)
        def _():
            for k, ref in enumerate((wq_ref, wk_ref, wv_ref)):
                pair = jnp.transpose(ref[:, m * 128 : (m + 1) * 128].astype(F32))
                picked = jnp.where(core == 0, pair[0:HEAD], pair[HEAD:128])
                wqkv_ref[k * HEAD : (k + 1) * HEAD, :] = picked.astype(BF16)
            for c in range(2):
                @pl.when(core == c)
                def _():
                    wo_head_ref[...] = wo_ref[m * 128 + c * HEAD : m * 128 + (c + 1) * HEAD, :]

    low_row = lax.broadcasted_iota(jnp.int32, (512, E_ROWS * 128), 0)
    high_row = lax.broadcasted_iota(jnp.int32, (1024, E_ROWS * 128), 0)
    for step in range(EDGES // (E_ROWS * 128)):
        rows = [step * E_ROWS + k for k in range(E_ROWS)]
        src = jnp.concatenate([src_ref[k : k + 1, :] for k in rows], axis=1)
        dst = jnp.concatenate([dst_ref[k : k + 1, :] for k in rows], axis=1)
        low = jnp.where(low_row == (src & 511), 1.0, 0.0).astype(BF16)
        high = jnp.where(high_row == ((src >> 9) * 256 + dst), 1.0, 0.0).astype(BF16)
        part = dot(low, high, NT)
        if step == 0:
            acc_ref[...] = part
        else:
            acc_ref[...] += part
    counts = acc_ref[...]
    per_row = jnp.sum(counts, axis=0, keepdims=True)
    per_row = per_row[:, 0:256] + per_row[:, 256:512] + per_row[:, 512:768] + per_row[:, 768:1024]
    degree = jnp.transpose(jnp.broadcast_to(jnp.maximum(per_row, 1.0), (128, ROWS)))
    degree_ref[...] = degree
    counts_t_ref[...] = jnp.transpose(counts).astype(BF16)
    counts = counts.astype(BF16)
    inverse = 1.0 / degree[:, 0:1]
    message = (dot(grad_ref[...], w_ref[...], NT) * inverse).astype(BF16)
    for high in range(4):
        part = dot(counts[:, high * 256 : (high + 1) * 256], message).astype(BF16)
        for k in range(4):
            slots_ref[high * 4 + k] = part[k * CAP : (k + 1) * CAP, :]


def mean_body(counts_t_ref, degree_ref, table_ref, x_ref, w_ref, mine_ref, other_ref, base_ref, means_ref):
    total = jnp.zeros((ROWS, D), F32)
    for high in range(4):
        table = jnp.concatenate([table_ref[high * 4 + k] for k in range(4)], axis=0)
        total = total + dot(counts_t_ref[high * 256 : (high + 1) * 256, :], table)
    mean_rows = (total / degree_ref[:, 0:1]).astype(BF16)
    base_ref[...] = x_ref[...].astype(F32) + dot(mean_rows, w_ref[...])
    turned = jnp.transpose(mean_rows.astype(F32)).astype(BF16)
    for h in range(BLK):
        means_ref[h] = turned[h * HEAD : (h + 1) * HEAD, :]
    z, core = position()
    for dz in range(4):
        chip = ((z + dz) & 3) * 2
        mine_ref[dz] = means_ref[chip + core]
        other_ref[dz] = means_ref[chip + (1 - core)]


def attention_body(
    p0_ref, p1_ref, p2_ref, p3_ref, p4_ref, p5_ref, p6_ref, p7_ref, wqkv_ref, wo_ref,
    r0_ref, r1_ref, r2_ref, r3_ref, dw_ref,
    y_ref, s_ref, qt_ref, kt_ref, k_ref, v_ref, vt_ref, w_ref, dq_ref, dk_ref, dv_ref, at_ref, ga_ref, sl_ref, qr_ref, gr_ref,
):
    pays = (p0_ref, p1_ref, p2_ref, p3_ref, p4_ref, p5_ref, p6_ref, p7_ref)
    outs = (r0_ref, r1_ref, r2_ref, r3_ref)
    z, core = position()
    row = lax.broadcasted_iota(jnp.int32, (HEAD, ROWS), 0)
    number = row.astype(F32)

    def head_scale(part):
        return lax.rsqrt(jnp.sum(part * part, axis=0, keepdims=True) * (1.0 / HEAD) + EPS)

    for r in range(BLK):
        pay = pays[r]
        projected = dot(wqkv_ref[...], pay[0:ROWS, :], NT)
        query, key, value = projected[0:HEAD], projected[HEAD:128], projected[128:192]
        scale_q, scale_k = head_scale(query), head_scale(key)
        query, key = query * scale_q, key * scale_k
        y_ref[r, 0:HEAD] = query
        y_ref[r, HEAD:128] = key
        s_ref[r, 0:1] = scale_q
        s_ref[r, 1:2] = scale_k
        tail = pay[2 * ROWS : PAY, 0:ROWS].astype(F32)
        same = jnp.where(number == tail[0:1], 32.0, 0.0)
        sender = ((z - (r & 3)) & 3) * 2 + (core ^ (r >> 2))
        wanted = jnp.concatenate([jnp.zeros((16, ROWS), F32), tail[1:9] * 32.0, jnp.zeros((40, ROWS), F32)], axis=0)
        owner = jnp.where(row == 16 + sender, 32.0, 0.0)
        qt_ref[r] = jnp.concatenate([query, same + wanted], axis=0).astype(BF16)
        key = jnp.concatenate([key, same + owner], axis=0)
        kt_ref[r] = key[0:HEAD].astype(BF16)
        k_ref[r] = jnp.transpose(key).astype(BF16)
        value = jnp.concatenate([value, jnp.where(row < 2, 1.0, 0.0)], axis=0)
        vt_ref[r] = value[0:80].astype(BF16)
        v_ref[r] = jnp.transpose(value).astype(BF16)
        ga_ref[r] = dot(wo_ref[...], pay[ROWS : 2 * ROWS, :], NT)
        qr_ref[r] = jnp.transpose(qt_ref[r].astype(F32)).astype(BF16)

    keys_t = jnp.concatenate([kt_ref[j] for j in range(BLK)], axis=1)
    values_t = jnp.concatenate([vt_ref[j] for j in range(BLK)], axis=1)

    def query_block(i, carry):
        query = qt_ref[i]
        for j in range(BLK):
            scores = dot(k_ref[j], query)
            w_ref[i, j] = jnp.exp2(scores * SCORE_MUL - SCORE_SUB).astype(BF16)
        numer = dot(values_t, w_ref[i].reshape(BLK * ROWS, ROWS))
        inverse = 1.0 / numer[HEAD : HEAD + 1]
        attn = (numer[0:HEAD] * inverse).astype(BF16)
        at_ref[i] = attn
        grad_attn = ga_ref[i]
        minus = jnp.sum(grad_attn * attn.astype(F32), axis=0, keepdims=True) * (-inverse)
        coarse = minus.astype(BF16).astype(F32)
        extra = jnp.where(row == 0, coarse, jnp.where(row == 1, minus - coarse, 0.0))
        grad = jnp.concatenate([grad_attn * inverse, extra], axis=0).astype(BF16)
        gr_ref[i] = jnp.transpose(grad.astype(F32)).astype(BF16)
        for j in range(BLK):
            sl_ref[i, j] = (w_ref[i, j].astype(F32) * dot(v_ref[j], grad)).astype(BF16)
        dq_ref[i] = dot(keys_t, sl_ref[i].reshape(BLK * ROWS, ROWS))
        return carry

    lax.fori_loop(0, BLK, query_block, 0)

    queries = jnp.concatenate([qr_ref[i] for i in range(BLK)], axis=0)
    grads = jnp.concatenate([gr_ref[i] for i in range(BLK)], axis=0)

    def key_block(j, carry):
        slopes = jnp.concatenate([sl_ref[i, j] for i in range(BLK)], axis=1)
        dk_ref[j] = jnp.transpose(dot(slopes, queries))[0:HEAD]
        weights = jnp.concatenate([w_ref[i, j] for i in range(BLK)], axis=1)
        dv_ref[j] = jnp.transpose(dot(weights, grads))[0:HEAD]
        return carry

    lax.fori_loop(0, BLK, key_block, 0)

    dw = jnp.zeros((192, D), F32)
    dwo = jnp.zeros((HEAD, D), F32)
    for r in range(BLK):
        pay = pays[r]

        def pull(grad, y, scale):
            grad = grad * (8.0 / HEAD)
            return scale * (grad - y * (jnp.sum(y * grad, axis=0, keepdims=True) * (1.0 / HEAD)))

        dquery = pull(dq_ref[r], y_ref[r, 0:HEAD], s_ref[r, 0:1])
        dkey = pull(dk_ref[r], y_ref[r, HEAD:128], s_ref[r, 1:2])
        first = jnp.concatenate([dquery, dkey], axis=0)
        second = jnp.concatenate([dv_ref[r], at_ref[r].astype(F32)], axis=0)
        outs[r & 3][r >> 2, :, 0:128] = jnp.transpose(first).astype(BF16)
        outs[r & 3][r >> 2, :, 128:256] = jnp.transpose(second).astype(BF16)
        left = jnp.concatenate([first, second[0:HEAD]], axis=0).astype(BF16)
        dw = dw + dot(left, pay[0:ROWS, :])
        dwo = dwo + dot(at_ref[r], pay[ROWS : 2 * ROWS, :])
    dw_ref[0:192, :] = dw
    dw_ref[192:256, :] = dwo


def chunks_body(
    p0_ref, p1_ref, p2_ref, p3_ref, p4_ref, p5_ref, p6_ref, p7_ref, m0_ref, m1_ref, m2_ref, m3_ref, dw_ref, out_ref
):
    pays = (p0_ref, p1_ref, p2_ref, p3_ref, p4_ref, p5_ref, p6_ref, p7_ref)
    total = jnp.zeros((HEAD, D), F32)
    for dz, m_ref in enumerate((m0_ref, m1_ref, m2_ref, m3_ref)):
        for c in range(2):
            total = total + dot(m_ref[c], pays[4 * c + dz][ROWS : 2 * ROWS, :])
    for a in range(4):
        for b in range(4):
            out_ref[a * 4 + b, 0:64, :] = dw_ref[a * 64 : (a + 1) * 64, b * 128 : (b + 1) * 128].astype(BF16)
            out_ref[a * 4 + b, 64:80, :] = total[a * 16 : (a + 1) * 16, b * 128 : (b + 1) * 128].astype(BF16)


def chunk_sum_body(in_ref, g0_ref, g1_ref, out_ref):
    total = in_ref[0].astype(F32)
    for p in range(1, DOM):
        total = total + in_ref[p].astype(F32)
    out_ref[0:CHUNK, :] = total.astype(BF16)
    z, core = position()
    one, two = g0_ref[...], g1_ref[...]
    gain = jnp.where(core == 0, one, two) + jnp.where(core == 0, two, one)
    coarse = gain.astype(BF16).astype(F32)
    fine = gain - coarse
    out_ref[CHUNK : CHUNK + 16, :] = jnp.concatenate([coarse, fine], axis=0).astype(BF16)


def spread_body(c0_ref, c1_ref, c2_ref, c3_ref, out_ref, gains_ref):
    z, core = position()
    for dz, c_ref in enumerate((c0_ref, c1_ref, c2_ref, c3_ref)):
        tail = c_ref[CHUNK : CHUNK + 16, :].astype(F32)
        gains_ref[dz] = tail[0:8] + tail[8:16]
    gain = jnp.zeros((8, 128), F32)
    for chip in range(4):
        gain = gain + gains_ref[(z - chip) & 3]
    coarse = gain.astype(BF16).astype(F32)
    fine = (gain - coarse).astype(BF16).astype(F32)
    tail = jnp.concatenate([coarse, fine], axis=0).astype(BF16)
    for p in range(DOM):
        for dz, c_ref in enumerate((c0_ref, c1_ref, c2_ref, c3_ref)):
            out_ref[p, dz * CHUNK : (dz + 1) * CHUNK, :] = c_ref[0:CHUNK, :]
        out_ref[p, 4 * CHUNK : SPREAD, :] = tail


def rows_body(
    counts_ref, r0_ref, r1_ref, r2_ref, r3_ref, t0_ref, t1_ref, t2_ref, t3_ref, back_ref, rows_ref, base_ref, x_ref,
    gain_ref, grad_ref, wq_ref, wk_ref, wv_ref, wo_ref,
    out_ref, feature_ref, gain_grad_ref, dq_ref, dk_ref, dv_ref, at_ref,
):
    left = lax.broadcasted_iota(jnp.int32, (ROWS, 128), 1) < HEAD
    z, core = position()
    even = core == 0
    for dz, (r_ref, t_ref) in enumerate(zip((r0_ref, r1_ref, r2_ref, r3_ref), (t0_ref, t1_ref, t2_ref, t3_ref))):
        chip = (z + dz) & 3
        one, two = r_ref[0].astype(F32), t_ref[...].astype(F32)
        low, high = jnp.where(even, one, two), jnp.where(even, two, one)
        low0, low1 = low[:, 0:128], low[:, 128:256]
        high0, high1 = high[:, 0:128], high[:, 128:256]
        dq_ref[chip] = jnp.where(left, low0, pltpu.roll(high0, HEAD, 1)).astype(BF16)
        dk_ref[chip] = jnp.where(left, pltpu.roll(low0, HEAD, 1), high0).astype(BF16)
        dv_ref[chip] = jnp.where(left, low1, pltpu.roll(high1, HEAD, 1)).astype(BF16)
        at_ref[chip] = jnp.where(left, pltpu.roll(low1, HEAD, 1), high1).astype(BF16)

    def whole(ref):
        return jnp.concatenate([ref[m] for m in range(4)], axis=1)

    out_ref[...] = (base_ref[...] + dot(whole(at_ref), wo_ref[...])).astype(BF16)
    dnormed = dot(whole(dq_ref), wq_ref[...], NT) + dot(whole(dk_ref), wk_ref[...], NT)
    dnormed = dnormed + dot(whole(dv_ref), wv_ref[...], NT)
    row = lax.broadcasted_iota(jnp.int32, (ROWS, CAP), 0)
    slot = lax.broadcasted_iota(jnp.int32, (ROWS, CAP), 1)
    for k in range(4):
        hits = []
        for p in range(4 * k, 4 * k + 4):
            hit = (row == rows_ref[p : p + 1, :]) & (slot < counts_ref[p])
            hits.append(jnp.where(hit, 1.0, 0.0).astype(BF16))
        part = jnp.concatenate([back_ref[p] for p in range(4 * k, 4 * k + 4)], axis=0)
        dnormed = dnormed + dot(jnp.concatenate(hits, axis=1), part)
    x = x_ref[...].astype(F32)
    scale = lax.rsqrt(jnp.mean(x * x, axis=-1, keepdims=True) + EPS)
    gain_grad = jnp.sum(dnormed * (x * scale), axis=0, keepdims=True)
    gain_grad_ref[...] = jnp.zeros((8, 128), F32)
    for k in range(4):
        gain_grad_ref[k : k + 1, :] = gain_grad[:, k * 128 : (k + 1) * 128]
    scaled = dnormed * gain_ref[...]
    inner = jnp.mean(scaled * x, axis=-1, keepdims=True)
    dx = scale * scaled - x * (scale * scale * scale * inner)
    feature_ref[...] = (grad_ref[...].astype(F32) + dx).astype(BF16)


def weights_body(mine_ref, other_ref, out_ref, gain_ref):
    which = pl.program_id(0)
    z, core = position()

    @pl.when(which == 0)
    def _():
        gain = jnp.zeros((8, 128), F32)
        for p in range(DOM):
            tail = mine_ref[p, 4 * CHUNK : SPREAD, :].astype(F32)
            gain = gain + (tail[0:8] + tail[8:16])
        for k in range(4):
            gain_ref[:, k * 128 : (k + 1) * 128] = gain[k : k + 1, :]

    for c in range(2):
        @pl.when(core == c)
        def _():
            def piece(h, p, top, size):
                start = ((z - (h >> 1)) & 3) * CHUNK + top
                ref = mine_ref if h & 1 == c else other_ref
                return ref[p, pl.ds(pl.multiple_of(start, 16), size), :].astype(F32)

            @pl.when(which < 3)
            def _():
                for b in range(4):
                    part = jnp.concatenate([piece(h, which * 4 + b, 0, 64) for h in range(BLK)], axis=0)
                    out_ref[0, b * 128 : (b + 1) * 128, :] = jnp.transpose(part)

            @pl.when(which == 3)
            def _():
                for h in range(BLK):
                    for b in range(4):
                        out_ref[0, h * 64 : (h + 1) * 64, b * 128 : (b + 1) * 128] = piece(h, 12 + b, 0, 64)

            @pl.when(which == 4)
            def _():
                for h in range(BLK):
                    for a in range(4):
                        for b in range(4):
                            top = h * 64 + a * 16
                            out_ref[0, top : top + 16, b * 128 : (b + 1) * 128] = piece(h, a * 4 + b, 64, 16)


def chip_shift(step, swap):
    return [(z * 2 + c, ((z + step) % 4) * 2 + (c ^ swap)) for z in range(4) for c in range(2)]


def along_chips(array, step):
    return lax.ppermute(array, "blk", chip_shift(step, 0))


def other_core(array):
    return lax.ppermute(array, "blk", chip_shift(0, 1))


def to_dom_peers(array):
    return lax.all_to_all(array, "dom", split_axis=0, concat_axis=0, tiled=True)


def local(
    x, gain, wq, wk, wv, wo, wm, cluster, pattern, send_rows, send_counts, edge_src, edge_dst, out_grad
):
    gain_row = gain.reshape(1, D)
    pay, outgoing = call(
        norm_body,
        (shape((PAY, D), BF16), shape((DOM, CAP, D), BF16)),
        (pattern, send_counts, x, gain_row, cluster.reshape(1, ROWS), out_grad, send_rows),
        scalars=2,
        micros=4,
    )
    incoming = to_dom_peers(outgoing)
    pays = [pay] + [along_chips(pay, step) for step in (1, 2, 3)]

    counts_t, degree, slot_grads, wqkv, wo_head = call(
        edges_body,
        (
            shape((1024, 512), BF16), shape((ROWS, 128), F32), shape((DOM, CAP, D), BF16),
            shape((192, D), BF16), shape((HEAD, D), BF16),
        ),
        (edge_src.reshape(32, 128), edge_dst.reshape(32, 128), out_grad, wm, wq, wk, wv, wo),
        scratch=[pltpu.VMEM((512, 1024), F32)],
        micros=10,
    )
    *pays, degree = lax.optimization_barrier((*pays, degree))
    pays = pays + [other_core(part) for part in pays]
    incoming, slot_grads = lax.optimization_barrier((incoming, slot_grads))
    back = to_dom_peers(slot_grads)

    mine, other, base = call(
        mean_body,
        (shape((4, HEAD, ROWS), BF16), shape((4, HEAD, ROWS), BF16), shape((ROWS, D), F32)),
        (counts_t, degree, incoming, x, wm),
        scratch=[pltpu.VMEM((BLK, HEAD, ROWS), BF16)],
        micros=4,
    )
    other = other_core(other)
    means = [jnp.stack([mine[dz], other[dz]]) for dz in range(4)]
    means = [means[0]] + [along_chips(means[dz], dz) for dz in (1, 2, 3)]

    *pays, base = lax.optimization_barrier((*pays, base))
    *results, dw = call(
        attention_body,
        (*[shape((2, ROWS, 256), BF16)] * 4, shape((256, D), F32)),
        (*pays, wqkv, wo_head),
        scratch=[
            pltpu.VMEM((BLK, 128, ROWS), F32),
            pltpu.VMEM((BLK, 8, ROWS), F32),
            pltpu.VMEM((BLK, 128, ROWS), BF16),
            pltpu.VMEM((BLK, HEAD, ROWS), BF16),
            pltpu.VMEM((BLK, ROWS, 128), BF16),
            pltpu.VMEM((BLK, ROWS, 128), BF16),
            pltpu.VMEM((BLK, 80, ROWS), BF16),
            pltpu.VMEM((BLK, BLK, ROWS, ROWS), BF16),
            pltpu.VMEM((BLK, HEAD, ROWS), F32),
            pltpu.VMEM((BLK, HEAD, ROWS), F32),
            pltpu.VMEM((BLK, HEAD, ROWS), F32),
            pltpu.VMEM((BLK, HEAD, ROWS), BF16),
            pltpu.VMEM((BLK, HEAD, ROWS), F32),
            pltpu.VMEM((BLK, BLK, ROWS, ROWS), BF16),
            pltpu.VMEM((BLK, ROWS, 128), BF16),
            pltpu.VMEM((BLK, ROWS, 128), BF16),
        ],
        micros=30,
    )

    chunks = call(chunks_body, shape((DOM, CHUNK, 128), BF16), (*pays, *means, dw), micros=3)
    chunks, back = lax.optimization_barrier((chunks, back))
    chunks = to_dom_peers(chunks)

    results = [results[0]] + [along_chips(results[dz], -dz) for dz in (1, 2, 3)]
    swapped = [other_core(part[1]) for part in results]
    layer_out, feature_grad, gain_part = call(
        rows_body,
        (shape((ROWS, D), BF16), shape((ROWS, D), BF16), shape((8, 128), F32)),
        (send_counts, *results, *swapped, back, send_rows, base, x, gain_row, out_grad, wq, wk, wv, wo),
        scratch=[pltpu.VMEM((4, ROWS, 128), BF16)] * 4,
        scalars=1,
        micros=5,
    )
    chunk = call(
        chunk_sum_body, shape((CHUNK + 16, 128), BF16), (chunks, gain_part, other_core(gain_part)), micros=1
    )
    chunk_parts = [chunk] + [along_chips(chunk, step) for step in (1, 2, 3)]
    spread = call(spread_body, shape((DOM, SPREAD, 128), BF16), chunk_parts, scratch=[pltpu.VMEM((4, 8, 128), F32)])
    gathered = to_dom_peers(spread)
    whole = pl.BlockSpec((DOM, SPREAD, 128), lambda t: (0, 0, 0))
    weight_grads, gain_grad = pl.pallas_call(
        weights_body,
        grid=(5,),
        out_shape=(shape((5, D, D), F32), shape((1, D), F32)),
        in_specs=[whole, whole],
        out_specs=(pl.BlockSpec((1, D, D), lambda t: (t, 0, 0)), pl.BlockSpec((1, D), lambda t: (0, 0))),
    )(gathered, other_core(gathered))
    return layer_out, feature_grad, weight_grads, gain_grad.reshape(D)


def solution(mesh):
    both = ("dom", "blk")
    placed = (
        P(both, None), P(), P(), P(), P(), P(), P(), P(both), P(both, None), P(both, None), P(both), P(both), P(both),
        P(both, None),
    )
    return jax.shard_map(
        local,
        mesh=mesh,
        in_specs=placed,
        out_specs=(P(both, None), P(both, None), P(), P()),
        check_vma=False,
    )
```

```python
import math

import jax
import jax.numpy as jnp
from jax import lax
from jax.experimental import pallas as pl
from jax.experimental.pallas import tpu as pltpu
from jax.sharding import PartitionSpec as P

F32 = jnp.float32
BF16 = jnp.bfloat16
EPS = 1e-06
D = 512
ROWS = 256
HEAD = 64
BLK = 8
DOM = 16
CAP = 128
EDGES = 4096
PAY = 2 * ROWS + 16
LOG2E = math.log2(math.e)
SCORE_MUL = LOG2E / 8.0
SCORE_SUB = (8.0 + 256.0) * LOG2E
CHUNK = 64 + 64 + 16
SPREAD = 4 * 64 + 64 + 16

NT = (((1,), (1,)), ((), ()))
NN = (((1,), (0,)), ((), ()))


def dot(a, b, dims=NN):
    return lax.dot_general(a, b, dims, preferred_element_type=F32)


def call(body, out_shape, operands, scratch=(), scalars=0, micros=2):
    specs = [pl.BlockSpec(memory_space=pltpu.SMEM)] * scalars
    specs += [pl.BlockSpec(memory_space=pltpu.VMEM)] * (len(operands) - scalars)
    return pl.pallas_call(
        body,
        out_shape=out_shape,
        in_specs=specs,
        out_specs=jax.tree.map(lambda _: pl.BlockSpec(memory_space=pltpu.VMEM), out_shape),
        scratch_shapes=list(scratch),
        cost_estimate=pl.CostEstimate(flops=int(micros * 1e9), transcendentals=0, bytes_accessed=1 << 20),
    )(*operands)


def shape(dims, dtype):
    return jax.ShapeDtypeStruct(dims, dtype)


def position():
    me = lax.axis_index("blk").astype(jnp.int32)
    return lax.shift_right_logical(me, 1), me & 1


def norm_body(pattern_ref, counts_ref, x_ref, gain_ref, label_ref, grad_ref, rows_ref, out_ref, slots_ref):
    x = x_ref[...].astype(F32)
    scale = lax.rsqrt(jnp.mean(x * x, axis=-1, keepdims=True) + EPS)
    normed = (x * scale * gain_ref[...]).astype(BF16)
    out_ref[0:ROWS, :] = normed
    out_ref[ROWS : 2 * ROWS, :] = grad_ref[...]
    row = lax.broadcasted_iota(jnp.int32, (16, ROWS), 0)
    lane = lax.broadcasted_iota(jnp.int32, (16, ROWS), 1)
    tail = jnp.where(row == 0, label_ref[...].astype(F32), 0.0)
    for b in range(BLK):
        flag = jnp.where(pattern_ref[0, b] == 1, 1.0, 0.0)
        tail = jnp.where((row == 1 + b) & (lane >= 0), flag, tail)
    out_ref[2 * ROWS : PAY, 0:ROWS] = tail.astype(BF16)
    out_ref[2 * ROWS : PAY, ROWS:D] = jnp.zeros((16, D - ROWS), BF16)
    columns = jnp.transpose(rows_ref[...].astype(F32))
    lane = lax.broadcasted_iota(jnp.int32, (CAP, ROWS), 1).astype(F32)
    slot = lax.broadcasted_iota(jnp.int32, (CAP, ROWS), 0)
    for p in range(DOM):
        hit = (lane == columns[:, p : p + 1]) & (slot < counts_ref[p])
        slots_ref[p] = dot(jnp.where(hit, 1.0, 0.0).astype(BF16), normed).astype(BF16)


E_ROWS = 4


def edges_body(
    src_ref, dst_ref, grad_ref, w_ref, wq_ref, wk_ref, wv_ref, wo_ref,
    counts_t_ref, degree_ref, slots_ref, wqkv_ref, wo_head_ref, acc_ref,
):
    z, core = position()
    for m in range(4):
        @pl.when(z == m)
        def _():
            for k, ref in enumerate((wq_ref, wk_ref, wv_ref)):
                pair = jnp.transpose(ref[:, m * 128 : (m + 1) * 128].astype(F32))
                picked = jnp.where(core == 0, pair[0:HEAD], pair[HEAD:128])
                wqkv_ref[k * HEAD : (k + 1) * HEAD, :] = picked.astype(BF16)
            for c in range(2):
                @pl.when(core == c)
                def _():
                    wo_head_ref[...] = wo_ref[m * 128 + c * HEAD : m * 128 + (c + 1) * HEAD, :]

    low_row = lax.broadcasted_iota(jnp.int32, (512, E_ROWS * 128), 0)
    high_row = lax.broadcasted_iota(jnp.int32, (1024, E_ROWS * 128), 0)
    for step in range(EDGES // (E_ROWS * 128)):
        rows = [step * E_ROWS + k for k in range(E_ROWS)]
        src = jnp.concatenate([src_ref[k : k + 1, :] for k in rows], axis=1)
        dst = jnp.concatenate([dst_ref[k : k + 1, :] for k in rows], axis=1)
        low = jnp.where(low_row == (src & 511), 1.0, 0.0).astype(BF16)
        high = jnp.where(high_row == ((src >> 9) * 256 + dst), 1.0, 0.0).astype(BF16)
        part = dot(low, high, NT)
        if step == 0:
            acc_ref[...] = part
        else:
            acc_ref[...] += part
    counts = acc_ref[...]
    per_row = jnp.sum(counts, axis=0, keepdims=True)
    per_row = per_row[:, 0:256] + per_row[:, 256:512] + per_row[:, 512:768] + per_row[:, 768:1024]
    degree = jnp.transpose(jnp.broadcast_to(jnp.maximum(per_row, 1.0), (128, ROWS)))
    degree_ref[...] = degree
    counts_t_ref[...] = jnp.transpose(counts).astype(BF16)
    counts = counts.astype(BF16)
    inverse = 1.0 / degree[:, 0:1]
    message = (dot(grad_ref[...], w_ref[...], NT) * inverse).astype(BF16)
    for high in range(4):
        part = dot(counts[:, high * 256 : (high + 1) * 256], message).astype(BF16)
        for k in range(4):
            slots_ref[high * 4 + k] = part[k * CAP : (k + 1) * CAP, :]


def mean_body(counts_t_ref, degree_ref, table_ref, x_ref, grad_ref, w_ref, base_ref, mine_ref, other_ref):
    total = jnp.zeros((ROWS, D), F32)
    for high in range(4):
        table = jnp.concatenate([table_ref[high * 4 + k] for k in range(4)], axis=0)
        total = total + dot(counts_t_ref[high * 256 : (high + 1) * 256, :], table)
    mean_rows = (total / degree_ref[:, 0:1]).astype(BF16)
    base_ref[...] = x_ref[...].astype(F32) + dot(mean_rows, w_ref[...])
    dw = dot(jnp.transpose(mean_rows.astype(F32)).astype(BF16), grad_ref[...]).astype(BF16)
    z, core = position()
    for half in range(2):
        def fill(ref):
            for p in range(DOM):
                top = half * 256 + p * 16
                for b in range(4):
                    ref[p, b * 16 : (b + 1) * 16, :] = dw[top : top + 16, b * 128 : (b + 1) * 128]

        @pl.when(core == half)
        def _():
            fill(mine_ref)

        @pl.when(core != half)
        def _():
            fill(other_ref)


def attention_body(
    p0_ref, p1_ref, t2_ref, b2_ref, p3_ref, p4_ref, p5_ref, t6_ref, b6_ref, p7_ref, wqkv_ref, wo_ref, mine_ref, other_ref,
    r0_ref, r1_ref, r2_ref, r3_ref, chunks_ref,
    y_ref, s_ref, qt_ref, kt_ref, k_ref, v_ref, vt_ref, w_ref, dq_ref, dk_ref, dv_ref, at_ref, ga_ref, sl_ref, qr_ref, gr_ref,
):
    pays = (p0_ref, p1_ref, (t2_ref, b2_ref), p3_ref, p4_ref, p5_ref, (t6_ref, b6_ref), p7_ref)

    def normed_of(pay):
        return pay[0][...] if isinstance(pay, tuple) else pay[0:ROWS, :]

    def grads_of(pay):
        return pay[1][0:ROWS, :] if isinstance(pay, tuple) else pay[ROWS : 2 * ROWS, :]

    def tail_of(pay):
        return pay[1][ROWS : PAY - ROWS, 0:ROWS] if isinstance(pay, tuple) else pay[2 * ROWS : PAY, 0:ROWS]

    outs = (r0_ref, r1_ref, r2_ref, r3_ref)
    z, core = position()
    row = lax.broadcasted_iota(jnp.int32, (HEAD, ROWS), 0)
    number = row.astype(F32)

    def head_scale(part):
        return lax.rsqrt(jnp.sum(part * part, axis=0, keepdims=True) * (1.0 / HEAD) + EPS)

    for r in range(BLK):
        pay = pays[r]
        projected = dot(wqkv_ref[...], normed_of(pay), NT)
        query, key, value = projected[0:HEAD], projected[HEAD:128], projected[128:192]
        scale_q, scale_k = head_scale(query), head_scale(key)
        query, key = query * scale_q, key * scale_k
        y_ref[r, 0:HEAD] = query
        y_ref[r, HEAD:128] = key
        s_ref[r, 0:1] = scale_q
        s_ref[r, 1:2] = scale_k
        tail = tail_of(pay).astype(F32)
        same = jnp.where(number == tail[0:1], 32.0, 0.0)
        sender = ((z - (r & 3)) & 3) * 2 + (core ^ (r >> 2))
        wanted = jnp.concatenate([jnp.zeros((16, ROWS), F32), tail[1:9] * 32.0, jnp.zeros((40, ROWS), F32)], axis=0)
        owner = jnp.where(row == 16 + sender, 32.0, 0.0)
        qt_ref[r] = jnp.concatenate([query, same + wanted], axis=0).astype(BF16)
        key = jnp.concatenate([key, same + owner], axis=0)
        kt_ref[r] = key[0:HEAD].astype(BF16)
        k_ref[r] = jnp.transpose(key).astype(BF16)
        value = jnp.concatenate([value, jnp.where(row < 2, 1.0, 0.0)], axis=0)
        vt_ref[r] = value[0:80].astype(BF16)
        v_ref[r] = jnp.transpose(value).astype(BF16)
        ga_ref[r] = dot(wo_ref[...], grads_of(pay), NT)
        qr_ref[r] = jnp.transpose(qt_ref[r].astype(F32)).astype(BF16)

    keys_t = jnp.concatenate([kt_ref[j] for j in range(BLK)], axis=1)
    values_t = jnp.concatenate([vt_ref[j] for j in range(BLK)], axis=1)

    def query_block(i, carry):
        query = qt_ref[i]
        for j in range(BLK):
            scores = dot(k_ref[j], query)
            w_ref[i, j] = jnp.exp2(scores * SCORE_MUL - SCORE_SUB).astype(BF16)
        numer = dot(values_t, w_ref[i].reshape(BLK * ROWS, ROWS))
        inverse = 1.0 / numer[HEAD : HEAD + 1]
        attn = (numer[0:HEAD] * inverse).astype(BF16)
        at_ref[i] = attn
        grad_attn = ga_ref[i]
        minus = jnp.sum(grad_attn * attn.astype(F32), axis=0, keepdims=True) * (-inverse)
        coarse = minus.astype(BF16).astype(F32)
        extra = jnp.where(row == 0, coarse, jnp.where(row == 1, minus - coarse, 0.0))
        grad = jnp.concatenate([grad_attn * inverse, extra], axis=0).astype(BF16)
        gr_ref[i] = jnp.transpose(grad.astype(F32)).astype(BF16)
        for j in range(BLK):
            sl_ref[i, j] = (w_ref[i, j].astype(F32) * dot(v_ref[j], grad)).astype(BF16)
        dq_ref[i] = dot(keys_t, sl_ref[i].reshape(BLK * ROWS, ROWS))
        return carry

    lax.fori_loop(0, BLK, query_block, 0)

    queries = jnp.concatenate([qr_ref[i] for i in range(BLK)], axis=0)
    grads = jnp.concatenate([gr_ref[i] for i in range(BLK)], axis=0)

    def key_block(j, carry):
        slopes = jnp.concatenate([sl_ref[i, j] for i in range(BLK)], axis=1)
        dk_ref[j] = jnp.transpose(dot(slopes, queries))[0:HEAD]
        weights = jnp.concatenate([w_ref[i, j] for i in range(BLK)], axis=1)
        dv_ref[j] = jnp.transpose(dot(weights, grads))[0:HEAD]
        return carry

    lax.fori_loop(0, BLK, key_block, 0)

    dw = jnp.zeros((192, D), F32)
    dwo = jnp.zeros((HEAD, D), F32)
    for r in range(BLK):
        pay = pays[r]

        def pull(grad, y, scale):
            grad = grad * (8.0 / HEAD)
            return scale * (grad - y * (jnp.sum(y * grad, axis=0, keepdims=True) * (1.0 / HEAD)))

        dquery = pull(dq_ref[r], y_ref[r, 0:HEAD], s_ref[r, 0:1])
        dkey = pull(dk_ref[r], y_ref[r, HEAD:128], s_ref[r, 1:2])
        first = jnp.concatenate([dquery, dkey], axis=0)
        second = jnp.concatenate([dv_ref[r], at_ref[r].astype(F32)], axis=0)
        outs[r & 3][r >> 2, :, 0:128] = jnp.transpose(first).astype(BF16)
        outs[r & 3][r >> 2, :, 128:256] = jnp.transpose(second).astype(BF16)
        left = jnp.concatenate([first, second[0:HEAD]], axis=0).astype(BF16)
        dw = dw + dot(left, normed_of(pay))
        dwo = dwo + dot(at_ref[r], grads_of(pay))
    dw = jnp.concatenate([dw, dwo], axis=0).astype(BF16)
    for a in range(4):
        for b in range(4):
            p = a * 4 + b
            chunks_ref[p, 0:64, :] = dw[a * 64 : (a + 1) * 64, b * 128 : (b + 1) * 128]
            chunks_ref[p, 64:128, :] = (mine_ref[p].astype(F32) + other_ref[p].astype(F32)).astype(BF16)


def chunk_sum_body(in_ref, g0_ref, g1_ref, out_ref):
    total = in_ref[0].astype(F32)
    for p in range(1, DOM):
        total = total + in_ref[p].astype(F32)
    out_ref[0:128, :] = total.astype(BF16)
    z, core = position()
    one, two = g0_ref[...], g1_ref[...]
    gain = jnp.where(core == 0, one, two) + jnp.where(core == 0, two, one)
    coarse = gain.astype(BF16).astype(F32)
    fine = gain - coarse
    out_ref[128:CHUNK, :] = jnp.concatenate([coarse, fine], axis=0).astype(BF16)


def spread_body(c0_ref, c1_ref, c2_ref, c3_ref, out_ref, parts_ref):
    z, core = position()
    for dz, c_ref in enumerate((c0_ref, c1_ref, c2_ref, c3_ref)):
        parts_ref[dz] = c_ref[64:CHUNK, :].astype(F32)
    total = jnp.zeros((80, 128), F32)
    for chip in range(4):
        total = total + parts_ref[(z - chip) & 3]
    gain = total[64:72] + total[72:80]
    coarse = gain.astype(BF16).astype(F32)
    tail = jnp.concatenate([total[0:64], coarse, gain - coarse], axis=0).astype(BF16)
    for p in range(DOM):
        for dz, c_ref in enumerate((c0_ref, c1_ref, c2_ref, c3_ref)):
            out_ref[p, dz * 64 : (dz + 1) * 64, :] = c_ref[0:64, :]
        out_ref[p, 256:SPREAD, :] = tail


def rows_body(
    counts_ref, r0_ref, r1_ref, r2_ref, r3_ref, t0_ref, t1_ref, t2_ref, t3_ref, back_ref, rows_ref, base_ref, x_ref,
    gain_ref, grad_ref, wq_ref, wk_ref, wv_ref, wo_ref,
    out_ref, feature_ref, gain_grad_ref, dq_ref, dk_ref, dv_ref, at_ref,
):
    left = lax.broadcasted_iota(jnp.int32, (ROWS, 128), 1) < HEAD
    z, core = position()
    even = core == 0
    for dz, (r_ref, t_ref) in enumerate(zip((r0_ref, r1_ref, r2_ref, r3_ref), (t0_ref, t1_ref, t2_ref, t3_ref))):
        chip = (z + dz) & 3
        one, two = r_ref[0].astype(F32), t_ref[...].astype(F32)
        low, high = jnp.where(even, one, two), jnp.where(even, two, one)
        low0, low1 = low[:, 0:128], low[:, 128:256]
        high0, high1 = high[:, 0:128], high[:, 128:256]
        dq_ref[chip] = jnp.where(left, low0, pltpu.roll(high0, HEAD, 1)).astype(BF16)
        dk_ref[chip] = jnp.where(left, pltpu.roll(low0, HEAD, 1), high0).astype(BF16)
        dv_ref[chip] = jnp.where(left, low1, pltpu.roll(high1, HEAD, 1)).astype(BF16)
        at_ref[chip] = jnp.where(left, pltpu.roll(low1, HEAD, 1), high1).astype(BF16)

    def whole(ref):
        return jnp.concatenate([ref[m] for m in range(4)], axis=1)

    out_ref[...] = (base_ref[...] + dot(whole(at_ref), wo_ref[...])).astype(BF16)
    dnormed = dot(whole(dq_ref), wq_ref[...], NT) + dot(whole(dk_ref), wk_ref[...], NT)
    dnormed = dnormed + dot(whole(dv_ref), wv_ref[...], NT)
    row = lax.broadcasted_iota(jnp.int32, (ROWS, CAP), 0)
    slot = lax.broadcasted_iota(jnp.int32, (ROWS, CAP), 1)
    for k in range(4):
        hits = []
        for p in range(4 * k, 4 * k + 4):
            hit = (row == rows_ref[p : p + 1, :]) & (slot < counts_ref[p])
            hits.append(jnp.where(hit, 1.0, 0.0).astype(BF16))
        part = jnp.concatenate([back_ref[p] for p in range(4 * k, 4 * k + 4)], axis=0)
        dnormed = dnormed + dot(jnp.concatenate(hits, axis=1), part)
    x = x_ref[...].astype(F32)
    scale = lax.rsqrt(jnp.mean(x * x, axis=-1, keepdims=True) + EPS)
    gain_grad = jnp.sum(dnormed * (x * scale), axis=0, keepdims=True)
    gain_grad_ref[...] = jnp.zeros((8, 128), F32)
    for k in range(4):
        gain_grad_ref[k : k + 1, :] = gain_grad[:, k * 128 : (k + 1) * 128]
    scaled = dnormed * gain_ref[...]
    inner = jnp.mean(scaled * x, axis=-1, keepdims=True)
    dx = scale * scaled - x * (scale * scale * scale * inner)
    feature_ref[...] = (grad_ref[...].astype(F32) + dx).astype(BF16)


def weights_body(mine_ref, other_ref, out_ref, gain_ref):
    which = pl.program_id(0)
    z, core = position()

    @pl.when(which == 0)
    def _():
        gain = jnp.zeros((8, 128), F32)
        for p in range(DOM):
            tail = mine_ref[p, 320:SPREAD, :].astype(F32)
            gain = gain + (tail[0:8] + tail[8:16])
        for k in range(4):
            gain_ref[:, k * 128 : (k + 1) * 128] = gain[k : k + 1, :]

    for c in range(2):
        @pl.when(core == c)
        def _():
            def piece(h, p):
                start = ((z - (h >> 1)) & 3) * 64
                ref = mine_ref if h & 1 == c else other_ref
                return ref[p, pl.ds(pl.multiple_of(start, 64), 64), :].astype(F32)

            @pl.when(which < 3)
            def _():
                for b in range(4):
                    part = jnp.concatenate([piece(h, which * 4 + b) for h in range(BLK)], axis=0)
                    out_ref[0, b * 128 : (b + 1) * 128, :] = jnp.transpose(part)

            @pl.when(which == 3)
            def _():
                for h in range(BLK):
                    for b in range(4):
                        out_ref[0, h * 64 : (h + 1) * 64, b * 128 : (b + 1) * 128] = piece(h, 12 + b)

            @pl.when(which == 4)
            def _():
                for half in range(2):
                    ref = mine_ref if half == c else other_ref
                    for p in range(DOM):
                        top = half * 256 + p * 16
                        for b in range(4):
                            part = ref[p, 256 + b * 16 : 272 + b * 16, :]
                            out_ref[0, top : top + 16, b * 128 : (b + 1) * 128] = part.astype(F32)


def chip_shift(step, swap):
    return [(z * 2 + c, ((z + step) % 4) * 2 + (c ^ swap)) for z in range(4) for c in range(2)]


def along_chips(array, step):
    return lax.ppermute(array, "blk", chip_shift(step, 0))


def other_core(array):
    return lax.ppermute(array, "blk", chip_shift(0, 1))


def to_dom_peers(array):
    return lax.all_to_all(array, "dom", split_axis=0, concat_axis=0, tiled=True)


def local(
    x, gain, wq, wk, wv, wo, wm, cluster, pattern, send_rows, send_counts, edge_src, edge_dst, out_grad
):
    gain_row = gain.reshape(1, D)
    pay, outgoing = call(
        norm_body,
        (shape((PAY, D), BF16), shape((DOM, CAP, D), BF16)),
        (pattern, send_counts, x, gain_row, cluster.reshape(1, ROWS), out_grad, send_rows),
        scalars=2,
        micros=4,
    )
    incoming = to_dom_peers(outgoing)
    near, far = along_chips(pay, 1), along_chips(pay, 3)

    counts_t, degree, slot_grads, wqkv, wo_head = call(
        edges_body,
        (
            shape((1024, 512), BF16), shape((ROWS, 128), F32), shape((DOM, CAP, D), BF16),
            shape((192, D), BF16), shape((HEAD, D), BF16),
        ),
        (edge_src.reshape(32, 128), edge_dst.reshape(32, 128), out_grad, wm, wq, wk, wv, wo),
        scratch=[pltpu.VMEM((512, 1024), F32)],
        micros=10,
    )
    near, far, degree = lax.optimization_barrier((near, far, degree))
    pays = [pay, near, along_chips(near[0:ROWS], 1), along_chips(far[ROWS:PAY], 3), far]
    pays = pays + [other_core(part) for part in pays]
    incoming, slot_grads = lax.optimization_barrier((incoming, slot_grads))
    back = to_dom_peers(slot_grads)

    base, mine, other = call(
        mean_body,
        (shape((ROWS, D), F32), shape((DOM, 64, 128), BF16), shape((DOM, 64, 128), BF16)),
        (counts_t, degree, incoming, x, out_grad, wm),
        micros=4,
    )

    *results, chunks = call(
        attention_body,
        (*[shape((2, ROWS, 256), BF16)] * 4, shape((DOM, 128, 128), BF16)),
        (*pays, wqkv, wo_head, mine, other_core(other)),
        scratch=[
            pltpu.VMEM((BLK, 128, ROWS), F32),
            pltpu.VMEM((BLK, 8, ROWS), F32),
            pltpu.VMEM((BLK, 128, ROWS), BF16),
            pltpu.VMEM((BLK, HEAD, ROWS), BF16),
            pltpu.VMEM((BLK, ROWS, 128), BF16),
            pltpu.VMEM((BLK, ROWS, 128), BF16),
            pltpu.VMEM((BLK, 80, ROWS), BF16),
            pltpu.VMEM((BLK, BLK, ROWS, ROWS), BF16),
            pltpu.VMEM((BLK, HEAD, ROWS), F32),
            pltpu.VMEM((BLK, HEAD, ROWS), F32),
            pltpu.VMEM((BLK, HEAD, ROWS), F32),
            pltpu.VMEM((BLK, HEAD, ROWS), BF16),
            pltpu.VMEM((BLK, HEAD, ROWS), F32),
            pltpu.VMEM((BLK, BLK, ROWS, ROWS), BF16),
            pltpu.VMEM((BLK, ROWS, 128), BF16),
            pltpu.VMEM((BLK, ROWS, 128), BF16),
        ],
        micros=12,
    )
    chunks, back = lax.optimization_barrier((chunks, back))
    chunks = to_dom_peers(chunks)

    results = [results[0]] + [along_chips(results[dz], -dz) for dz in (1, 2, 3)]
    *results, back = lax.optimization_barrier((*results, back))
    swapped = [other_core(part[1]) for part in results]
    layer_out, feature_grad, gain_part = call(
        rows_body,
        (shape((ROWS, D), BF16), shape((ROWS, D), BF16), shape((8, 128), F32)),
        (send_counts, *results, *swapped, back, send_rows, base, x, gain_row, out_grad, wq, wk, wv, wo),
        scratch=[pltpu.VMEM((4, ROWS, 128), BF16)] * 4,
        scalars=1,
        micros=0.001,
    )
    chunk = call(
        chunk_sum_body, shape((CHUNK, 128), BF16), (chunks, gain_part, other_core(gain_part)), micros=1
    )
    chunk_parts = [chunk] + [along_chips(chunk, step) for step in (1, 2, 3)]
    spread = call(spread_body, shape((DOM, SPREAD, 128), BF16), chunk_parts, scratch=[pltpu.VMEM((4, 80, 128), F32)])
    gathered = to_dom_peers(spread)
    whole = pl.BlockSpec((DOM, SPREAD, 128), lambda t: (0, 0, 0))
    weight_grads, gain_grad = pl.pallas_call(
        weights_body,
        grid=(5,),
        out_shape=(shape((5, D, D), F32), shape((1, D), F32)),
        in_specs=[whole, whole],
        out_specs=(pl.BlockSpec((1, D, D), lambda t: (t, 0, 0)), pl.BlockSpec((1, D), lambda t: (0, 0))),
    )(gathered, other_core(gathered))
    return layer_out, feature_grad, weight_grads, gain_grad.reshape(D)


def solution(mesh):
    both = ("dom", "blk")
    placed = (
        P(both, None), P(), P(), P(), P(), P(), P(), P(both), P(both, None), P(both, None), P(both), P(both), P(both),
        P(both, None),
    )
    return jax.shard_map(
        local,
        mesh=mesh,
        in_specs=placed,
        out_specs=(P(both, None), P(both, None), P(), P()),
        check_vma=False,
    )
```

```python
import math

import jax
import jax.numpy as jnp
from jax import lax
from jax.experimental import pallas as pl
from jax.experimental.pallas import tpu as pltpu
from jax.sharding import PartitionSpec as P

F32 = jnp.float32
BF16 = jnp.bfloat16
EPS = 1e-06
D = 512
ROWS = 256
HEAD = 64
BLK = 8
DOM = 16
CAP = 128
EDGES = 4096
PAY = 2 * ROWS + 16
LOG2E = math.log2(math.e)
SCORE_MUL = LOG2E / 8.0
SCORE_SUB = (8.0 + 256.0) * LOG2E
CHUNK = 64 + 64 + 16
SPREAD = 4 * 64 + 64 + 16
PART = 160

NT = (((1,), (1,)), ((), ()))
NN = (((1,), (0,)), ((), ()))


def dot(a, b, dims=NN):
    return lax.dot_general(a, b, dims, preferred_element_type=F32)


def call(body, out_shape, operands, scratch=(), scalars=0, micros=2):
    specs = [pl.BlockSpec(memory_space=pltpu.SMEM)] * scalars
    specs += [pl.BlockSpec(memory_space=pltpu.VMEM)] * (len(operands) - scalars)
    return pl.pallas_call(
        body,
        out_shape=out_shape,
        in_specs=specs,
        out_specs=jax.tree.map(lambda _: pl.BlockSpec(memory_space=pltpu.VMEM), out_shape),
        scratch_shapes=list(scratch),
        cost_estimate=pl.CostEstimate(flops=int(micros * 1e9), transcendentals=0, bytes_accessed=1 << 20),
    )(*operands)


def shape(dims, dtype):
    return jax.ShapeDtypeStruct(dims, dtype)


def dom_position():
    me = lax.axis_index("dom").astype(jnp.int32)
    return lax.shift_right_logical(me, 2), me & 3


def position():
    me = lax.axis_index("blk").astype(jnp.int32)
    return lax.shift_right_logical(me, 1), me & 1


def norm_body(pattern_ref, counts_ref, x_ref, gain_ref, label_ref, grad_ref, rows_ref, out_ref, slots_ref):
    x = x_ref[...].astype(F32)
    scale = lax.rsqrt(jnp.mean(x * x, axis=-1, keepdims=True) + EPS)
    normed = (x * scale * gain_ref[...]).astype(BF16)
    out_ref[0:ROWS, :] = normed
    out_ref[ROWS : 2 * ROWS, :] = grad_ref[...]
    row = lax.broadcasted_iota(jnp.int32, (16, ROWS), 0)
    lane = lax.broadcasted_iota(jnp.int32, (16, ROWS), 1)
    tail = jnp.where(row == 0, label_ref[...].astype(F32), 0.0)
    for b in range(BLK):
        flag = jnp.where(pattern_ref[0, b] == 1, 1.0, 0.0)
        tail = jnp.where((row == 1 + b) & (lane >= 0), flag, tail)
    out_ref[2 * ROWS : PAY, 0:ROWS] = tail.astype(BF16)
    out_ref[2 * ROWS : PAY, ROWS:D] = jnp.zeros((16, D - ROWS), BF16)
    columns = jnp.transpose(rows_ref[...].astype(F32))
    lane = lax.broadcasted_iota(jnp.int32, (CAP, ROWS), 1).astype(F32)
    slot = lax.broadcasted_iota(jnp.int32, (CAP, ROWS), 0)
    for p in range(DOM):
        hit = (lane == columns[:, p : p + 1]) & (slot < counts_ref[p])
        slots_ref[p] = dot(jnp.where(hit, 1.0, 0.0).astype(BF16), normed).astype(BF16)


E_ROWS = 4


def edges_body(
    src_ref, dst_ref, grad_ref, w_ref, wq_ref, wk_ref, wv_ref, wo_ref,
    counts_t_ref, degree_ref, slots_ref, wqkv_ref, wo_head_ref, acc_ref,
):
    z, core = position()
    for m in range(4):
        @pl.when(z == m)
        def _():
            for k, ref in enumerate((wq_ref, wk_ref, wv_ref)):
                pair = jnp.transpose(ref[:, m * 128 : (m + 1) * 128].astype(F32))
                picked = jnp.where(core == 0, pair[0:HEAD], pair[HEAD:128])
                wqkv_ref[k * HEAD : (k + 1) * HEAD, :] = picked.astype(BF16)
            for c in range(2):
                @pl.when(core == c)
                def _():
                    wo_head_ref[...] = wo_ref[m * 128 + c * HEAD : m * 128 + (c + 1) * HEAD, :]

    low_row = lax.broadcasted_iota(jnp.int32, (512, E_ROWS * 128), 0)
    high_row = lax.broadcasted_iota(jnp.int32, (1024, E_ROWS * 128), 0)
    for step in range(EDGES // (E_ROWS * 128)):
        rows = [step * E_ROWS + k for k in range(E_ROWS)]
        src = jnp.concatenate([src_ref[k : k + 1, :] for k in rows], axis=1)
        dst = jnp.concatenate([dst_ref[k : k + 1, :] for k in rows], axis=1)
        low = jnp.where(low_row == (src & 511), 1.0, 0.0).astype(BF16)
        high = jnp.where(high_row == ((src >> 9) * 256 + dst), 1.0, 0.0).astype(BF16)
        part = dot(low, high, NT)
        if step == 0:
            acc_ref[...] = part
        else:
            acc_ref[...] += part
    counts = acc_ref[...]
    per_row = jnp.sum(counts, axis=0, keepdims=True)
    per_row = per_row[:, 0:256] + per_row[:, 256:512] + per_row[:, 512:768] + per_row[:, 768:1024]
    degree = jnp.transpose(jnp.broadcast_to(jnp.maximum(per_row, 1.0), (128, ROWS)))
    degree_ref[...] = degree
    counts_t_ref[...] = jnp.transpose(counts).astype(BF16)
    counts = counts.astype(BF16)
    inverse = 1.0 / degree[:, 0:1]
    message = (dot(grad_ref[...], w_ref[...], NT) * inverse).astype(BF16)
    for high in range(4):
        part = dot(counts[:, high * 256 : (high + 1) * 256], message).astype(BF16)
        for k in range(4):
            slots_ref[high * 4 + k] = part[k * CAP : (k + 1) * CAP, :]


def mean_body(counts_t_ref, degree_ref, table_ref, x_ref, grad_ref, w_ref, base_ref, mine_ref, other_ref):
    total = jnp.zeros((ROWS, D), F32)
    for high in range(4):
        table = jnp.concatenate([table_ref[high * 4 + k] for k in range(4)], axis=0)
        total = total + dot(counts_t_ref[high * 256 : (high + 1) * 256, :], table)
    mean_rows = (total / degree_ref[:, 0:1]).astype(BF16)
    base_ref[...] = x_ref[...].astype(F32) + dot(mean_rows, w_ref[...])
    dw = dot(jnp.transpose(mean_rows.astype(F32)).astype(BF16), grad_ref[...]).astype(BF16)
    z, core = position()
    for half in range(2):
        def fill(ref):
            for p in range(DOM):
                top = half * 256 + p * 16
                for b in range(4):
                    ref[p, b * 16 : (b + 1) * 16, :] = dw[top : top + 16, b * 128 : (b + 1) * 128]

        @pl.when(core == half)
        def _():
            fill(mine_ref)

        @pl.when(core != half)
        def _():
            fill(other_ref)


def attention_body(
    p0_ref, p1_ref, t2_ref, b2_ref, p3_ref, p4_ref, p5_ref, t6_ref, b6_ref, p7_ref, wqkv_ref, wo_ref, mine_ref, other_ref,
    r0_ref, r1_ref, r2_ref, r3_ref, chunks_ref,
    y_ref, s_ref, qt_ref, kt_ref, k_ref, v_ref, vt_ref, w_ref, dq_ref, dk_ref, dv_ref, at_ref, ga_ref, sl_ref, qr_ref, gr_ref,
):
    pays = (p0_ref, p1_ref, (t2_ref, b2_ref), p3_ref, p4_ref, p5_ref, (t6_ref, b6_ref), p7_ref)

    def normed_of(pay):
        return pay[0][...] if isinstance(pay, tuple) else pay[0:ROWS, :]

    def grads_of(pay):
        return pay[1][0:ROWS, :] if isinstance(pay, tuple) else pay[ROWS : 2 * ROWS, :]

    def tail_of(pay):
        return pay[1][ROWS : PAY - ROWS, 0:ROWS] if isinstance(pay, tuple) else pay[2 * ROWS : PAY, 0:ROWS]

    outs = (r0_ref, r1_ref, r2_ref, r3_ref)
    z, core = position()
    row = lax.broadcasted_iota(jnp.int32, (HEAD, ROWS), 0)
    number = row.astype(F32)

    def head_scale(part):
        return lax.rsqrt(jnp.sum(part * part, axis=0, keepdims=True) * (1.0 / HEAD) + EPS)

    for r in range(BLK):
        pay = pays[r]
        projected = dot(wqkv_ref[...], normed_of(pay), NT)
        query, key, value = projected[0:HEAD], projected[HEAD:128], projected[128:192]
        scale_q, scale_k = head_scale(query), head_scale(key)
        query, key = query * scale_q, key * scale_k
        y_ref[r, 0:HEAD] = query
        y_ref[r, HEAD:128] = key
        s_ref[r, 0:1] = scale_q
        s_ref[r, 1:2] = scale_k
        tail = tail_of(pay).astype(F32)
        same = jnp.where(number == tail[0:1], 32.0, 0.0)
        sender = ((z - (r & 3)) & 3) * 2 + (core ^ (r >> 2))
        wanted = jnp.concatenate([jnp.zeros((16, ROWS), F32), tail[1:9] * 32.0, jnp.zeros((40, ROWS), F32)], axis=0)
        owner = jnp.where(row == 16 + sender, 32.0, 0.0)
        qt_ref[r] = jnp.concatenate([query, same + wanted], axis=0).astype(BF16)
        key = jnp.concatenate([key, same + owner], axis=0)
        kt_ref[r] = key[0:HEAD].astype(BF16)
        k_ref[r] = jnp.transpose(key).astype(BF16)
        value = jnp.concatenate([value, jnp.where(row < 2, 1.0, 0.0)], axis=0)
        vt_ref[r] = value[0:80].astype(BF16)
        v_ref[r] = jnp.transpose(value).astype(BF16)
        ga_ref[r] = dot(wo_ref[...], grads_of(pay), NT)
        qr_ref[r] = jnp.transpose(qt_ref[r].astype(F32)).astype(BF16)

    keys_t = jnp.concatenate([kt_ref[j] for j in range(BLK)], axis=1)
    values_t = jnp.concatenate([vt_ref[j] for j in range(BLK)], axis=1)

    def query_block(i, carry):
        query = qt_ref[i]
        for j in range(BLK):
            scores = dot(k_ref[j], query)
            w_ref[i, j] = jnp.exp2(scores * SCORE_MUL - SCORE_SUB).astype(BF16)
        numer = dot(values_t, w_ref[i].reshape(BLK * ROWS, ROWS))
        inverse = 1.0 / numer[HEAD : HEAD + 1]
        attn = (numer[0:HEAD] * inverse).astype(BF16)
        at_ref[i] = attn
        grad_attn = ga_ref[i]
        minus = jnp.sum(grad_attn * attn.astype(F32), axis=0, keepdims=True) * (-inverse)
        coarse = minus.astype(BF16).astype(F32)
        extra = jnp.where(row == 0, coarse, jnp.where(row == 1, minus - coarse, 0.0))
        grad = jnp.concatenate([grad_attn * inverse, extra], axis=0).astype(BF16)
        gr_ref[i] = jnp.transpose(grad.astype(F32)).astype(BF16)
        for j in range(BLK):
            sl_ref[i, j] = (w_ref[i, j].astype(F32) * dot(v_ref[j], grad)).astype(BF16)
        dq_ref[i] = dot(keys_t, sl_ref[i].reshape(BLK * ROWS, ROWS))
        return carry

    lax.fori_loop(0, BLK, query_block, 0)

    queries = jnp.concatenate([qr_ref[i] for i in range(BLK)], axis=0)
    grads = jnp.concatenate([gr_ref[i] for i in range(BLK)], axis=0)

    def key_block(j, carry):
        slopes = jnp.concatenate([sl_ref[i, j] for i in range(BLK)], axis=1)
        dk_ref[j] = jnp.transpose(dot(slopes, queries))[0:HEAD]
        weights = jnp.concatenate([w_ref[i, j] for i in range(BLK)], axis=1)
        dv_ref[j] = jnp.transpose(dot(weights, grads))[0:HEAD]
        return carry

    lax.fori_loop(0, BLK, key_block, 0)

    dw = jnp.zeros((192, D), F32)
    dwo = jnp.zeros((HEAD, D), F32)
    for r in range(BLK):
        pay = pays[r]

        def pull(grad, y, scale):
            grad = grad * (8.0 / HEAD)
            return scale * (grad - y * (jnp.sum(y * grad, axis=0, keepdims=True) * (1.0 / HEAD)))

        dquery = pull(dq_ref[r], y_ref[r, 0:HEAD], s_ref[r, 0:1])
        dkey = pull(dk_ref[r], y_ref[r, HEAD:128], s_ref[r, 1:2])
        first = jnp.concatenate([dquery, dkey], axis=0)
        second = jnp.concatenate([dv_ref[r], at_ref[r].astype(F32)], axis=0)
        outs[r & 3][r >> 2, :, 0:128] = jnp.transpose(first).astype(BF16)
        outs[r & 3][r >> 2, :, 128:256] = jnp.transpose(second).astype(BF16)
        left = jnp.concatenate([first, second[0:HEAD]], axis=0).astype(BF16)
        dw = dw + dot(left, normed_of(pay))
        dwo = dwo + dot(at_ref[r], grads_of(pay))
    dw = jnp.concatenate([dw, dwo], axis=0).astype(BF16)
    for a in range(4):
        for b in range(4):
            p = a * 4 + b
            chunks_ref[p, 0:64, :] = dw[a * 64 : (a + 1) * 64, b * 128 : (b + 1) * 128]
            chunks_ref[p, 64:128, :] = (mine_ref[p].astype(F32) + other_ref[p].astype(F32)).astype(BF16)


def chunk_sum_body(in_ref, g0_ref, g1_ref, wqkv_ref, out_ref, extra_ref):
    total = in_ref[0].astype(F32)
    for p in range(1, DOM):
        total = total + in_ref[p].astype(F32)
    out_ref[0:128, :] = total.astype(BF16)
    z, core = position()
    kind, lanes = dom_position()
    one, two = g0_ref[...], g1_ref[...]
    extra_ref[...] = jnp.where(core == 0, one, two) + jnp.where(core == 0, two, one)
    for b in range(4):
        @pl.when((kind < 3) & (lanes == b))
        def _():
            start = pl.multiple_of(jnp.minimum(kind, 2) * HEAD, HEAD)
            weights = wqkv_ref[pl.ds(start, HEAD), b * 128 : (b + 1) * 128].astype(F32)
            extra_ref[4:5, :] = jnp.sum(weights * total[0:HEAD], axis=0, keepdims=True)
    extra = extra_ref[...]
    coarse = extra.astype(BF16).astype(F32)
    out_ref[128:CHUNK, :] = jnp.concatenate([coarse, extra - coarse], axis=0).astype(BF16)


def spread_body(c0_ref, c1_ref, c2_ref, c3_ref, first_ref, second_ref, parts_ref):
    z, core = position()
    for dz, c_ref in enumerate((c0_ref, c1_ref, c2_ref, c3_ref)):
        parts_ref[dz] = c_ref[64:CHUNK, :].astype(F32)
    total = jnp.zeros((80, 128), F32)
    for chip in range(4):
        total = total + parts_ref[(z - chip) & 3]
    gain = total[64:72] + total[72:80]
    coarse = gain.astype(BF16).astype(F32)
    tail = jnp.concatenate([total[0:64], coarse, gain - coarse], axis=0).astype(BF16)
    whole = jnp.concatenate([c_ref[0:64, :] for c_ref in (c0_ref, c1_ref, c2_ref, c3_ref)] + [tail], axis=0)
    first_ref[...] = whole[0:PART]
    second_ref[...] = whole[PART:SPREAD]


def halo_body(counts_ref, back_ref, rows_ref, x_ref, out_ref, gain_grad_ref):
    row = lax.broadcasted_iota(jnp.int32, (ROWS, CAP), 0)
    slot = lax.broadcasted_iota(jnp.int32, (ROWS, CAP), 1)
    total = jnp.zeros((ROWS, D), F32)
    for k in range(4):
        hits = []
        for p in range(4 * k, 4 * k + 4):
            hit = (row == rows_ref[p : p + 1, :]) & (slot < counts_ref[p])
            hits.append(jnp.where(hit, 1.0, 0.0).astype(BF16))
        part = jnp.concatenate([back_ref[p] for p in range(4 * k, 4 * k + 4)], axis=0)
        total = total + dot(jnp.concatenate(hits, axis=1), part)
    out_ref[...] = total
    x = x_ref[...].astype(F32)
    scale = lax.rsqrt(jnp.mean(x * x, axis=-1, keepdims=True) + EPS)
    gain_grad = jnp.sum(total * (x * scale), axis=0, keepdims=True)
    gain_grad_ref[...] = jnp.zeros((8, 128), F32)
    for k in range(4):
        gain_grad_ref[k : k + 1, :] = gain_grad[:, k * 128 : (k + 1) * 128]


def rows_body(
    r0_ref, r1_ref, r2_ref, r3_ref, t0_ref, t1_ref, t2_ref, t3_ref, halo_ref, base_ref, x_ref,
    gain_ref, grad_ref, wq_ref, wk_ref, wv_ref, wo_ref,
    out_ref, feature_ref, dq_ref, dk_ref, dv_ref, at_ref,
):
    left = lax.broadcasted_iota(jnp.int32, (ROWS, 128), 1) < HEAD
    z, core = position()
    even = core == 0
    for dz, (r_ref, t_ref) in enumerate(zip((r0_ref, r1_ref, r2_ref, r3_ref), (t0_ref, t1_ref, t2_ref, t3_ref))):
        chip = (z + dz) & 3
        one, two = r_ref[0].astype(F32), t_ref[...].astype(F32)
        low, high = jnp.where(even, one, two), jnp.where(even, two, one)
        low0, low1 = low[:, 0:128], low[:, 128:256]
        high0, high1 = high[:, 0:128], high[:, 128:256]
        dq_ref[chip] = jnp.where(left, low0, pltpu.roll(high0, HEAD, 1)).astype(BF16)
        dk_ref[chip] = jnp.where(left, pltpu.roll(low0, HEAD, 1), high0).astype(BF16)
        dv_ref[chip] = jnp.where(left, low1, pltpu.roll(high1, HEAD, 1)).astype(BF16)
        at_ref[chip] = jnp.where(left, pltpu.roll(low1, HEAD, 1), high1).astype(BF16)

    def whole(ref):
        return jnp.concatenate([ref[m] for m in range(4)], axis=1)

    out_ref[...] = (base_ref[...] + dot(whole(at_ref), wo_ref[...])).astype(BF16)
    dnormed = dot(whole(dq_ref), wq_ref[...], NT) + dot(whole(dk_ref), wk_ref[...], NT)
    dnormed = dnormed + dot(whole(dv_ref), wv_ref[...], NT) + halo_ref[...]
    x = x_ref[...].astype(F32)
    scale = lax.rsqrt(jnp.mean(x * x, axis=-1, keepdims=True) + EPS)
    scaled = dnormed * gain_ref[...]
    inner = jnp.mean(scaled * x, axis=-1, keepdims=True)
    dx = scale * scaled - x * (scale * scale * scale * inner)
    feature_ref[...] = (grad_ref[...].astype(F32) + dx).astype(BF16)


def weights_body(*refs):
    gain_in_ref, out_ref, gain_ref, all_ref = refs[16:20]
    which = pl.program_id(0)

    @pl.when(which == 0)
    def _():
        z, core = position()
        x, y = dom_position()
        for c in range(2):
            owner = core ^ c
            for dx in range(4):
                for dy in range(4):
                    p = ((x - dx) & 3) * 4 + ((y - dy) & 3)
                    all_ref[owner, p, 0:PART, :] = refs[c * 8 + dx][dy]
                    all_ref[owner, p, PART:SPREAD, :] = refs[c * 8 + 4 + dy][dx]
        gain = jnp.zeros((8, 128), F32)
        through = []
        for p in range(DOM):
            tails = [all_ref[c, p, 320:SPREAD, :].astype(F32) for c in range(2)]
            tails = [tail[0:8] + tail[8:16] for tail in tails]
            gain = gain + jnp.where(core == 0, tails[0], tails[1])
            through.append(tails[0] + tails[1])
        for b in range(4):
            part = (through[b] + through[4 + b] + through[8 + b])[4:5]
            lanes = slice(b * 128, (b + 1) * 128)
            gain_ref[:, lanes] = gain[b : b + 1] + part / gain_in_ref[:, lanes]

    def piece(h, p):
        z, core = position()
        start = pl.multiple_of(((z - (h >> 1)) & 3) * 64, 64)
        return all_ref[h & 1, p, pl.ds(start, 64), :].astype(F32)

    @pl.when(which < 3)
    def _():
        for b in range(4):
            part = jnp.concatenate([piece(h, which * 4 + b) for h in range(BLK)], axis=0)
            out_ref[0, b * 128 : (b + 1) * 128, :] = jnp.transpose(part)

    @pl.when(which == 3)
    def _():
        for h in range(BLK):
            for b in range(4):
                out_ref[0, h * 64 : (h + 1) * 64, b * 128 : (b + 1) * 128] = piece(h, 12 + b)

    @pl.when(which == 4)
    def _():
        for half in range(2):
            for p in range(DOM):
                top = half * 256 + p * 16
                for b in range(4):
                    part = all_ref[half, p, 256 + b * 16 : 272 + b * 16, :]
                    out_ref[0, top : top + 16, b * 128 : (b + 1) * 128] = part.astype(F32)


def chip_shift(step, swap):
    return [(z * 2 + c, ((z + step) % 4) * 2 + (c ^ swap)) for z in range(4) for c in range(2)]


def along_chips(array, step):
    return lax.ppermute(array, "blk", chip_shift(step, 0))


def other_core(array):
    return lax.ppermute(array, "blk", chip_shift(0, 1))


def along_dom(array, x_step, y_step):
    pairs = [(x * 4 + y, (x + x_step) % 4 * 4 + (y + y_step) % 4) for x in range(4) for y in range(4)]
    return lax.ppermute(array, "dom", pairs)


def to_dom_peers(array):
    return lax.all_to_all(array, "dom", split_axis=0, concat_axis=0, tiled=True)


def local(
    x, gain, wq, wk, wv, wo, wm, cluster, pattern, send_rows, send_counts, edge_src, edge_dst, out_grad
):
    gain_row = gain.reshape(1, D)
    pay, outgoing = call(
        norm_body,
        (shape((PAY, D), BF16), shape((DOM, CAP, D), BF16)),
        (pattern, send_counts, x, gain_row, cluster.reshape(1, ROWS), out_grad, send_rows),
        scalars=2,
        micros=4,
    )
    incoming = to_dom_peers(outgoing)
    near, far = along_chips(pay, 1), along_chips(pay, 3)

    counts_t, degree, slot_grads, wqkv, wo_head = call(
        edges_body,
        (
            shape((1024, 512), BF16), shape((ROWS, 128), F32), shape((DOM, CAP, D), BF16),
            shape((192, D), BF16), shape((HEAD, D), BF16),
        ),
        (edge_src.reshape(32, 128), edge_dst.reshape(32, 128), out_grad, wm, wq, wk, wv, wo),
        scratch=[pltpu.VMEM((512, 1024), F32)],
        micros=10,
    )
    near, far, degree = lax.optimization_barrier((near, far, degree))
    pays = [pay, near, along_chips(near[0:ROWS], 1), along_chips(far[ROWS:PAY], 3), far]
    pays = pays + [other_core(part) for part in pays]
    incoming, slot_grads = lax.optimization_barrier((incoming, slot_grads))
    back = to_dom_peers(slot_grads)

    base, mine, other = call(
        mean_body,
        (shape((ROWS, D), F32), shape((DOM, 64, 128), BF16), shape((DOM, 64, 128), BF16)),
        (counts_t, degree, incoming, x, out_grad, wm),
        micros=4,
    )

    *results, chunks = call(
        attention_body,
        (*[shape((2, ROWS, 256), BF16)] * 4, shape((DOM, 128, 128), BF16)),
        (*pays, wqkv, wo_head, mine, other_core(other)),
        scratch=[
            pltpu.VMEM((BLK, 128, ROWS), F32),
            pltpu.VMEM((BLK, 8, ROWS), F32),
            pltpu.VMEM((BLK, 128, ROWS), BF16),
            pltpu.VMEM((BLK, HEAD, ROWS), BF16),
            pltpu.VMEM((BLK, ROWS, 128), BF16),
            pltpu.VMEM((BLK, ROWS, 128), BF16),
            pltpu.VMEM((BLK, 80, ROWS), BF16),
            pltpu.VMEM((BLK, BLK, ROWS, ROWS), BF16),
            pltpu.VMEM((BLK, HEAD, ROWS), F32),
            pltpu.VMEM((BLK, HEAD, ROWS), F32),
            pltpu.VMEM((BLK, HEAD, ROWS), F32),
            pltpu.VMEM((BLK, HEAD, ROWS), BF16),
            pltpu.VMEM((BLK, HEAD, ROWS), F32),
            pltpu.VMEM((BLK, BLK, ROWS, ROWS), BF16),
            pltpu.VMEM((BLK, ROWS, 128), BF16),
            pltpu.VMEM((BLK, ROWS, 128), BF16),
        ],
        micros=12,
    )
    chunks, back, *results = lax.optimization_barrier((chunks, back, *results))
    chunks = to_dom_peers(chunks)
    halo, gain_part = call(
        halo_body,
        (shape((ROWS, D), F32), shape((8, 128), F32)),
        (send_counts, back, send_rows, x),
        scalars=1,
        micros=3,
    )
    results = [results[0]] + [along_chips(results[dz], -dz) for dz in (1, 2, 3)]
    swapped = [other_core(part[1]) for part in results]
    chunks, *swapped = lax.optimization_barrier((chunks, *swapped))
    chunk = call(
        chunk_sum_body,
        shape((CHUNK, 128), BF16),
        (chunks, gain_part, other_core(gain_part), wqkv),
        scratch=[pltpu.VMEM((8, 128), F32)],
        micros=1,
    )
    chunk_parts = [chunk] + [along_chips(chunk, step) for step in (1, 2, 3)]
    first, second = call(
        spread_body,
        (shape((PART, 128), BF16), shape((SPREAD - PART, 128), BF16)),
        chunk_parts,
        scratch=[pltpu.VMEM((4, 80, 128), F32)],
        micros=1,
    )
    first = jnp.stack([first] + [along_dom(first, 0, step) for step in (1, 2, 3)])
    second = jnp.stack([second] + [along_dom(second, step, 0) for step in (1, 2, 3)])
    parts = [first] + [along_dom(first, step, 0) for step in (1, 2, 3)]
    parts = parts + [second] + [along_dom(second, 0, step) for step in (1, 2, 3)]
    parts = parts + [other_core(part) for part in parts]
    weight_grads, gain_grad = pl.pallas_call(
        weights_body,
        grid=(5,),
        out_shape=(shape((5, D, D), F32), shape((1, D), F32)),
        in_specs=[pl.BlockSpec(part.shape, lambda t: (0, 0, 0)) for part in parts] + [pl.BlockSpec((1, D), lambda t: (0, 0))],
        out_specs=(pl.BlockSpec((1, D, D), lambda t: (t, 0, 0)), pl.BlockSpec((1, D), lambda t: (0, 0))),
        scratch_shapes=[pltpu.VMEM((2, DOM, SPREAD, 128), BF16)],
    )(*parts, gain_row)

    layer_out, feature_grad = call(
        rows_body,
        (shape((ROWS, D), BF16), shape((ROWS, D), BF16)),
        (*results, *swapped, halo, base, x, gain_row, out_grad, wq, wk, wv, wo),
        scratch=[pltpu.VMEM((4, ROWS, 128), BF16)] * 4,
        micros=5,
    )
    return layer_out, feature_grad, weight_grads, gain_grad.reshape(D)


def solution(mesh):
    both = ("dom", "blk")
    placed = (
        P(both, None), P(), P(), P(), P(), P(), P(), P(both), P(both, None), P(both, None), P(both), P(both), P(both),
        P(both, None),
    )
    return jax.shard_map(
        local,
        mesh=mesh,
        in_specs=placed,
        out_specs=(P(both, None), P(both, None), P(), P()),
        check_vma=False,
    )
```

```python
import math

import jax
import jax.numpy as jnp
from jax import lax
from jax.experimental import pallas as pl
from jax.experimental.pallas import tpu as pltpu
from jax.sharding import PartitionSpec as P

F32 = jnp.float32
BF16 = jnp.bfloat16
EPS = 1e-06
D = 512
ROWS = 256
HEAD = 64
BLK = 8
DOM = 16
CAP = 128
EDGES = 4096
PAY = 2 * ROWS + 16
LOG2E = math.log2(math.e)
SCORE_MUL = LOG2E / 8.0
SCORE_SUB = (8.0 + 256.0) * LOG2E
CHUNK = 64 + 64 + 16
SPREAD = 4 * 64 + 64 + 16

NT = (((1,), (1,)), ((), ()))
NN = (((1,), (0,)), ((), ()))


def dot(a, b, dims=NN):
    return lax.dot_general(a, b, dims, preferred_element_type=F32)


def call(body, out_shape, operands, scratch=(), scalars=0, micros=2):
    specs = [pl.BlockSpec(memory_space=pltpu.SMEM)] * scalars
    specs += [pl.BlockSpec(memory_space=pltpu.VMEM)] * (len(operands) - scalars)
    return pl.pallas_call(
        body,
        out_shape=out_shape,
        in_specs=specs,
        out_specs=jax.tree.map(lambda _: pl.BlockSpec(memory_space=pltpu.VMEM), out_shape),
        scratch_shapes=list(scratch),
        cost_estimate=pl.CostEstimate(flops=int(micros * 1e9), transcendentals=0, bytes_accessed=1 << 20),
    )(*operands)


def shape(dims, dtype):
    return jax.ShapeDtypeStruct(dims, dtype)


def dom_position():
    me = lax.axis_index("dom").astype(jnp.int32)
    return lax.shift_right_logical(me, 2), me & 3


def position():
    me = lax.axis_index("blk").astype(jnp.int32)
    return lax.shift_right_logical(me, 1), me & 1


def norm_body(pattern_ref, counts_ref, x_ref, gain_ref, label_ref, grad_ref, rows_ref, out_ref, slots_ref):
    x = x_ref[...].astype(F32)
    scale = lax.rsqrt(jnp.mean(x * x, axis=-1, keepdims=True) + EPS)
    normed = (x * scale * gain_ref[...]).astype(BF16)
    out_ref[0:ROWS, :] = normed
    out_ref[ROWS : 2 * ROWS, :] = grad_ref[...]
    row = lax.broadcasted_iota(jnp.int32, (16, ROWS), 0)
    lane = lax.broadcasted_iota(jnp.int32, (16, ROWS), 1)
    tail = jnp.where(row == 0, label_ref[...].astype(F32), 0.0)
    for b in range(BLK):
        flag = jnp.where(pattern_ref[0, b] == 1, 1.0, 0.0)
        tail = jnp.where((row == 1 + b) & (lane >= 0), flag, tail)
    out_ref[2 * ROWS : PAY, 0:ROWS] = tail.astype(BF16)
    out_ref[2 * ROWS : PAY, ROWS:D] = jnp.zeros((16, D - ROWS), BF16)
    columns = jnp.transpose(rows_ref[...].astype(F32))
    lane = lax.broadcasted_iota(jnp.int32, (CAP, ROWS), 1).astype(F32)
    slot = lax.broadcasted_iota(jnp.int32, (CAP, ROWS), 0)
    for p in range(DOM):
        hit = (lane == columns[:, p : p + 1]) & (slot < counts_ref[p])
        slots_ref[p] = dot(jnp.where(hit, 1.0, 0.0).astype(BF16), normed).astype(BF16)


E_ROWS = 4


def edges_body(
    src_ref, dst_ref, grad_ref, w_ref, wq_ref, wk_ref, wv_ref, wo_ref,
    counts_t_ref, degree_ref, slots_ref, wqkv_ref, wo_head_ref, acc_ref,
):
    z, core = position()
    for m in range(4):
        @pl.when(z == m)
        def _():
            for k, ref in enumerate((wq_ref, wk_ref, wv_ref)):
                pair = jnp.transpose(ref[:, m * 128 : (m + 1) * 128].astype(F32))
                picked = jnp.where(core == 0, pair[0:HEAD], pair[HEAD:128])
                wqkv_ref[k * HEAD : (k + 1) * HEAD, :] = picked.astype(BF16)
            for c in range(2):
                @pl.when(core == c)
                def _():
                    wo_head_ref[...] = wo_ref[m * 128 + c * HEAD : m * 128 + (c + 1) * HEAD, :]

    low_row = lax.broadcasted_iota(jnp.int32, (512, E_ROWS * 128), 0)
    high_row = lax.broadcasted_iota(jnp.int32, (1024, E_ROWS * 128), 0)
    for step in range(EDGES // (E_ROWS * 128)):
        rows = [step * E_ROWS + k for k in range(E_ROWS)]
        src = jnp.concatenate([src_ref[k : k + 1, :] for k in rows], axis=1)
        dst = jnp.concatenate([dst_ref[k : k + 1, :] for k in rows], axis=1)
        low = jnp.where(low_row == (src & 511), 1.0, 0.0).astype(BF16)
        high = jnp.where(high_row == ((src >> 9) * 256 + dst), 1.0, 0.0).astype(BF16)
        part = dot(low, high, NT)
        if step == 0:
            acc_ref[...] = part
        else:
            acc_ref[...] += part
    counts = acc_ref[...]
    per_row = jnp.sum(counts, axis=0, keepdims=True)
    per_row = per_row[:, 0:256] + per_row[:, 256:512] + per_row[:, 512:768] + per_row[:, 768:1024]
    degree = jnp.transpose(jnp.broadcast_to(jnp.maximum(per_row, 1.0), (128, ROWS)))
    degree_ref[...] = degree
    counts_t_ref[...] = jnp.transpose(counts).astype(BF16)
    counts = counts.astype(BF16)
    inverse = 1.0 / degree[:, 0:1]
    message = (dot(grad_ref[...], w_ref[...], NT) * inverse).astype(BF16)
    for high in range(4):
        part = dot(counts[:, high * 256 : (high + 1) * 256], message).astype(BF16)
        for k in range(4):
            slots_ref[high * 4 + k] = part[k * CAP : (k + 1) * CAP, :]


def mean_body(counts_t_ref, degree_ref, table_ref, x_ref, grad_ref, w_ref, base_ref, mine_ref, other_ref):
    total = jnp.zeros((ROWS, D), F32)
    for high in range(4):
        table = jnp.concatenate([table_ref[high * 4 + k] for k in range(4)], axis=0)
        total = total + dot(counts_t_ref[high * 256 : (high + 1) * 256, :], table)
    mean_rows = (total / degree_ref[:, 0:1]).astype(BF16)
    base_ref[...] = x_ref[...].astype(F32) + dot(mean_rows, w_ref[...])
    dw = dot(jnp.transpose(mean_rows.astype(F32)).astype(BF16), grad_ref[...]).astype(BF16)
    z, core = position()
    for half in range(2):
        def fill(ref):
            for p in range(DOM):
                top = half * 256 + p * 16
                for b in range(4):
                    ref[p, b * 16 : (b + 1) * 16, :] = dw[top : top + 16, b * 128 : (b + 1) * 128]

        @pl.when(core == half)
        def _():
            fill(mine_ref)

        @pl.when(core != half)
        def _():
            fill(other_ref)


def attention_body(
    p0_ref, p1_ref, t2_ref, b2_ref, p3_ref, p4_ref, p5_ref, t6_ref, b6_ref, p7_ref, wqkv_ref, wo_ref, mine_ref, other_ref,
    r0_ref, r1_ref, r2_ref, r3_ref, chunks_ref,
    y_ref, s_ref, qt_ref, kt_ref, k_ref, v_ref, vt_ref, w_ref, dq_ref, dk_ref, dv_ref, at_ref, ga_ref, sl_ref, qr_ref, gr_ref,
):
    pays = (p0_ref, p1_ref, (t2_ref, b2_ref), p3_ref, p4_ref, p5_ref, (t6_ref, b6_ref), p7_ref)

    def normed_of(pay):
        return pay[0][...] if isinstance(pay, tuple) else pay[0:ROWS, :]

    def grads_of(pay):
        return pay[1][0:ROWS, :] if isinstance(pay, tuple) else pay[ROWS : 2 * ROWS, :]

    def tail_of(pay):
        return pay[1][ROWS : PAY - ROWS, 0:ROWS] if isinstance(pay, tuple) else pay[2 * ROWS : PAY, 0:ROWS]

    outs = (r0_ref, r1_ref, r2_ref, r3_ref)
    z, core = position()
    row = lax.broadcasted_iota(jnp.int32, (HEAD, ROWS), 0)
    number = row.astype(F32)

    def head_scale(part):
        return lax.rsqrt(jnp.sum(part * part, axis=0, keepdims=True) * (1.0 / HEAD) + EPS)

    for r in range(BLK):
        pay = pays[r]
        projected = dot(wqkv_ref[...], normed_of(pay), NT)
        query, key, value = projected[0:HEAD], projected[HEAD:128], projected[128:192]
        scale_q, scale_k = head_scale(query), head_scale(key)
        query, key = query * scale_q, key * scale_k
        y_ref[r, 0:HEAD] = query
        y_ref[r, HEAD:128] = key
        s_ref[r, 0:1] = scale_q
        s_ref[r, 1:2] = scale_k
        tail = tail_of(pay).astype(F32)
        same = jnp.where(number == tail[0:1], 32.0, 0.0)
        sender = ((z - (r & 3)) & 3) * 2 + (core ^ (r >> 2))
        wanted = jnp.concatenate([jnp.zeros((16, ROWS), F32), tail[1:9] * 32.0, jnp.zeros((40, ROWS), F32)], axis=0)
        owner = jnp.where(row == 16 + sender, 32.0, 0.0)
        qt_ref[r] = jnp.concatenate([query, same + wanted], axis=0).astype(BF16)
        key = jnp.concatenate([key, same + owner], axis=0)
        kt_ref[r] = key[0:HEAD].astype(BF16)
        k_ref[r] = jnp.transpose(key).astype(BF16)
        value = jnp.concatenate([value, jnp.where(row < 2, 1.0, 0.0)], axis=0)
        vt_ref[r] = value[0:80].astype(BF16)
        v_ref[r] = jnp.transpose(value).astype(BF16)
        ga_ref[r] = dot(wo_ref[...], grads_of(pay), NT)
        qr_ref[r] = jnp.transpose(qt_ref[r].astype(F32)).astype(BF16)

    keys_t = jnp.concatenate([kt_ref[j] for j in range(BLK)], axis=1)
    values_t = jnp.concatenate([vt_ref[j] for j in range(BLK)], axis=1)

    def query_block(i, carry):
        query = qt_ref[i]
        for j in range(BLK):
            scores = dot(k_ref[j], query)
            w_ref[i, j] = jnp.exp2(scores * SCORE_MUL - SCORE_SUB).astype(BF16)
        numer = dot(values_t, w_ref[i].reshape(BLK * ROWS, ROWS))
        inverse = 1.0 / numer[HEAD : HEAD + 1]
        attn = (numer[0:HEAD] * inverse).astype(BF16)
        at_ref[i] = attn
        grad_attn = ga_ref[i]
        minus = jnp.sum(grad_attn * attn.astype(F32), axis=0, keepdims=True) * (-inverse)
        coarse = minus.astype(BF16).astype(F32)
        extra = jnp.where(row == 0, coarse, jnp.where(row == 1, minus - coarse, 0.0))
        grad = jnp.concatenate([grad_attn * inverse, extra], axis=0).astype(BF16)
        gr_ref[i] = jnp.transpose(grad.astype(F32)).astype(BF16)
        for j in range(BLK):
            sl_ref[i, j] = (w_ref[i, j].astype(F32) * dot(v_ref[j], grad)).astype(BF16)
        dq_ref[i] = dot(keys_t, sl_ref[i].reshape(BLK * ROWS, ROWS))
        return carry

    lax.fori_loop(0, BLK, query_block, 0)

    queries = jnp.concatenate([qr_ref[i] for i in range(BLK)], axis=0)
    grads = jnp.concatenate([gr_ref[i] for i in range(BLK)], axis=0)

    def key_block(j, carry):
        slopes = jnp.concatenate([sl_ref[i, j] for i in range(BLK)], axis=1)
        dk_ref[j] = jnp.transpose(dot(slopes, queries))[0:HEAD]
        weights = jnp.concatenate([w_ref[i, j] for i in range(BLK)], axis=1)
        dv_ref[j] = jnp.transpose(dot(weights, grads))[0:HEAD]
        return carry

    lax.fori_loop(0, BLK, key_block, 0)

    dw = jnp.zeros((192, D), F32)
    dwo = jnp.zeros((HEAD, D), F32)
    for r in range(BLK):
        pay = pays[r]

        def pull(grad, y, scale):
            grad = grad * (8.0 / HEAD)
            return scale * (grad - y * (jnp.sum(y * grad, axis=0, keepdims=True) * (1.0 / HEAD)))

        dquery = pull(dq_ref[r], y_ref[r, 0:HEAD], s_ref[r, 0:1])
        dkey = pull(dk_ref[r], y_ref[r, HEAD:128], s_ref[r, 1:2])
        first = jnp.concatenate([dquery, dkey], axis=0)
        second = jnp.concatenate([dv_ref[r], at_ref[r].astype(F32)], axis=0)
        outs[r & 3][r >> 2, :, 0:128] = jnp.transpose(first).astype(BF16)
        outs[r & 3][r >> 2, :, 128:256] = jnp.transpose(second).astype(BF16)
        left = jnp.concatenate([first, second[0:HEAD]], axis=0).astype(BF16)
        dw = dw + dot(left, normed_of(pay))
        dwo = dwo + dot(at_ref[r], grads_of(pay))
    dw = jnp.concatenate([dw, dwo], axis=0).astype(BF16)
    for a in range(4):
        for b in range(4):
            p = a * 4 + b
            chunks_ref[p, 0:64, :] = dw[a * 64 : (a + 1) * 64, b * 128 : (b + 1) * 128]
            chunks_ref[p, 64:128, :] = (mine_ref[p].astype(F32) + other_ref[p].astype(F32)).astype(BF16)


def chunk_sum_body(in_ref, g0_ref, g1_ref, wqkv_ref, out_ref, extra_ref):
    total = in_ref[0].astype(F32)
    for p in range(1, DOM):
        total = total + in_ref[p].astype(F32)
    out_ref[0:128, :] = total.astype(BF16)
    z, core = position()
    kind, lanes = dom_position()
    one, two = g0_ref[...], g1_ref[...]
    extra_ref[...] = jnp.where(core == 0, one, two) + jnp.where(core == 0, two, one)
    for b in range(4):
        @pl.when((kind < 3) & (lanes == b))
        def _():
            start = pl.multiple_of(jnp.minimum(kind, 2) * HEAD, HEAD)
            weights = wqkv_ref[pl.ds(start, HEAD), b * 128 : (b + 1) * 128].astype(F32)
            extra_ref[4:5, :] = jnp.sum(weights * total[0:HEAD], axis=0, keepdims=True)
    extra = extra_ref[...]
    coarse = extra.astype(BF16).astype(F32)
    out_ref[128:CHUNK, :] = jnp.concatenate([coarse, extra - coarse], axis=0).astype(BF16)


def spread_body(c0_ref, c1_ref, c2_ref, c3_ref, out_ref, parts_ref):
    z, core = position()
    for dz, c_ref in enumerate((c0_ref, c1_ref, c2_ref, c3_ref)):
        parts_ref[dz] = c_ref[64:CHUNK, :].astype(F32)
    total = jnp.zeros((80, 128), F32)
    for chip in range(4):
        total = total + parts_ref[(z - chip) & 3]
    gain = total[64:72] + total[72:80]
    coarse = gain.astype(BF16).astype(F32)
    tail = jnp.concatenate([total[0:64], coarse, gain - coarse], axis=0).astype(BF16)
    whole = jnp.concatenate([c_ref[0:64, :] for c_ref in (c0_ref, c1_ref, c2_ref, c3_ref)] + [tail], axis=0)
    for p in range(DOM):
        out_ref[p] = whole


def halo_body(counts_ref, back_ref, rows_ref, x_ref, out_ref, gain_grad_ref):
    row = lax.broadcasted_iota(jnp.int32, (ROWS, CAP), 0)
    slot = lax.broadcasted_iota(jnp.int32, (ROWS, CAP), 1)
    total = jnp.zeros((ROWS, D), F32)
    for k in range(4):
        hits = []
        for p in range(4 * k, 4 * k + 4):
            hit = (row == rows_ref[p : p + 1, :]) & (slot < counts_ref[p])
            hits.append(jnp.where(hit, 1.0, 0.0).astype(BF16))
        part = jnp.concatenate([back_ref[p] for p in range(4 * k, 4 * k + 4)], axis=0)
        total = total + dot(jnp.concatenate(hits, axis=1), part)
    out_ref[...] = total
    x = x_ref[...].astype(F32)
    scale = lax.rsqrt(jnp.mean(x * x, axis=-1, keepdims=True) + EPS)
    gain_grad = jnp.sum(total * (x * scale), axis=0, keepdims=True)
    gain_grad_ref[...] = jnp.zeros((8, 128), F32)
    for k in range(4):
        gain_grad_ref[k : k + 1, :] = gain_grad[:, k * 128 : (k + 1) * 128]


def rows_body(
    r0_ref, r1_ref, r2_ref, r3_ref, t0_ref, t1_ref, t2_ref, t3_ref, halo_ref, base_ref, x_ref,
    gain_ref, grad_ref, wq_ref, wk_ref, wv_ref, wo_ref,
    out_ref, feature_ref, dq_ref, dk_ref, dv_ref, at_ref,
):
    left = lax.broadcasted_iota(jnp.int32, (ROWS, 128), 1) < HEAD
    z, core = position()
    even = core == 0
    for dz, (r_ref, t_ref) in enumerate(zip((r0_ref, r1_ref, r2_ref, r3_ref), (t0_ref, t1_ref, t2_ref, t3_ref))):
        chip = (z + dz) & 3
        one, two = r_ref[0].astype(F32), t_ref[...].astype(F32)
        low, high = jnp.where(even, one, two), jnp.where(even, two, one)
        low0, low1 = low[:, 0:128], low[:, 128:256]
        high0, high1 = high[:, 0:128], high[:, 128:256]
        dq_ref[chip] = jnp.where(left, low0, pltpu.roll(high0, HEAD, 1)).astype(BF16)
        dk_ref[chip] = jnp.where(left, pltpu.roll(low0, HEAD, 1), high0).astype(BF16)
        dv_ref[chip] = jnp.where(left, low1, pltpu.roll(high1, HEAD, 1)).astype(BF16)
        at_ref[chip] = jnp.where(left, pltpu.roll(low1, HEAD, 1), high1).astype(BF16)

    def whole(ref):
        return jnp.concatenate([ref[m] for m in range(4)], axis=1)

    out_ref[...] = (base_ref[...] + dot(whole(at_ref), wo_ref[...])).astype(BF16)
    dnormed = dot(whole(dq_ref), wq_ref[...], NT) + dot(whole(dk_ref), wk_ref[...], NT)
    dnormed = dnormed + dot(whole(dv_ref), wv_ref[...], NT) + halo_ref[...]
    x = x_ref[...].astype(F32)
    scale = lax.rsqrt(jnp.mean(x * x, axis=-1, keepdims=True) + EPS)
    scaled = dnormed * gain_ref[...]
    inner = jnp.mean(scaled * x, axis=-1, keepdims=True)
    dx = scale * scaled - x * (scale * scale * scale * inner)
    feature_ref[...] = (grad_ref[...].astype(F32) + dx).astype(BF16)


def weights_body(mine_ref, other_ref, gain_in_ref, out_ref, gain_ref, all_ref):
    which = pl.program_id(0)

    @pl.when(which == 0)
    def _():
        z, core = position()
        all_ref[core] = mine_ref[...]
        all_ref[1 - core] = other_ref[...]
        gain = jnp.zeros((8, 128), F32)
        through = []
        for p in range(DOM):
            tails = [ref[p, 320:SPREAD, :].astype(F32) for ref in (mine_ref, other_ref)]
            tails = [tail[0:8] + tail[8:16] for tail in tails]
            gain = gain + tails[0]
            through.append(tails[0] + tails[1])
        for b in range(4):
            part = (through[b] + through[4 + b] + through[8 + b])[4:5]
            lanes = slice(b * 128, (b + 1) * 128)
            gain_ref[:, lanes] = gain[b : b + 1] + part / gain_in_ref[:, lanes]

    def piece(h, p):
        z, core = position()
        start = pl.multiple_of(((z - (h >> 1)) & 3) * 64, 64)
        return all_ref[h & 1, p, pl.ds(start, 64), :].astype(F32)

    @pl.when(which < 3)
    def _():
        for b in range(4):
            part = jnp.concatenate([piece(h, which * 4 + b) for h in range(BLK)], axis=0)
            out_ref[0, b * 128 : (b + 1) * 128, :] = jnp.transpose(part)

    @pl.when(which == 3)
    def _():
        for h in range(BLK):
            for b in range(4):
                out_ref[0, h * 64 : (h + 1) * 64, b * 128 : (b + 1) * 128] = piece(h, 12 + b)

    @pl.when(which == 4)
    def _():
        for half in range(2):
            for p in range(DOM):
                top = half * 256 + p * 16
                for b in range(4):
                    part = all_ref[half, p, 256 + b * 16 : 272 + b * 16, :]
                    out_ref[0, top : top + 16, b * 128 : (b + 1) * 128] = part.astype(F32)


def chip_shift(step, swap):
    return [(z * 2 + c, ((z + step) % 4) * 2 + (c ^ swap)) for z in range(4) for c in range(2)]


def along_chips(array, step):
    return lax.ppermute(array, "blk", chip_shift(step, 0))


def other_core(array):
    return lax.ppermute(array, "blk", chip_shift(0, 1))


def to_dom_peers(array):
    return lax.all_to_all(array, "dom", split_axis=0, concat_axis=0, tiled=True)


def local(
    x, gain, wq, wk, wv, wo, wm, cluster, pattern, send_rows, send_counts, edge_src, edge_dst, out_grad
):
    gain_row = gain.reshape(1, D)
    pay, outgoing = call(
        norm_body,
        (shape((PAY, D), BF16), shape((DOM, CAP, D), BF16)),
        (pattern, send_counts, x, gain_row, cluster.reshape(1, ROWS), out_grad, send_rows),
        scalars=2,
        micros=4,
    )
    incoming = to_dom_peers(outgoing)
    near, far = along_chips(pay, 1), along_chips(pay, 3)

    counts_t, degree, slot_grads, wqkv, wo_head = call(
        edges_body,
        (
            shape((1024, 512), BF16), shape((ROWS, 128), F32), shape((DOM, CAP, D), BF16),
            shape((192, D), BF16), shape((HEAD, D), BF16),
        ),
        (edge_src.reshape(32, 128), edge_dst.reshape(32, 128), out_grad, wm, wq, wk, wv, wo),
        scratch=[pltpu.VMEM((512, 1024), F32)],
        micros=10,
    )
    near, far, degree = lax.optimization_barrier((near, far, degree))
    pays = [pay, near, along_chips(near[0:ROWS], 1), along_chips(far[ROWS:PAY], 3), far]
    pays = pays + [other_core(part) for part in pays]
    incoming, slot_grads = lax.optimization_barrier((incoming, slot_grads))
    back = to_dom_peers(slot_grads)

    base, mine, other = call(
        mean_body,
        (shape((ROWS, D), F32), shape((DOM, 64, 128), BF16), shape((DOM, 64, 128), BF16)),
        (counts_t, degree, incoming, x, out_grad, wm),
        micros=4,
    )

    *results, chunks = call(
        attention_body,
        (*[shape((2, ROWS, 256), BF16)] * 4, shape((DOM, 128, 128), BF16)),
        (*pays, wqkv, wo_head, mine, other_core(other)),
        scratch=[
            pltpu.VMEM((BLK, 128, ROWS), F32),
            pltpu.VMEM((BLK, 8, ROWS), F32),
            pltpu.VMEM((BLK, 128, ROWS), BF16),
            pltpu.VMEM((BLK, HEAD, ROWS), BF16),
            pltpu.VMEM((BLK, ROWS, 128), BF16),
            pltpu.VMEM((BLK, ROWS, 128), BF16),
            pltpu.VMEM((BLK, 80, ROWS), BF16),
            pltpu.VMEM((BLK, BLK, ROWS, ROWS), BF16),
            pltpu.VMEM((BLK, HEAD, ROWS), F32),
            pltpu.VMEM((BLK, HEAD, ROWS), F32),
            pltpu.VMEM((BLK, HEAD, ROWS), F32),
            pltpu.VMEM((BLK, HEAD, ROWS), BF16),
            pltpu.VMEM((BLK, HEAD, ROWS), F32),
            pltpu.VMEM((BLK, BLK, ROWS, ROWS), BF16),
            pltpu.VMEM((BLK, ROWS, 128), BF16),
            pltpu.VMEM((BLK, ROWS, 128), BF16),
        ],
        micros=12,
    )
    chunks, back = lax.optimization_barrier((chunks, back))
    chunks = to_dom_peers(chunks)
    halo, gain_part = call(
        halo_body,
        (shape((ROWS, D), F32), shape((8, 128), F32)),
        (send_counts, back, send_rows, x),
        scalars=1,
        micros=3,
    )
    chunk = call(
        chunk_sum_body,
        shape((CHUNK, 128), BF16),
        (chunks, gain_part, other_core(gain_part), wqkv),
        scratch=[pltpu.VMEM((8, 128), F32)],
        micros=1,
    )
    chunk_parts = [chunk] + [along_chips(chunk, step) for step in (1, 2, 3)]
    spread = call(
        spread_body, shape((DOM, SPREAD, 128), BF16), chunk_parts, scratch=[pltpu.VMEM((4, 80, 128), F32)], micros=1
    )
    spread, *results = lax.optimization_barrier((spread, *results))
    gathered = to_dom_peers(spread)
    results = [results[0]] + [along_chips(results[dz], -dz) for dz in (1, 2, 3)]
    swapped = [other_core(part[1]) for part in results]
    layer_out, feature_grad = call(
        rows_body,
        (shape((ROWS, D), BF16), shape((ROWS, D), BF16)),
        (*results, *swapped, halo, base, x, gain_row, out_grad, wq, wk, wv, wo),
        scratch=[pltpu.VMEM((4, ROWS, 128), BF16)] * 4,
        micros=2,
    )
    gathered, layer_out, feature_grad = lax.optimization_barrier((gathered, layer_out, feature_grad))
    whole = pl.BlockSpec((DOM, SPREAD, 128), lambda t: (0, 0, 0))
    row = pl.BlockSpec((1, D), lambda t: (0, 0))
    weight_grads, gain_grad = pl.pallas_call(
        weights_body,
        grid=(5,),
        out_shape=(shape((5, D, D), F32), shape((1, D), F32)),
        in_specs=[whole, whole, row],
        out_specs=(pl.BlockSpec((1, D, D), lambda t: (t, 0, 0)), row),
        scratch_shapes=[pltpu.VMEM((2, DOM, SPREAD, 128), BF16)],
    )(gathered, other_core(gathered), gain_row)
    return layer_out, feature_grad, weight_grads, gain_grad.reshape(D)


def solution(mesh):
    both = ("dom", "blk")
    placed = (
        P(both, None), P(), P(), P(), P(), P(), P(), P(both), P(both, None), P(both, None), P(both), P(both), P(both),
        P(both, None),
    )
    return jax.shard_map(
        local,
        mesh=mesh,
        in_specs=placed,
        out_specs=(P(both, None), P(both, None), P(), P()),
        check_vma=False,
    )
```

```python
import math

import jax
import jax.numpy as jnp
from jax import lax
from jax.experimental import pallas as pl
from jax.experimental.pallas import tpu as pltpu
from jax.sharding import PartitionSpec as P

F32 = jnp.float32
BF16 = jnp.bfloat16
EPS = 1e-06
D = 512
ROWS = 256
HEAD = 64
BLK = 8
DOM = 16
CAP = 128
EDGES = 4096
PAY = 2 * ROWS + 16
LOG2E = math.log2(math.e)
SCORE_MUL = LOG2E / 8.0
SCORE_SUB = (8.0 + 256.0) * LOG2E
CHUNK = 64 + 64 + 16
SPREAD = 4 * 64 + 64 + 16

NT = (((1,), (1,)), ((), ()))
NN = (((1,), (0,)), ((), ()))


def dot(a, b, dims=NN):
    return lax.dot_general(a, b, dims, preferred_element_type=F32)


def call(body, out_shape, operands, scratch=(), scalars=0, micros=2):
    specs = [pl.BlockSpec(memory_space=pltpu.SMEM)] * scalars
    specs += [pl.BlockSpec(memory_space=pltpu.VMEM)] * (len(operands) - scalars)
    return pl.pallas_call(
        body,
        out_shape=out_shape,
        in_specs=specs,
        out_specs=jax.tree.map(lambda _: pl.BlockSpec(memory_space=pltpu.VMEM), out_shape),
        scratch_shapes=list(scratch),
        cost_estimate=pl.CostEstimate(flops=int(micros * 1e9), transcendentals=0, bytes_accessed=1 << 20),
    )(*operands)


def shape(dims, dtype):
    return jax.ShapeDtypeStruct(dims, dtype)


def dom_position():
    me = lax.axis_index("dom").astype(jnp.int32)
    return lax.shift_right_logical(me, 2), me & 3


def position():
    me = lax.axis_index("blk").astype(jnp.int32)
    return lax.shift_right_logical(me, 1), me & 1


def norm_body(pattern_ref, counts_ref, x_ref, gain_ref, label_ref, grad_ref, rows_ref, out_ref, slots_ref):
    x = x_ref[...].astype(F32)
    scale = lax.rsqrt(jnp.mean(x * x, axis=-1, keepdims=True) + EPS)
    normed = (x * scale * gain_ref[...]).astype(BF16)
    out_ref[0:ROWS, :] = normed
    out_ref[ROWS : 2 * ROWS, :] = grad_ref[...]
    row = lax.broadcasted_iota(jnp.int32, (16, ROWS), 0)
    lane = lax.broadcasted_iota(jnp.int32, (16, ROWS), 1)
    tail = jnp.where(row == 0, label_ref[...].astype(F32), 0.0)
    for b in range(BLK):
        flag = jnp.where(pattern_ref[0, b] == 1, 1.0, 0.0)
        tail = jnp.where((row == 1 + b) & (lane >= 0), flag, tail)
    out_ref[2 * ROWS : PAY, 0:ROWS] = tail.astype(BF16)
    out_ref[2 * ROWS : PAY, ROWS:D] = jnp.zeros((16, D - ROWS), BF16)
    columns = jnp.transpose(rows_ref[...].astype(F32))
    lane = lax.broadcasted_iota(jnp.int32, (CAP, ROWS), 1).astype(F32)
    slot = lax.broadcasted_iota(jnp.int32, (CAP, ROWS), 0)
    for p in range(DOM):
        hit = (lane == columns[:, p : p + 1]) & (slot < counts_ref[p])
        slots_ref[p] = dot(jnp.where(hit, 1.0, 0.0).astype(BF16), normed).astype(BF16)


E_ROWS = 4


def edges_body(
    src_ref, dst_ref, grad_ref, w_ref, wq_ref, wk_ref, wv_ref, wo_ref,
    counts_t_ref, degree_ref, slots_ref, wqkv_ref, wo_head_ref, acc_ref,
):
    z, core = position()
    for m in range(4):
        @pl.when(z == m)
        def _():
            for k, ref in enumerate((wq_ref, wk_ref, wv_ref)):
                pair = jnp.transpose(ref[:, m * 128 : (m + 1) * 128].astype(F32))
                picked = jnp.where(core == 0, pair[0:HEAD], pair[HEAD:128])
                wqkv_ref[k * HEAD : (k + 1) * HEAD, :] = picked.astype(BF16)
            for c in range(2):
                @pl.when(core == c)
                def _():
                    wo_head_ref[...] = wo_ref[m * 128 + c * HEAD : m * 128 + (c + 1) * HEAD, :]

    low_row = lax.broadcasted_iota(jnp.int32, (512, E_ROWS * 128), 0)
    high_row = lax.broadcasted_iota(jnp.int32, (1024, E_ROWS * 128), 0)
    for step in range(EDGES // (E_ROWS * 128)):
        rows = [step * E_ROWS + k for k in range(E_ROWS)]
        src = jnp.concatenate([src_ref[k : k + 1, :] for k in rows], axis=1)
        dst = jnp.concatenate([dst_ref[k : k + 1, :] for k in rows], axis=1)
        low = jnp.where(low_row == (src & 511), 1.0, 0.0).astype(BF16)
        high = jnp.where(high_row == ((src >> 9) * 256 + dst), 1.0, 0.0).astype(BF16)
        part = dot(low, high, NT)
        if step == 0:
            acc_ref[...] = part
        else:
            acc_ref[...] += part
    counts = acc_ref[...]
    per_row = jnp.sum(counts, axis=0, keepdims=True)
    per_row = per_row[:, 0:256] + per_row[:, 256:512] + per_row[:, 512:768] + per_row[:, 768:1024]
    degree = jnp.transpose(jnp.broadcast_to(jnp.maximum(per_row, 1.0), (128, ROWS)))
    degree_ref[...] = degree
    counts_t_ref[...] = jnp.transpose(counts).astype(BF16)
    counts = counts.astype(BF16)
    inverse = 1.0 / degree[:, 0:1]
    message = (dot(grad_ref[...], w_ref[...], NT) * inverse).astype(BF16)
    for high in range(4):
        part = dot(counts[:, high * 256 : (high + 1) * 256], message).astype(BF16)
        for k in range(4):
            slots_ref[high * 4 + k] = part[k * CAP : (k + 1) * CAP, :]


def mean_body(counts_t_ref, degree_ref, table_ref, x_ref, grad_ref, w_ref, base_ref, mine_ref, other_ref):
    total = jnp.zeros((ROWS, D), F32)
    for high in range(4):
        table = jnp.concatenate([table_ref[high * 4 + k] for k in range(4)], axis=0)
        total = total + dot(counts_t_ref[high * 256 : (high + 1) * 256, :], table)
    mean_rows = (total / degree_ref[:, 0:1]).astype(BF16)
    base_ref[...] = x_ref[...].astype(F32) + dot(mean_rows, w_ref[...])
    dw = dot(jnp.transpose(mean_rows.astype(F32)).astype(BF16), grad_ref[...]).astype(BF16)
    z, core = position()
    for half in range(2):
        def fill(ref):
            for p in range(DOM):
                top = half * 256 + p * 16
                for b in range(4):
                    ref[p, b * 16 : (b + 1) * 16, :] = dw[top : top + 16, b * 128 : (b + 1) * 128]

        @pl.when(core == half)
        def _():
            fill(mine_ref)

        @pl.when(core != half)
        def _():
            fill(other_ref)


def unpack(refs):
    p0, p1, t2, b2, p3, p4, p5, t6, b6, p7 = refs

    def split(pay):
        return pay.at[0:ROWS], pay.at[ROWS : 2 * ROWS], pay.at[2 * ROWS : PAY]

    def joined(top, bottom):
        return top, bottom.at[0:ROWS], bottom.at[ROWS : PAY - ROWS]

    return [split(p0), split(p1), joined(t2, b2), split(p3), split(p4), split(p5), joined(t6, b6), split(p7)]


def projections_body(*refs):
    blocks = unpack(refs[0:10])
    wqkv_ref, wo_ref, y_ref, s_ref, qt_ref, kt_ref, k_ref, v_ref, vt_ref, ga_ref, qr_ref = refs[10:]
    z, core = position()
    row = lax.broadcasted_iota(jnp.int32, (HEAD, ROWS), 0)
    number = row.astype(F32)

    def head_scale(part):
        return lax.rsqrt(jnp.sum(part * part, axis=0, keepdims=True) * (1.0 / HEAD) + EPS)

    for r in range(BLK):
        normed_ref, grads_ref, tail_ref = blocks[r]
        projected = dot(wqkv_ref[...], normed_ref[...], NT)
        query, key, value = projected[0:HEAD], projected[HEAD:128], projected[128:192]
        scale_q, scale_k = head_scale(query), head_scale(key)
        query, key = query * scale_q, key * scale_k
        y_ref[r, 0:HEAD] = query
        y_ref[r, HEAD:128] = key
        s_ref[r, 0:1] = scale_q
        s_ref[r, 1:2] = scale_k
        tail = tail_ref[:, 0:ROWS].astype(F32)
        same = jnp.where(number == tail[0:1], 32.0, 0.0)
        sender = ((z - (r & 3)) & 3) * 2 + (core ^ (r >> 2))
        wanted = jnp.concatenate([jnp.zeros((16, ROWS), F32), tail[1:9] * 32.0, jnp.zeros((40, ROWS), F32)], axis=0)
        owner = jnp.where(row == 16 + sender, 32.0, 0.0)
        qt_ref[r] = jnp.concatenate([query, same + wanted], axis=0).astype(BF16)
        key = jnp.concatenate([key, same + owner], axis=0)
        kt_ref[r] = key[0:HEAD].astype(BF16)
        k_ref[r] = jnp.transpose(key).astype(BF16)
        value = jnp.concatenate([value, jnp.where(row < 2, 1.0, 0.0)], axis=0)
        vt_ref[r] = value[0:80].astype(BF16)
        v_ref[r] = jnp.transpose(value).astype(BF16)
        ga_ref[r] = dot(wo_ref[...], grads_ref[...], NT)
        qr_ref[r] = jnp.transpose(qt_ref[r].astype(F32)).astype(BF16)


def attention_body(*refs):
    blocks = unpack(refs[0:10])
    mine_ref, other_ref, y_ref, s_ref, qt_ref, kt_ref, k_ref, v_ref, vt_ref, ga_ref, qr_ref = refs[10:21]
    *outs, chunks_ref = refs[21:26]
    w_ref, dq_ref, dk_ref, dv_ref, at_ref, sl_ref, gr_ref = refs[26:]
    row = lax.broadcasted_iota(jnp.int32, (HEAD, ROWS), 0)
    keys_t = jnp.concatenate([kt_ref[j] for j in range(BLK)], axis=1)
    values_t = jnp.concatenate([vt_ref[j] for j in range(BLK)], axis=1)

    def query_block(i, carry):
        query = qt_ref[i]
        for j in range(BLK):
            scores = dot(k_ref[j], query)
            w_ref[i, j] = jnp.exp2(scores * SCORE_MUL - SCORE_SUB).astype(BF16)
        numer = dot(values_t, w_ref[i].reshape(BLK * ROWS, ROWS))
        inverse = 1.0 / numer[HEAD : HEAD + 1]
        attn = (numer[0:HEAD] * inverse).astype(BF16)
        at_ref[i] = attn
        grad_attn = ga_ref[i]
        minus = jnp.sum(grad_attn * attn.astype(F32), axis=0, keepdims=True) * (-inverse)
        coarse = minus.astype(BF16).astype(F32)
        extra = jnp.where(row == 0, coarse, jnp.where(row == 1, minus - coarse, 0.0))
        grad = jnp.concatenate([grad_attn * inverse, extra], axis=0).astype(BF16)
        gr_ref[i] = jnp.transpose(grad.astype(F32)).astype(BF16)
        for j in range(BLK):
            sl_ref[i, j] = (w_ref[i, j].astype(F32) * dot(v_ref[j], grad)).astype(BF16)
        dq_ref[i] = dot(keys_t, sl_ref[i].reshape(BLK * ROWS, ROWS))
        return carry

    lax.fori_loop(0, BLK, query_block, 0)

    queries = jnp.concatenate([qr_ref[i] for i in range(BLK)], axis=0)
    grads = jnp.concatenate([gr_ref[i] for i in range(BLK)], axis=0)

    def key_block(j, carry):
        slopes = jnp.concatenate([sl_ref[i, j] for i in range(BLK)], axis=1)
        dk_ref[j] = jnp.transpose(dot(slopes, queries))[0:HEAD]
        weights = jnp.concatenate([w_ref[i, j] for i in range(BLK)], axis=1)
        dv_ref[j] = jnp.transpose(dot(weights, grads))[0:HEAD]
        return carry

    lax.fori_loop(0, BLK, key_block, 0)

    dw = jnp.zeros((192, D), F32)
    dwo = jnp.zeros((HEAD, D), F32)
    for r in range(BLK):
        normed_ref, grads_ref, tail_ref = blocks[r]

        def pull(grad, y, scale):
            grad = grad * (8.0 / HEAD)
            return scale * (grad - y * (jnp.sum(y * grad, axis=0, keepdims=True) * (1.0 / HEAD)))

        dquery = pull(dq_ref[r], y_ref[r, 0:HEAD], s_ref[r, 0:1])
        dkey = pull(dk_ref[r], y_ref[r, HEAD:128], s_ref[r, 1:2])
        first = jnp.concatenate([dquery, dkey], axis=0)
        second = jnp.concatenate([dv_ref[r], at_ref[r].astype(F32)], axis=0)
        outs[r & 3][r >> 2, :, 0:128] = jnp.transpose(first).astype(BF16)
        outs[r & 3][r >> 2, :, 128:256] = jnp.transpose(second).astype(BF16)
        left = jnp.concatenate([first, second[0:HEAD]], axis=0).astype(BF16)
        dw = dw + dot(left, normed_ref[...])
        dwo = dwo + dot(at_ref[r], grads_ref[...])
    dw = jnp.concatenate([dw, dwo], axis=0).astype(BF16)
    for a in range(4):
        for b in range(4):
            p = a * 4 + b
            chunks_ref[p, 0:64, :] = dw[a * 64 : (a + 1) * 64, b * 128 : (b + 1) * 128]
            chunks_ref[p, 64:128, :] = (mine_ref[p].astype(F32) + other_ref[p].astype(F32)).astype(BF16)


def chunk_sum_body(in_ref, g0_ref, g1_ref, wqkv_ref, out_ref, extra_ref):
    total = in_ref[0].astype(F32)
    for p in range(1, DOM):
        total = total + in_ref[p].astype(F32)
    out_ref[0:128, :] = total.astype(BF16)
    z, core = position()
    kind, lanes = dom_position()
    one, two = g0_ref[...], g1_ref[...]
    extra_ref[...] = jnp.where(core == 0, one, two) + jnp.where(core == 0, two, one)
    for b in range(4):
        @pl.when((kind < 3) & (lanes == b))
        def _():
            start = pl.multiple_of(jnp.minimum(kind, 2) * HEAD, HEAD)
            weights = wqkv_ref[pl.ds(start, HEAD), b * 128 : (b + 1) * 128].astype(F32)
            extra_ref[4:5, :] = jnp.sum(weights * total[0:HEAD], axis=0, keepdims=True)
    extra = extra_ref[...]
    coarse = extra.astype(BF16).astype(F32)
    out_ref[128:CHUNK, :] = jnp.concatenate([coarse, extra - coarse], axis=0).astype(BF16)


def spread_body(c0_ref, c1_ref, c2_ref, c3_ref, out_ref, parts_ref):
    z, core = position()
    for dz, c_ref in enumerate((c0_ref, c1_ref, c2_ref, c3_ref)):
        parts_ref[dz] = c_ref[64:CHUNK, :].astype(F32)
    total = jnp.zeros((80, 128), F32)
    for chip in range(4):
        total = total + parts_ref[(z - chip) & 3]
    gain = total[64:72] + total[72:80]
    coarse = gain.astype(BF16).astype(F32)
    tail = jnp.concatenate([total[0:64], coarse, gain - coarse], axis=0).astype(BF16)
    whole = jnp.concatenate([c_ref[0:64, :] for c_ref in (c0_ref, c1_ref, c2_ref, c3_ref)] + [tail], axis=0)
    for p in range(DOM):
        out_ref[p] = whole


def halo_body(counts_ref, back_ref, rows_ref, x_ref, out_ref, gain_grad_ref):
    row = lax.broadcasted_iota(jnp.int32, (ROWS, CAP), 0)
    slot = lax.broadcasted_iota(jnp.int32, (ROWS, CAP), 1)
    total = jnp.zeros((ROWS, D), F32)
    for k in range(4):
        hits = []
        for p in range(4 * k, 4 * k + 4):
            hit = (row == rows_ref[p : p + 1, :]) & (slot < counts_ref[p])
            hits.append(jnp.where(hit, 1.0, 0.0).astype(BF16))
        part = jnp.concatenate([back_ref[p] for p in range(4 * k, 4 * k + 4)], axis=0)
        total = total + dot(jnp.concatenate(hits, axis=1), part)
    out_ref[...] = total
    x = x_ref[...].astype(F32)
    scale = lax.rsqrt(jnp.mean(x * x, axis=-1, keepdims=True) + EPS)
    gain_grad = jnp.sum(total * (x * scale), axis=0, keepdims=True)
    gain_grad_ref[...] = jnp.zeros((8, 128), F32)
    for k in range(4):
        gain_grad_ref[k : k + 1, :] = gain_grad[:, k * 128 : (k + 1) * 128]


def rows_body(
    r0_ref, r1_ref, r2_ref, r3_ref, t0_ref, t1_ref, t2_ref, t3_ref, halo_ref, base_ref, x_ref,
    gain_ref, grad_ref, wq_ref, wk_ref, wv_ref, wo_ref,
    out_ref, feature_ref, dq_ref, dk_ref, dv_ref, at_ref,
):
    left = lax.broadcasted_iota(jnp.int32, (ROWS, 128), 1) < HEAD
    z, core = position()
    even = core == 0
    for dz, (r_ref, t_ref) in enumerate(zip((r0_ref, r1_ref, r2_ref, r3_ref), (t0_ref, t1_ref, t2_ref, t3_ref))):
        chip = (z + dz) & 3
        one, two = r_ref[0].astype(F32), t_ref[...].astype(F32)
        low, high = jnp.where(even, one, two), jnp.where(even, two, one)
        low0, low1 = low[:, 0:128], low[:, 128:256]
        high0, high1 = high[:, 0:128], high[:, 128:256]
        dq_ref[chip] = jnp.where(left, low0, pltpu.roll(high0, HEAD, 1)).astype(BF16)
        dk_ref[chip] = jnp.where(left, pltpu.roll(low0, HEAD, 1), high0).astype(BF16)
        dv_ref[chip] = jnp.where(left, low1, pltpu.roll(high1, HEAD, 1)).astype(BF16)
        at_ref[chip] = jnp.where(left, pltpu.roll(low1, HEAD, 1), high1).astype(BF16)

    def whole(ref):
        return jnp.concatenate([ref[m] for m in range(4)], axis=1)

    out_ref[...] = (base_ref[...] + dot(whole(at_ref), wo_ref[...])).astype(BF16)
    dnormed = dot(whole(dq_ref), wq_ref[...], NT) + dot(whole(dk_ref), wk_ref[...], NT)
    dnormed = dnormed + dot(whole(dv_ref), wv_ref[...], NT) + halo_ref[...]
    x = x_ref[...].astype(F32)
    scale = lax.rsqrt(jnp.mean(x * x, axis=-1, keepdims=True) + EPS)
    scaled = dnormed * gain_ref[...]
    inner = jnp.mean(scaled * x, axis=-1, keepdims=True)
    dx = scale * scaled - x * (scale * scale * scale * inner)
    feature_ref[...] = (grad_ref[...].astype(F32) + dx).astype(BF16)


def weights_body(mine_ref, other_ref, gain_in_ref, out_ref, gain_ref, all_ref):
    which = pl.program_id(0)

    @pl.when(which == 0)
    def _():
        z, core = position()
        all_ref[core] = mine_ref[...]
        all_ref[1 - core] = other_ref[...]
        gain = jnp.zeros((8, 128), F32)
        through = []
        for p in range(DOM):
            tails = [ref[p, 320:SPREAD, :].astype(F32) for ref in (mine_ref, other_ref)]
            tails = [tail[0:8] + tail[8:16] for tail in tails]
            gain = gain + tails[0]
            through.append(tails[0] + tails[1])
        for b in range(4):
            part = (through[b] + through[4 + b] + through[8 + b])[4:5]
            lanes = slice(b * 128, (b + 1) * 128)
            gain_ref[:, lanes] = gain[b : b + 1] + part / gain_in_ref[:, lanes]

    def piece(h, p):
        z, core = position()
        start = pl.multiple_of(((z - (h >> 1)) & 3) * 64, 64)
        return all_ref[h & 1, p, pl.ds(start, 64), :].astype(F32)

    @pl.when(which < 3)
    def _():
        for b in range(4):
            part = jnp.concatenate([piece(h, which * 4 + b) for h in range(BLK)], axis=0)
            out_ref[0, b * 128 : (b + 1) * 128, :] = jnp.transpose(part)

    @pl.when(which == 3)
    def _():
        for h in range(BLK):
            for b in range(4):
                out_ref[0, h * 64 : (h + 1) * 64, b * 128 : (b + 1) * 128] = piece(h, 12 + b)

    @pl.when(which == 4)
    def _():
        for half in range(2):
            for p in range(DOM):
                top = half * 256 + p * 16
                for b in range(4):
                    part = all_ref[half, p, 256 + b * 16 : 272 + b * 16, :]
                    out_ref[0, top : top + 16, b * 128 : (b + 1) * 128] = part.astype(F32)


def chip_shift(step, swap):
    return [(z * 2 + c, ((z + step) % 4) * 2 + (c ^ swap)) for z in range(4) for c in range(2)]


def along_chips(array, step):
    return lax.ppermute(array, "blk", chip_shift(step, 0))


def other_core(array):
    return lax.ppermute(array, "blk", chip_shift(0, 1))


def to_dom_peers(array):
    return lax.all_to_all(array, "dom", split_axis=0, concat_axis=0, tiled=True)


def local(
    x, gain, wq, wk, wv, wo, wm, cluster, pattern, send_rows, send_counts, edge_src, edge_dst, out_grad
):
    gain_row = gain.reshape(1, D)
    pay, outgoing = call(
        norm_body,
        (shape((PAY, D), BF16), shape((DOM, CAP, D), BF16)),
        (pattern, send_counts, x, gain_row, cluster.reshape(1, ROWS), out_grad, send_rows),
        scalars=2,
        micros=4,
    )
    incoming = to_dom_peers(outgoing)
    near, far = along_chips(pay, 1), along_chips(pay, 3)

    counts_t, degree, slot_grads, wqkv, wo_head = call(
        edges_body,
        (
            shape((1024, 512), BF16), shape((ROWS, 128), F32), shape((DOM, CAP, D), BF16),
            shape((192, D), BF16), shape((HEAD, D), BF16),
        ),
        (edge_src.reshape(32, 128), edge_dst.reshape(32, 128), out_grad, wm, wq, wk, wv, wo),
        scratch=[pltpu.VMEM((512, 1024), F32)],
        micros=10,
    )
    near, far, degree = lax.optimization_barrier((near, far, degree))
    pays = [pay, near, along_chips(near[0:ROWS], 1), along_chips(far[ROWS:PAY], 3), far]
    pays = pays + [other_core(part) for part in pays]
    projections = call(
        projections_body,
        (
            shape((BLK, 128, ROWS), F32), shape((BLK, 8, ROWS), F32), shape((BLK, 128, ROWS), BF16),
            shape((BLK, HEAD, ROWS), BF16), shape((BLK, ROWS, 128), BF16), shape((BLK, ROWS, 128), BF16),
            shape((BLK, 80, ROWS), BF16), shape((BLK, HEAD, ROWS), F32), shape((BLK, ROWS, 128), BF16),
        ),
        (*pays, wqkv, wo_head),
        micros=3,
    )
    incoming, slot_grads, *projections = lax.optimization_barrier((incoming, slot_grads, *projections))
    back = to_dom_peers(slot_grads)

    base, mine, other = call(
        mean_body,
        (shape((ROWS, D), F32), shape((DOM, 64, 128), BF16), shape((DOM, 64, 128), BF16)),
        (counts_t, degree, incoming, x, out_grad, wm),
        micros=4,
    )

    *results, chunks = call(
        attention_body,
        (*[shape((2, ROWS, 256), BF16)] * 4, shape((DOM, 128, 128), BF16)),
        (*pays, mine, other_core(other), *projections),
        scratch=[
            pltpu.VMEM((BLK, BLK, ROWS, ROWS), BF16),
            pltpu.VMEM((BLK, HEAD, ROWS), F32),
            pltpu.VMEM((BLK, HEAD, ROWS), F32),
            pltpu.VMEM((BLK, HEAD, ROWS), F32),
            pltpu.VMEM((BLK, HEAD, ROWS), BF16),
            pltpu.VMEM((BLK, BLK, ROWS, ROWS), BF16),
            pltpu.VMEM((BLK, ROWS, 128), BF16),
        ],
        micros=12,
    )
    chunks, back = lax.optimization_barrier((chunks, back))
    chunks = to_dom_peers(chunks)
    halo, gain_part = call(
        halo_body,
        (shape((ROWS, D), F32), shape((8, 128), F32)),
        (send_counts, back, send_rows, x),
        scalars=1,
        micros=3,
    )
    *results, gain_part = lax.optimization_barrier((*results, gain_part))
    results = [results[0]] + [along_chips(results[dz], -dz) for dz in (1, 2, 3)]
    chunk = call(
        chunk_sum_body,
        shape((CHUNK, 128), BF16),
        (chunks, gain_part, other_core(gain_part), wqkv),
        scratch=[pltpu.VMEM((8, 128), F32)],
        micros=1,
    )
    chunk_parts = [chunk] + [along_chips(chunk, step) for step in (1, 2, 3)]
    *chunk_parts, r1, r2, r3 = lax.optimization_barrier((*chunk_parts, *results[1:]))
    results = [results[0], r1, r2, r3]
    spread = call(
        spread_body, shape((DOM, SPREAD, 128), BF16), chunk_parts, scratch=[pltpu.VMEM((4, 80, 128), F32)], micros=1
    )
    spread, *results = lax.optimization_barrier((spread, *results))
    gathered = to_dom_peers(spread)
    swapped = [other_core(part[1]) for part in results]
    layer_out, feature_grad = call(
        rows_body,
        (shape((ROWS, D), BF16), shape((ROWS, D), BF16)),
        (*results, *swapped, halo, base, x, gain_row, out_grad, wq, wk, wv, wo),
        scratch=[pltpu.VMEM((4, ROWS, 128), BF16)] * 4,
        micros=2,
    )
    gathered, layer_out, feature_grad = lax.optimization_barrier((gathered, layer_out, feature_grad))
    whole = pl.BlockSpec((DOM, SPREAD, 128), lambda t: (0, 0, 0))
    row = pl.BlockSpec((1, D), lambda t: (0, 0))
    weight_grads, gain_grad = pl.pallas_call(
        weights_body,
        grid=(5,),
        out_shape=(shape((5, D, D), F32), shape((1, D), F32)),
        in_specs=[whole, whole, row],
        out_specs=(pl.BlockSpec((1, D, D), lambda t: (t, 0, 0)), row),
        scratch_shapes=[pltpu.VMEM((2, DOM, SPREAD, 128), BF16)],
    )(gathered, other_core(gathered), gain_row)
    return layer_out, feature_grad, weight_grads, gain_grad.reshape(D)


def solution(mesh):
    both = ("dom", "blk")
    placed = (
        P(both, None), P(), P(), P(), P(), P(), P(), P(both), P(both, None), P(both, None), P(both), P(both), P(both),
        P(both, None),
    )
    return jax.shard_map(
        local,
        mesh=mesh,
        in_specs=placed,
        out_specs=(P(both, None), P(both, None), P(), P()),
        check_vma=False,
    )
```

```python
import math

import jax
import jax.numpy as jnp
from jax import lax
from jax.experimental import pallas as pl
from jax.experimental.pallas import tpu as pltpu
from jax.sharding import PartitionSpec as P

F32 = jnp.float32
BF16 = jnp.bfloat16
EPS = 1e-06
D = 512
ROWS = 256
HEAD = 64
BLK = 8
DOM = 16
CAP = 128
EDGES = 4096
PAY = 2 * ROWS + 16
LOG2E = math.log2(math.e)
SCORE_MUL = LOG2E / 8.0
SCORE_SUB = (8.0 + 256.0) * LOG2E
CHUNK = 64 + 64 + 16
SPREAD = 4 * 64 + 64 + 16

NT = (((1,), (1,)), ((), ()))
NN = (((1,), (0,)), ((), ()))


def dot(a, b, dims=NN):
    return lax.dot_general(a, b, dims, preferred_element_type=F32)


def call(body, out_shape, operands, scratch=(), scalars=0, micros=2, left=()):
    specs = [pl.BlockSpec(memory_space=pltpu.SMEM)] * scalars
    specs += [pl.BlockSpec(memory_space=pltpu.VMEM)] * (len(operands) - scalars)
    for at in left:
        specs[at] = pl.BlockSpec(memory_space=pltpu.HBM)
    return pl.pallas_call(
        body,
        out_shape=out_shape,
        in_specs=specs,
        out_specs=jax.tree.map(lambda _: pl.BlockSpec(memory_space=pltpu.VMEM), out_shape),
        scratch_shapes=list(scratch),
        cost_estimate=pl.CostEstimate(flops=int(micros * 1e9), transcendentals=0, bytes_accessed=1 << 20),
    )(*operands)


def shape(dims, dtype):
    return jax.ShapeDtypeStruct(dims, dtype)


def dom_position():
    me = lax.axis_index("dom").astype(jnp.int32)
    return lax.shift_right_logical(me, 2), me & 3


def position():
    me = lax.axis_index("blk").astype(jnp.int32)
    return lax.shift_right_logical(me, 1), me & 1


def norm_body(pattern_ref, counts_ref, x_ref, gain_ref, label_ref, grad_ref, rows_ref, out_ref, slots_ref):
    x = x_ref[...].astype(F32)
    scale = lax.rsqrt(jnp.mean(x * x, axis=-1, keepdims=True) + EPS)
    normed = (x * scale * gain_ref[...]).astype(BF16)
    out_ref[0:ROWS, :] = normed
    out_ref[ROWS : 2 * ROWS, :] = grad_ref[...]
    row = lax.broadcasted_iota(jnp.int32, (16, ROWS), 0)
    lane = lax.broadcasted_iota(jnp.int32, (16, ROWS), 1)
    tail = jnp.where(row == 0, label_ref[...].astype(F32), 0.0)
    for b in range(BLK):
        flag = jnp.where(pattern_ref[0, b] == 1, 1.0, 0.0)
        tail = jnp.where((row == 1 + b) & (lane >= 0), flag, tail)
    out_ref[2 * ROWS : PAY, 0:ROWS] = tail.astype(BF16)
    out_ref[2 * ROWS : PAY, ROWS:D] = jnp.zeros((16, D - ROWS), BF16)
    columns = jnp.transpose(rows_ref[...].astype(F32))
    lane = lax.broadcasted_iota(jnp.int32, (CAP, ROWS), 1).astype(F32)
    slot = lax.broadcasted_iota(jnp.int32, (CAP, ROWS), 0)
    for p in range(DOM):
        hit = (lane == columns[:, p : p + 1]) & (slot < counts_ref[p])
        slots_ref[p] = dot(jnp.where(hit, 1.0, 0.0).astype(BF16), normed).astype(BF16)


E_ROWS = 4


def edges_body(
    src_ref, dst_ref, grad_ref, w_ref, wq_ref, wk_ref, wv_ref, wo_ref,
    counts_t_ref, degree_ref, slots_ref, wqkv_ref, wo_head_ref, acc_ref,
):
    z, core = position()
    for m in range(4):
        @pl.when(z == m)
        def _():
            for k, ref in enumerate((wq_ref, wk_ref, wv_ref)):
                pair = jnp.transpose(ref[:, m * 128 : (m + 1) * 128].astype(F32))
                picked = jnp.where(core == 0, pair[0:HEAD], pair[HEAD:128])
                wqkv_ref[k * HEAD : (k + 1) * HEAD, :] = picked.astype(BF16)
            for c in range(2):
                @pl.when(core == c)
                def _():
                    wo_head_ref[...] = wo_ref[m * 128 + c * HEAD : m * 128 + (c + 1) * HEAD, :]

    low_row = lax.broadcasted_iota(jnp.int32, (512, E_ROWS * 128), 0)
    high_row = lax.broadcasted_iota(jnp.int32, (1024, E_ROWS * 128), 0)
    for step in range(EDGES // (E_ROWS * 128)):
        rows = [step * E_ROWS + k for k in range(E_ROWS)]
        src = jnp.concatenate([src_ref[k : k + 1, :] for k in rows], axis=1)
        dst = jnp.concatenate([dst_ref[k : k + 1, :] for k in rows], axis=1)
        low = jnp.where(low_row == (src & 511), 1.0, 0.0).astype(BF16)
        high = jnp.where(high_row == ((src >> 9) * 256 + dst), 1.0, 0.0).astype(BF16)
        part = dot(low, high, NT)
        if step == 0:
            acc_ref[...] = part
        else:
            acc_ref[...] += part
    counts = acc_ref[...]
    per_row = jnp.sum(counts, axis=0, keepdims=True)
    per_row = per_row[:, 0:256] + per_row[:, 256:512] + per_row[:, 512:768] + per_row[:, 768:1024]
    degree = jnp.transpose(jnp.broadcast_to(jnp.maximum(per_row, 1.0), (128, ROWS)))
    degree_ref[...] = degree
    counts_t_ref[...] = jnp.transpose(counts).astype(BF16)
    counts = counts.astype(BF16)
    inverse = 1.0 / degree[:, 0:1]
    message = (dot(grad_ref[...], w_ref[...], NT) * inverse).astype(BF16)
    for high in range(4):
        part = dot(counts[:, high * 256 : (high + 1) * 256], message).astype(BF16)
        for k in range(4):
            slots_ref[high * 4 + k] = part[k * CAP : (k + 1) * CAP, :]


def mean_body(counts_t_ref, degree_ref, table_ref, x_ref, grad_ref, w_ref, base_ref, mine_ref, other_ref):
    total = jnp.zeros((ROWS, D), F32)
    for high in range(4):
        table = jnp.concatenate([table_ref[high * 4 + k] for k in range(4)], axis=0)
        total = total + dot(counts_t_ref[high * 256 : (high + 1) * 256, :], table)
    mean_rows = (total / degree_ref[:, 0:1]).astype(BF16)
    base_ref[...] = x_ref[...].astype(F32) + dot(mean_rows, w_ref[...])
    dw = dot(jnp.transpose(mean_rows.astype(F32)).astype(BF16), grad_ref[...]).astype(BF16)
    z, core = position()
    for half in range(2):
        def fill(ref):
            for p in range(DOM):
                top = half * 256 + p * 16
                for b in range(4):
                    ref[p, b * 16 : (b + 1) * 16, :] = dw[top : top + 16, b * 128 : (b + 1) * 128]

        @pl.when(core == half)
        def _():
            fill(mine_ref)

        @pl.when(core != half)
        def _():
            fill(other_ref)


def attention_body(
    p0_ref, p1_ref, t2_ref, b2_ref, p3_ref, p4_ref, p5_ref, t6_ref, b6_ref, p7_ref, wqkv_ref, wo_ref, mine_ref, other_ref,
    r0_ref, r1_ref, r2_ref, r3_ref, chunks_ref,
    y_ref, s_ref, qt_ref, kt_ref, k_ref, v_ref, vt_ref, w_ref, dq_ref, dk_ref, dv_ref, at_ref, ga_ref, sl_ref, qr_ref, gr_ref,
):
    pays = (p0_ref, p1_ref, (t2_ref, b2_ref), p3_ref, p4_ref, p5_ref, (t6_ref, b6_ref), p7_ref)

    def normed_of(pay):
        return pay[0][...] if isinstance(pay, tuple) else pay[0:ROWS, :]

    def grads_of(pay):
        return pay[1][0:ROWS, :] if isinstance(pay, tuple) else pay[ROWS : 2 * ROWS, :]

    def tail_of(pay):
        return pay[1][ROWS : PAY - ROWS, 0:ROWS] if isinstance(pay, tuple) else pay[2 * ROWS : PAY, 0:ROWS]

    outs = (r0_ref, r1_ref, r2_ref, r3_ref)
    z, core = position()
    row = lax.broadcasted_iota(jnp.int32, (HEAD, ROWS), 0)
    number = row.astype(F32)

    def head_scale(part):
        return lax.rsqrt(jnp.sum(part * part, axis=0, keepdims=True) * (1.0 / HEAD) + EPS)

    for r in range(BLK):
        pay = pays[r]
        projected = dot(wqkv_ref[...], normed_of(pay), NT)
        query, key, value = projected[0:HEAD], projected[HEAD:128], projected[128:192]
        scale_q, scale_k = head_scale(query), head_scale(key)
        query, key = query * scale_q, key * scale_k
        y_ref[r, 0:HEAD] = query
        y_ref[r, HEAD:128] = key
        s_ref[r, 0:1] = scale_q
        s_ref[r, 1:2] = scale_k
        tail = tail_of(pay).astype(F32)
        same = jnp.where(number == tail[0:1], 32.0, 0.0)
        sender = ((z - (r & 3)) & 3) * 2 + (core ^ (r >> 2))
        wanted = jnp.concatenate([jnp.zeros((16, ROWS), F32), tail[1:9] * 32.0, jnp.zeros((40, ROWS), F32)], axis=0)
        owner = jnp.where(row == 16 + sender, 32.0, 0.0)
        qt_ref[r] = jnp.concatenate([query, same + wanted], axis=0).astype(BF16)
        key = jnp.concatenate([key, same + owner], axis=0)
        kt_ref[r] = key[0:HEAD].astype(BF16)
        k_ref[r] = jnp.transpose(key).astype(BF16)
        value = jnp.concatenate([value, jnp.where(row < 2, 1.0, 0.0)], axis=0)
        vt_ref[r] = value[0:80].astype(BF16)
        v_ref[r] = jnp.transpose(value).astype(BF16)
        ga_ref[r] = dot(wo_ref[...], grads_of(pay), NT)
        qr_ref[r] = jnp.transpose(qt_ref[r].astype(F32)).astype(BF16)

    keys_t = jnp.concatenate([kt_ref[j] for j in range(BLK)], axis=1)
    values_t = jnp.concatenate([vt_ref[j] for j in range(BLK)], axis=1)

    def query_block(i, carry):
        query = qt_ref[i]
        for j in range(BLK):
            scores = dot(k_ref[j], query)
            w_ref[i, j] = jnp.exp2(scores * SCORE_MUL - SCORE_SUB).astype(BF16)
        numer = dot(values_t, w_ref[i].reshape(BLK * ROWS, ROWS))
        inverse = 1.0 / numer[HEAD : HEAD + 1]
        attn = (numer[0:HEAD] * inverse).astype(BF16)
        at_ref[i] = attn
        grad_attn = ga_ref[i]
        minus = jnp.sum(grad_attn * attn.astype(F32), axis=0, keepdims=True) * (-inverse)
        coarse = minus.astype(BF16).astype(F32)
        extra = jnp.where(row == 0, coarse, jnp.where(row == 1, minus - coarse, 0.0))
        grad = jnp.concatenate([grad_attn * inverse, extra], axis=0).astype(BF16)
        gr_ref[i] = jnp.transpose(grad.astype(F32)).astype(BF16)
        for j in range(BLK):
            sl_ref[i, j] = (w_ref[i, j].astype(F32) * dot(v_ref[j], grad)).astype(BF16)
        dq_ref[i] = dot(keys_t, sl_ref[i].reshape(BLK * ROWS, ROWS))
        return carry

    lax.fori_loop(0, BLK, query_block, 0)

    queries = jnp.concatenate([qr_ref[i] for i in range(BLK)], axis=0)
    grads = jnp.concatenate([gr_ref[i] for i in range(BLK)], axis=0)

    def key_block(j, carry):
        slopes = jnp.concatenate([sl_ref[i, j] for i in range(BLK)], axis=1)
        dk_ref[j] = jnp.transpose(dot(slopes, queries))[0:HEAD]
        weights = jnp.concatenate([w_ref[i, j] for i in range(BLK)], axis=1)
        dv_ref[j] = jnp.transpose(dot(weights, grads))[0:HEAD]
        return carry

    lax.fori_loop(0, BLK, key_block, 0)

    dw = jnp.zeros((192, D), F32)
    dwo = jnp.zeros((HEAD, D), F32)
    for r in range(BLK):
        pay = pays[r]

        def pull(grad, y, scale):
            grad = grad * (8.0 / HEAD)
            return scale * (grad - y * (jnp.sum(y * grad, axis=0, keepdims=True) * (1.0 / HEAD)))

        dquery = pull(dq_ref[r], y_ref[r, 0:HEAD], s_ref[r, 0:1])
        dkey = pull(dk_ref[r], y_ref[r, HEAD:128], s_ref[r, 1:2])
        first = jnp.concatenate([dquery, dkey], axis=0)
        second = jnp.concatenate([dv_ref[r], at_ref[r].astype(F32)], axis=0)
        outs[r & 3][r >> 2, :, 0:128] = jnp.transpose(first).astype(BF16)
        outs[r & 3][r >> 2, :, 128:256] = jnp.transpose(second).astype(BF16)
        left = jnp.concatenate([first, second[0:HEAD]], axis=0).astype(BF16)
        dw = dw + dot(left, normed_of(pay))
        dwo = dwo + dot(at_ref[r], grads_of(pay))
    dw = jnp.concatenate([dw, dwo], axis=0).astype(BF16)
    for a in range(4):
        for b in range(4):
            p = a * 4 + b
            chunks_ref[p, 0:64, :] = dw[a * 64 : (a + 1) * 64, b * 128 : (b + 1) * 128]
            chunks_ref[p, 64:128, :] = (mine_ref[p].astype(F32) + other_ref[p].astype(F32)).astype(BF16)


def chunk_sum_body(in_ref, g0_ref, g1_ref, wqkv_ref, out_ref, extra_ref):
    total = in_ref[0].astype(F32)
    for p in range(1, DOM):
        total = total + in_ref[p].astype(F32)
    out_ref[0:128, :] = total.astype(BF16)
    z, core = position()
    kind, lanes = dom_position()
    one, two = g0_ref[...], g1_ref[...]
    extra_ref[...] = jnp.where(core == 0, one, two) + jnp.where(core == 0, two, one)
    for b in range(4):
        @pl.when((kind < 3) & (lanes == b))
        def _():
            start = pl.multiple_of(jnp.minimum(kind, 2) * HEAD, HEAD)
            weights = wqkv_ref[pl.ds(start, HEAD), b * 128 : (b + 1) * 128].astype(F32)
            extra_ref[4:5, :] = jnp.sum(weights * total[0:HEAD], axis=0, keepdims=True)
    extra = extra_ref[...]
    coarse = extra.astype(BF16).astype(F32)
    out_ref[128:CHUNK, :] = jnp.concatenate([coarse, extra - coarse], axis=0).astype(BF16)


def spread_body(c0_ref, c1_ref, c2_ref, c3_ref, out_ref, parts_ref):
    z, core = position()
    for dz, c_ref in enumerate((c0_ref, c1_ref, c2_ref, c3_ref)):
        parts_ref[dz] = c_ref[64:CHUNK, :].astype(F32)
    total = jnp.zeros((80, 128), F32)
    for chip in range(4):
        total = total + parts_ref[(z - chip) & 3]
    gain = total[64:72] + total[72:80]
    coarse = gain.astype(BF16).astype(F32)
    tail = jnp.concatenate([total[0:64], coarse, gain - coarse], axis=0).astype(BF16)
    whole = jnp.concatenate([c_ref[0:64, :] for c_ref in (c0_ref, c1_ref, c2_ref, c3_ref)] + [tail], axis=0)
    for p in range(DOM):
        out_ref[p] = whole


def halo_body(counts_ref, back_ref, rows_ref, x_ref, out_ref, gain_grad_ref):
    row = lax.broadcasted_iota(jnp.int32, (ROWS, CAP), 0)
    slot = lax.broadcasted_iota(jnp.int32, (ROWS, CAP), 1)
    total = jnp.zeros((ROWS, D), F32)
    for k in range(4):
        hits = []
        for p in range(4 * k, 4 * k + 4):
            hit = (row == rows_ref[p : p + 1, :]) & (slot < counts_ref[p])
            hits.append(jnp.where(hit, 1.0, 0.0).astype(BF16))
        part = jnp.concatenate([back_ref[p] for p in range(4 * k, 4 * k + 4)], axis=0)
        total = total + dot(jnp.concatenate(hits, axis=1), part)
    out_ref[...] = total
    x = x_ref[...].astype(F32)
    scale = lax.rsqrt(jnp.mean(x * x, axis=-1, keepdims=True) + EPS)
    gain_grad = jnp.sum(total * (x * scale), axis=0, keepdims=True)
    gain_grad_ref[...] = jnp.zeros((8, 128), F32)
    for k in range(4):
        gain_grad_ref[k : k + 1, :] = gain_grad[:, k * 128 : (k + 1) * 128]


def rows_body(
    r0_ref, r1_ref, r2_ref, r3_ref, t0_ref, t1_ref, t2_ref, t3_ref, halo_ref, base_ref, x_ref,
    gain_ref, grad_ref, wq_ref, wk_ref, wv_ref, wo_ref,
    out_ref, feature_ref, dq_ref, dk_ref, dv_ref, at_ref,
):
    left = lax.broadcasted_iota(jnp.int32, (ROWS, 128), 1) < HEAD
    z, core = position()
    even = core == 0
    for dz, (r_ref, t_ref) in enumerate(zip((r0_ref, r1_ref, r2_ref, r3_ref), (t0_ref, t1_ref, t2_ref, t3_ref))):
        chip = (z + dz) & 3
        one, two = r_ref[0].astype(F32), t_ref[...].astype(F32)
        low, high = jnp.where(even, one, two), jnp.where(even, two, one)
        low0, low1 = low[:, 0:128], low[:, 128:256]
        high0, high1 = high[:, 0:128], high[:, 128:256]
        dq_ref[chip] = jnp.where(left, low0, pltpu.roll(high0, HEAD, 1)).astype(BF16)
        dk_ref[chip] = jnp.where(left, pltpu.roll(low0, HEAD, 1), high0).astype(BF16)
        dv_ref[chip] = jnp.where(left, low1, pltpu.roll(high1, HEAD, 1)).astype(BF16)
        at_ref[chip] = jnp.where(left, pltpu.roll(low1, HEAD, 1), high1).astype(BF16)

    def whole(ref):
        return jnp.concatenate([ref[m] for m in range(4)], axis=1)

    out_ref[...] = (base_ref[...] + dot(whole(at_ref), wo_ref[...])).astype(BF16)
    dnormed = dot(whole(dq_ref), wq_ref[...], NT) + dot(whole(dk_ref), wk_ref[...], NT)
    dnormed = dnormed + dot(whole(dv_ref), wv_ref[...], NT) + halo_ref[...]
    x = x_ref[...].astype(F32)
    scale = lax.rsqrt(jnp.mean(x * x, axis=-1, keepdims=True) + EPS)
    scaled = dnormed * gain_ref[...]
    inner = jnp.mean(scaled * x, axis=-1, keepdims=True)
    dx = scale * scaled - x * (scale * scale * scale * inner)
    feature_ref[...] = (grad_ref[...].astype(F32) + dx).astype(BF16)


def weights_body(mine_ref, other_ref, gain_in_ref, out_ref, gain_ref, all_ref):
    which = pl.program_id(0)

    @pl.when(which == 0)
    def _():
        z, core = position()
        all_ref[core] = mine_ref[...]
        all_ref[1 - core] = other_ref[...]
        gain = jnp.zeros((8, 128), F32)
        through = []
        for p in range(DOM):
            tails = [ref[p, 320:SPREAD, :].astype(F32) for ref in (mine_ref, other_ref)]
            tails = [tail[0:8] + tail[8:16] for tail in tails]
            gain = gain + tails[0]
            through.append(tails[0] + tails[1])
        for b in range(4):
            part = (through[b] + through[4 + b] + through[8 + b])[4:5]
            lanes = slice(b * 128, (b + 1) * 128)
            gain_ref[:, lanes] = gain[b : b + 1] + part / gain_in_ref[:, lanes]

    def piece(h, p):
        z, core = position()
        start = pl.multiple_of(((z - (h >> 1)) & 3) * 64, 64)
        return all_ref[h & 1, p, pl.ds(start, 64), :].astype(F32)

    @pl.when(which < 3)
    def _():
        for b in range(4):
            part = jnp.concatenate([piece(h, which * 4 + b) for h in range(BLK)], axis=0)
            out_ref[0, b * 128 : (b + 1) * 128, :] = jnp.transpose(part)

    @pl.when(which == 3)
    def _():
        for h in range(BLK):
            for b in range(4):
                out_ref[0, h * 64 : (h + 1) * 64, b * 128 : (b + 1) * 128] = piece(h, 12 + b)

    @pl.when(which == 4)
    def _():
        for half in range(2):
            for p in range(DOM):
                top = half * 256 + p * 16
                for b in range(4):
                    part = all_ref[half, p, 256 + b * 16 : 272 + b * 16, :]
                    out_ref[0, top : top + 16, b * 128 : (b + 1) * 128] = part.astype(F32)


def chip_shift(step, swap):
    return [(z * 2 + c, ((z + step) % 4) * 2 + (c ^ swap)) for z in range(4) for c in range(2)]


def along_chips(array, step):
    return lax.ppermute(array, "blk", chip_shift(step, 0))


def other_core(array):
    return lax.ppermute(array, "blk", chip_shift(0, 1))


def to_dom_peers(array):
    return lax.all_to_all(array, "dom", split_axis=0, concat_axis=0, tiled=True)


def local(
    x, gain, wq, wk, wv, wo, wm, cluster, pattern, send_rows, send_counts, edge_src, edge_dst, out_grad
):
    gain_row = gain.reshape(1, D)
    pay, outgoing = call(
        norm_body,
        (shape((PAY, D), BF16), shape((DOM, CAP, D), BF16)),
        (pattern, send_counts, x, gain_row, cluster.reshape(1, ROWS), out_grad, send_rows),
        scalars=2,
        micros=4,
    )
    incoming = to_dom_peers(outgoing)
    near, far = along_chips(pay, 1), along_chips(pay, 3)

    counts_t, degree, slot_grads, wqkv, wo_head = call(
        edges_body,
        (
            shape((1024, 512), BF16), shape((ROWS, 128), F32), shape((DOM, CAP, D), BF16),
            shape((192, D), BF16), shape((HEAD, D), BF16),
        ),
        (edge_src.reshape(32, 128), edge_dst.reshape(32, 128), out_grad, wm, wq, wk, wv, wo),
        scratch=[pltpu.VMEM((512, 1024), F32)],
        micros=10,
    )
    near, far, degree = lax.optimization_barrier((near, far, degree))
    pays = [pay, near, along_chips(near[0:ROWS], 1), along_chips(far[ROWS:PAY], 3), far]
    pays = pays + [other_core(part) for part in pays]
    slot_grads = lax.optimization_barrier((incoming, slot_grads))[1]
    back = to_dom_peers(slot_grads)

    base, mine, other = call(
        mean_body,
        (shape((ROWS, D), F32), shape((DOM, 64, 128), BF16), shape((DOM, 64, 128), BF16)),
        (counts_t, degree, incoming, x, out_grad, wm),
        micros=4,
    )

    *results, chunks = call(
        attention_body,
        (*[shape((2, ROWS, 256), BF16)] * 4, shape((DOM, 128, 128), BF16)),
        (*pays, wqkv, wo_head, mine, other_core(other)),
        scratch=[
            pltpu.VMEM((BLK, 128, ROWS), F32),
            pltpu.VMEM((BLK, 8, ROWS), F32),
            pltpu.VMEM((BLK, 128, ROWS), BF16),
            pltpu.VMEM((BLK, HEAD, ROWS), BF16),
            pltpu.VMEM((BLK, ROWS, 128), BF16),
            pltpu.VMEM((BLK, ROWS, 128), BF16),
            pltpu.VMEM((BLK, 80, ROWS), BF16),
            pltpu.VMEM((BLK, BLK, ROWS, ROWS), BF16),
            pltpu.VMEM((BLK, HEAD, ROWS), F32),
            pltpu.VMEM((BLK, HEAD, ROWS), F32),
            pltpu.VMEM((BLK, HEAD, ROWS), F32),
            pltpu.VMEM((BLK, HEAD, ROWS), BF16),
            pltpu.VMEM((BLK, HEAD, ROWS), F32),
            pltpu.VMEM((BLK, BLK, ROWS, ROWS), BF16),
            pltpu.VMEM((BLK, ROWS, 128), BF16),
            pltpu.VMEM((BLK, ROWS, 128), BF16),
        ],
        micros=12,
    )
    chunks = lax.optimization_barrier((chunks, back))[0]
    chunks = to_dom_peers(chunks)
    halo, gain_part = call(
        halo_body,
        (shape((ROWS, D), F32), shape((8, 128), F32)),
        (send_counts, back, send_rows, x),
        scalars=1,
        micros=3,
    )
    chunk = call(
        chunk_sum_body,
        shape((CHUNK, 128), BF16),
        (chunks, gain_part, other_core(gain_part), wqkv),
        scratch=[pltpu.VMEM((8, 128), F32)],
        micros=1,
    )
    chunk_parts = [chunk] + [along_chips(chunk, step) for step in (1, 2, 3)]
    spread = call(
        spread_body, shape((DOM, SPREAD, 128), BF16), chunk_parts, scratch=[pltpu.VMEM((4, 80, 128), F32)], micros=1
    )
    spread, *results = lax.optimization_barrier((spread, *results))
    gathered = to_dom_peers(spread)
    results = [results[0]] + [along_chips(results[dz], -dz) for dz in (1, 2, 3)]
    swapped = [other_core(part[1]) for part in results]
    gathered, *swapped = lax.optimization_barrier((gathered, *swapped))
    gathered_other = other_core(gathered)
    layer_out, feature_grad = call(
        rows_body,
        (shape((ROWS, D), BF16), shape((ROWS, D), BF16)),
        (*results, *swapped, halo, base, x, gain_row, out_grad, wq, wk, wv, wo),
        scratch=[pltpu.VMEM((4, ROWS, 128), BF16)] * 4,
        micros=2,
    )
    gathered, gathered_other, layer_out, feature_grad = lax.optimization_barrier(
        (gathered, gathered_other, layer_out, feature_grad)
    )
    whole = pl.BlockSpec((DOM, SPREAD, 128), lambda t: (0, 0, 0))
    row = pl.BlockSpec((1, D), lambda t: (0, 0))
    weight_grads, gain_grad = pl.pallas_call(
        weights_body,
        grid=(5,),
        out_shape=(shape((5, D, D), F32), shape((1, D), F32)),
        in_specs=[whole, whole, row],
        out_specs=(pl.BlockSpec((1, D, D), lambda t: (t, 0, 0)), row),
        scratch_shapes=[pltpu.VMEM((2, DOM, SPREAD, 128), BF16)],
    )(gathered, gathered_other, gain_row)
    return layer_out, feature_grad, weight_grads, gain_grad.reshape(D)


def solution(mesh):
    both = ("dom", "blk")
    placed = (
        P(both, None), P(), P(), P(), P(), P(), P(), P(both), P(both, None), P(both, None), P(both), P(both), P(both),
        P(both, None),
    )
    return jax.shard_map(
        local,
        mesh=mesh,
        in_specs=placed,
        out_specs=(P(both, None), P(both, None), P(), P()),
        check_vma=False,
    )
```

```python
import math

import jax
import jax.numpy as jnp
from jax import lax
from jax.experimental import pallas as pl
from jax.experimental.pallas import tpu as pltpu
from jax.sharding import PartitionSpec as P

F32 = jnp.float32
BF16 = jnp.bfloat16
EPS = 1e-06
D = 512
ROWS = 256
HEAD = 64
BLK = 8
DOM = 16
CAP = 128
EDGES = 4096
PAY = 2 * ROWS + 16
LOG2E = math.log2(math.e)
SCORE_MUL = LOG2E / 8.0
SCORE_SUB = (8.0 + 256.0) * LOG2E
CHUNK = 64 + 64 + 16
SPREAD = 4 * 64 + 64 + 16

NT = (((1,), (1,)), ((), ()))
NN = (((1,), (0,)), ((), ()))


def dot(a, b, dims=NN):
    return lax.dot_general(a, b, dims, preferred_element_type=F32)


def call(body, out_shape, operands, scratch=(), scalars=0, micros=2, left=()):
    specs = [pl.BlockSpec(memory_space=pltpu.SMEM)] * scalars
    specs += [pl.BlockSpec(memory_space=pltpu.VMEM)] * (len(operands) - scalars)
    for at in left:
        specs[at] = pl.BlockSpec(memory_space=pltpu.HBM)
    return pl.pallas_call(
        body,
        out_shape=out_shape,
        in_specs=specs,
        out_specs=jax.tree.map(lambda _: pl.BlockSpec(memory_space=pltpu.VMEM), out_shape),
        scratch_shapes=list(scratch),
        cost_estimate=pl.CostEstimate(flops=int(micros * 1e9), transcendentals=0, bytes_accessed=1 << 20),
    )(*operands)


def shape(dims, dtype):
    return jax.ShapeDtypeStruct(dims, dtype)


def dom_position():
    me = lax.axis_index("dom").astype(jnp.int32)
    return lax.shift_right_logical(me, 2), me & 3


def position():
    me = lax.axis_index("blk").astype(jnp.int32)
    return lax.shift_right_logical(me, 1), me & 1


def norm_body(pattern_ref, counts_ref, x_ref, gain_ref, label_ref, grad_ref, rows_ref, out_ref, slots_ref):
    x = x_ref[...].astype(F32)
    scale = lax.rsqrt(jnp.mean(x * x, axis=-1, keepdims=True) + EPS)
    normed = (x * scale * gain_ref[...]).astype(BF16)
    out_ref[0:ROWS, :] = normed
    out_ref[ROWS : 2 * ROWS, :] = grad_ref[...]
    row = lax.broadcasted_iota(jnp.int32, (16, ROWS), 0)
    lane = lax.broadcasted_iota(jnp.int32, (16, ROWS), 1)
    tail = jnp.where(row == 0, label_ref[...].astype(F32), 0.0)
    for b in range(BLK):
        flag = jnp.where(pattern_ref[0, b] == 1, 1.0, 0.0)
        tail = jnp.where((row == 1 + b) & (lane >= 0), flag, tail)
    out_ref[2 * ROWS : PAY, 0:ROWS] = tail.astype(BF16)
    out_ref[2 * ROWS : PAY, ROWS:D] = jnp.zeros((16, D - ROWS), BF16)
    columns = jnp.transpose(rows_ref[...].astype(F32))
    lane = lax.broadcasted_iota(jnp.int32, (CAP, ROWS), 1).astype(F32)
    slot = lax.broadcasted_iota(jnp.int32, (CAP, ROWS), 0)
    for p in range(DOM):
        hit = (lane == columns[:, p : p + 1]) & (slot < counts_ref[p])
        slots_ref[p] = dot(jnp.where(hit, 1.0, 0.0).astype(BF16), normed).astype(BF16)


E_ROWS = 4


def edges_body(
    src_ref, dst_ref, grad_ref, w_ref, wq_ref, wk_ref, wv_ref, wo_ref,
    counts_t_ref, degree_ref, slots_ref, wqkv_ref, wo_head_ref, acc_ref,
):
    z, core = position()
    head = core * 4 + z
    for m in range(4):
        @pl.when(head >> 1 == m)
        def _():
            for k, ref in enumerate((wq_ref, wk_ref, wv_ref)):
                pair = jnp.transpose(ref[:, m * 128 : (m + 1) * 128].astype(F32))
                picked = jnp.where(head & 1 == 0, pair[0:HEAD], pair[HEAD:128])
                wqkv_ref[k * HEAD : (k + 1) * HEAD, :] = picked.astype(BF16)
            for c in range(2):
                @pl.when(head & 1 == c)
                def _():
                    wo_head_ref[...] = wo_ref[m * 128 + c * HEAD : m * 128 + (c + 1) * HEAD, :]

    low_row = lax.broadcasted_iota(jnp.int32, (512, E_ROWS * 128), 0)
    high_row = lax.broadcasted_iota(jnp.int32, (1024, E_ROWS * 128), 0)
    for step in range(EDGES // (E_ROWS * 128)):
        rows = [step * E_ROWS + k for k in range(E_ROWS)]
        src = jnp.concatenate([src_ref[k : k + 1, :] for k in rows], axis=1)
        dst = jnp.concatenate([dst_ref[k : k + 1, :] for k in rows], axis=1)
        low = jnp.where(low_row == (src & 511), 1.0, 0.0).astype(BF16)
        high = jnp.where(high_row == ((src >> 9) * 256 + dst), 1.0, 0.0).astype(BF16)
        part = dot(low, high, NT)
        if step == 0:
            acc_ref[...] = part
        else:
            acc_ref[...] += part
    counts = acc_ref[...]
    per_row = jnp.sum(counts, axis=0, keepdims=True)
    per_row = per_row[:, 0:256] + per_row[:, 256:512] + per_row[:, 512:768] + per_row[:, 768:1024]
    degree = jnp.transpose(jnp.broadcast_to(jnp.maximum(per_row, 1.0), (128, ROWS)))
    degree_ref[...] = degree
    counts_t_ref[...] = jnp.transpose(counts).astype(BF16)
    counts = counts.astype(BF16)
    inverse = 1.0 / degree[:, 0:1]
    message = (dot(grad_ref[...], w_ref[...], NT) * inverse).astype(BF16)
    for high in range(4):
        part = dot(counts[:, high * 256 : (high + 1) * 256], message).astype(BF16)
        for k in range(4):
            slots_ref[high * 4 + k] = part[k * CAP : (k + 1) * CAP, :]


def mean_body(counts_t_ref, degree_ref, table_ref, x_ref, grad_ref, w_ref, base_ref, mine_ref, other_ref):
    total = jnp.zeros((ROWS, D), F32)
    for high in range(4):
        table = jnp.concatenate([table_ref[high * 4 + k] for k in range(4)], axis=0)
        total = total + dot(counts_t_ref[high * 256 : (high + 1) * 256, :], table)
    mean_rows = (total / degree_ref[:, 0:1]).astype(BF16)
    base_ref[...] = x_ref[...].astype(F32) + dot(mean_rows, w_ref[...])
    dw = dot(jnp.transpose(mean_rows.astype(F32)).astype(BF16), grad_ref[...]).astype(BF16)
    z, core = position()
    for half in range(2):
        def fill(ref):
            for p in range(DOM):
                top = half * 256 + p * 16
                for b in range(4):
                    ref[p, b * 16 : (b + 1) * 16, :] = dw[top : top + 16, b * 128 : (b + 1) * 128]

        @pl.when(core == half)
        def _():
            fill(mine_ref)

        @pl.when(core != half)
        def _():
            fill(other_ref)


def attention_body(
    p0_ref, p1_ref, t2_ref, b2_ref, p3_ref, p4_ref, p5_ref, t6_ref, b6_ref, p7_ref, wqkv_ref, wo_ref, mine_ref, other_ref,
    r0_ref, r1_ref, r2_ref, r3_ref, chunks_ref,
    y_ref, s_ref, qt_ref, kt_ref, k_ref, v_ref, vt_ref, w_ref, dq_ref, dk_ref, dv_ref, at_ref, ga_ref, sl_ref, qr_ref, gr_ref,
):
    pays = (p0_ref, p1_ref, (t2_ref, b2_ref), p3_ref, p4_ref, p5_ref, (t6_ref, b6_ref), p7_ref)

    def normed_of(pay):
        return pay[0][...] if isinstance(pay, tuple) else pay[0:ROWS, :]

    def grads_of(pay):
        return pay[1][0:ROWS, :] if isinstance(pay, tuple) else pay[ROWS : 2 * ROWS, :]

    def tail_of(pay):
        return pay[1][ROWS : PAY - ROWS, 0:ROWS] if isinstance(pay, tuple) else pay[2 * ROWS : PAY, 0:ROWS]

    outs = (r0_ref, r1_ref, r2_ref, r3_ref)
    z, core = position()
    row = lax.broadcasted_iota(jnp.int32, (HEAD, ROWS), 0)
    number = row.astype(F32)

    def head_scale(part):
        return lax.rsqrt(jnp.sum(part * part, axis=0, keepdims=True) * (1.0 / HEAD) + EPS)

    for r in range(BLK):
        pay = pays[r]
        projected = dot(wqkv_ref[...], normed_of(pay), NT)
        query, key, value = projected[0:HEAD], projected[HEAD:128], projected[128:192]
        scale_q, scale_k = head_scale(query), head_scale(key)
        query, key = query * scale_q, key * scale_k
        y_ref[r, 0:HEAD] = query
        y_ref[r, HEAD:128] = key
        s_ref[r, 0:1] = scale_q
        s_ref[r, 1:2] = scale_k
        tail = tail_of(pay).astype(F32)
        same = jnp.where(number == tail[0:1], 32.0, 0.0)
        sender = ((z - (r & 3)) & 3) * 2 + (core ^ (r >> 2))
        wanted = jnp.concatenate([jnp.zeros((16, ROWS), F32), tail[1:9] * 32.0, jnp.zeros((40, ROWS), F32)], axis=0)
        owner = jnp.where(row == 16 + sender, 32.0, 0.0)
        qt_ref[r] = jnp.concatenate([query, same + wanted], axis=0).astype(BF16)
        key = jnp.concatenate([key, same + owner], axis=0)
        kt_ref[r] = key[0:HEAD].astype(BF16)
        k_ref[r] = jnp.transpose(key).astype(BF16)
        value = jnp.concatenate([value, jnp.where(row < 2, 1.0, 0.0)], axis=0)
        vt_ref[r] = value[0:80].astype(BF16)
        v_ref[r] = jnp.transpose(value).astype(BF16)
        ga_ref[r] = dot(wo_ref[...], grads_of(pay), NT)
        qr_ref[r] = jnp.transpose(qt_ref[r].astype(F32)).astype(BF16)

    keys_t = jnp.concatenate([kt_ref[j] for j in range(BLK)], axis=1)
    values_t = jnp.concatenate([vt_ref[j] for j in range(BLK)], axis=1)

    def query_block(i, carry):
        query = qt_ref[i]
        for j in range(BLK):
            scores = dot(k_ref[j], query)
            w_ref[i, j] = jnp.exp2(scores * SCORE_MUL - SCORE_SUB).astype(BF16)
        numer = dot(values_t, w_ref[i].reshape(BLK * ROWS, ROWS))
        inverse = 1.0 / numer[HEAD : HEAD + 1]
        attn = (numer[0:HEAD] * inverse).astype(BF16)
        at_ref[i] = attn
        grad_attn = ga_ref[i]
        minus = jnp.sum(grad_attn * attn.astype(F32), axis=0, keepdims=True) * (-inverse)
        coarse = minus.astype(BF16).astype(F32)
        extra = jnp.where(row == 0, coarse, jnp.where(row == 1, minus - coarse, 0.0))
        grad = jnp.concatenate([grad_attn * inverse, extra], axis=0).astype(BF16)
        gr_ref[i] = jnp.transpose(grad.astype(F32)).astype(BF16)
        for j in range(BLK):
            sl_ref[i, j] = (w_ref[i, j].astype(F32) * dot(v_ref[j], grad)).astype(BF16)
        dq_ref[i] = dot(keys_t, sl_ref[i].reshape(BLK * ROWS, ROWS))
        return carry

    lax.fori_loop(0, BLK, query_block, 0)

    queries = jnp.concatenate([qr_ref[i] for i in range(BLK)], axis=0)
    grads = jnp.concatenate([gr_ref[i] for i in range(BLK)], axis=0)

    def key_block(j, carry):
        slopes = jnp.concatenate([sl_ref[i, j] for i in range(BLK)], axis=1)
        dk_ref[j] = jnp.transpose(dot(slopes, queries))[0:HEAD]
        weights = jnp.concatenate([w_ref[i, j] for i in range(BLK)], axis=1)
        dv_ref[j] = jnp.transpose(dot(weights, grads))[0:HEAD]
        return carry

    lax.fori_loop(0, BLK, key_block, 0)

    dw = jnp.zeros((192, D), F32)
    dwo = jnp.zeros((HEAD, D), F32)
    for r in range(BLK):
        pay = pays[r]

        def pull(grad, y, scale):
            grad = grad * (8.0 / HEAD)
            return scale * (grad - y * (jnp.sum(y * grad, axis=0, keepdims=True) * (1.0 / HEAD)))

        dquery = pull(dq_ref[r], y_ref[r, 0:HEAD], s_ref[r, 0:1])
        dkey = pull(dk_ref[r], y_ref[r, HEAD:128], s_ref[r, 1:2])
        first = jnp.concatenate([dquery, dkey], axis=0)
        second = jnp.concatenate([dv_ref[r], at_ref[r].astype(F32)], axis=0)
        outs[r & 3][r >> 2, :, 0:128] = jnp.transpose(first).astype(BF16)
        outs[r & 3][r >> 2, :, 128:256] = jnp.transpose(second).astype(BF16)
        left = jnp.concatenate([first, second[0:HEAD]], axis=0).astype(BF16)
        dw = dw + dot(left, normed_of(pay))
        dwo = dwo + dot(at_ref[r], grads_of(pay))
    dw = jnp.concatenate([dw, dwo], axis=0).astype(BF16)
    for a in range(4):
        for b in range(4):
            p = a * 4 + b
            chunks_ref[p, 0:64, :] = dw[a * 64 : (a + 1) * 64, b * 128 : (b + 1) * 128]
            chunks_ref[p, 64:128, :] = (mine_ref[p].astype(F32) + other_ref[p].astype(F32)).astype(BF16)


def chunk_sum_body(in_ref, g0_ref, g1_ref, wqkv_ref, out_ref, extra_ref):
    total = in_ref[0].astype(F32)
    for p in range(1, DOM):
        total = total + in_ref[p].astype(F32)
    out_ref[0:128, :] = total.astype(BF16)
    z, core = position()
    kind, lanes = dom_position()
    one, two = g0_ref[...], g1_ref[...]
    extra_ref[...] = jnp.where(core == 0, one, two) + jnp.where(core == 0, two, one)
    for b in range(4):
        @pl.when((kind < 3) & (lanes == b))
        def _():
            start = pl.multiple_of(jnp.minimum(kind, 2) * HEAD, HEAD)
            weights = wqkv_ref[pl.ds(start, HEAD), b * 128 : (b + 1) * 128].astype(F32)
            extra_ref[4:5, :] = jnp.sum(weights * total[0:HEAD], axis=0, keepdims=True)
    extra = extra_ref[...]
    coarse = extra.astype(BF16).astype(F32)
    out_ref[128:CHUNK, :] = jnp.concatenate([coarse, extra - coarse], axis=0).astype(BF16)


def spread_body(c0_ref, c1_ref, c2_ref, c3_ref, out_ref, parts_ref):
    z, core = position()
    for dz, c_ref in enumerate((c0_ref, c1_ref, c2_ref, c3_ref)):
        parts_ref[dz] = c_ref[64:CHUNK, :].astype(F32)
    total = jnp.zeros((80, 128), F32)
    for chip in range(4):
        total = total + parts_ref[(z - chip) & 3]
    gain = total[64:72] + total[72:80]
    coarse = gain.astype(BF16).astype(F32)
    tail = jnp.concatenate([total[0:64], coarse, gain - coarse], axis=0).astype(BF16)
    whole = jnp.concatenate([c_ref[0:64, :] for c_ref in (c0_ref, c1_ref, c2_ref, c3_ref)] + [tail], axis=0)
    for p in range(DOM):
        out_ref[p] = whole


def halo_body(counts_ref, back_ref, rows_ref, x_ref, out_ref, gain_grad_ref):
    row = lax.broadcasted_iota(jnp.int32, (ROWS, CAP), 0)
    slot = lax.broadcasted_iota(jnp.int32, (ROWS, CAP), 1)
    total = jnp.zeros((ROWS, D), F32)
    for k in range(4):
        hits = []
        for p in range(4 * k, 4 * k + 4):
            hit = (row == rows_ref[p : p + 1, :]) & (slot < counts_ref[p])
            hits.append(jnp.where(hit, 1.0, 0.0).astype(BF16))
        part = jnp.concatenate([back_ref[p] for p in range(4 * k, 4 * k + 4)], axis=0)
        total = total + dot(jnp.concatenate(hits, axis=1), part)
    out_ref[...] = total
    x = x_ref[...].astype(F32)
    scale = lax.rsqrt(jnp.mean(x * x, axis=-1, keepdims=True) + EPS)
    gain_grad = jnp.sum(total * (x * scale), axis=0, keepdims=True)
    gain_grad_ref[...] = jnp.zeros((8, 128), F32)
    for k in range(4):
        gain_grad_ref[k : k + 1, :] = gain_grad[:, k * 128 : (k + 1) * 128]


def rows_body(
    r0_ref, r1_ref, r2_ref, r3_ref, t0_ref, t1_ref, t2_ref, t3_ref, halo_ref, base_ref, x_ref,
    gain_ref, grad_ref, wq_ref, wk_ref, wv_ref, wo_ref,
    out_ref, feature_ref, dq_ref, dk_ref, dv_ref, at_ref, heads_ref,
):
    left = lax.broadcasted_iota(jnp.int32, (ROWS, 128), 1) < HEAD
    z, core = position()
    for dz, (r_ref, t_ref) in enumerate(zip((r0_ref, r1_ref, r2_ref, r3_ref), (t0_ref, t1_ref, t2_ref, t3_ref))):
        chip = (z + dz) & 3
        heads_ref[core * 4 + chip] = r_ref[0]
        heads_ref[(1 - core) * 4 + chip] = t_ref[...]
    for m in range(4):
        low, high = heads_ref[2 * m].astype(F32), heads_ref[2 * m + 1].astype(F32)
        low0, low1 = low[:, 0:128], low[:, 128:256]
        high0, high1 = high[:, 0:128], high[:, 128:256]
        dq_ref[m] = jnp.where(left, low0, pltpu.roll(high0, HEAD, 1)).astype(BF16)
        dk_ref[m] = jnp.where(left, pltpu.roll(low0, HEAD, 1), high0).astype(BF16)
        dv_ref[m] = jnp.where(left, low1, pltpu.roll(high1, HEAD, 1)).astype(BF16)
        at_ref[m] = jnp.where(left, pltpu.roll(low1, HEAD, 1), high1).astype(BF16)

    def whole(ref):
        return jnp.concatenate([ref[m] for m in range(4)], axis=1)

    out_ref[...] = (base_ref[...] + dot(whole(at_ref), wo_ref[...])).astype(BF16)
    dnormed = dot(whole(dq_ref), wq_ref[...], NT) + dot(whole(dk_ref), wk_ref[...], NT)
    dnormed = dnormed + dot(whole(dv_ref), wv_ref[...], NT) + halo_ref[...]
    x = x_ref[...].astype(F32)
    scale = lax.rsqrt(jnp.mean(x * x, axis=-1, keepdims=True) + EPS)
    scaled = dnormed * gain_ref[...]
    inner = jnp.mean(scaled * x, axis=-1, keepdims=True)
    dx = scale * scaled - x * (scale * scale * scale * inner)
    feature_ref[...] = (grad_ref[...].astype(F32) + dx).astype(BF16)


def half_body(core, in_ref, out_hbm, tall_ref, wide_ref, sems):
    z, _ = position()
    first = pl.multiple_of(core * 256, 256)
    copies = [
        pltpu.make_async_copy(tall_ref.at[t], out_hbm.at[t, :, pl.ds(first, 256)], sems.at[t]) for t in range(3)
    ] + [
        pltpu.make_async_copy(wide_ref.at[t], out_hbm.at[3 + t, pl.ds(first, 256), :], sems.at[3 + t]) for t in range(2)
    ]

    def piece(chip, p):
        start = pl.multiple_of(((z - chip) & 3) * 64, 64)
        return in_ref[p, pl.ds(start, 64), :].astype(F32)

    for t in range(3):
        for b in range(4):
            part = jnp.concatenate([piece(chip, t * 4 + b) for chip in range(4)], axis=0)
            tall_ref[t, b * 128 : (b + 1) * 128, :] = jnp.transpose(part)
        copies[t].start()
    for b in range(4):
        for chip in range(4):
            wide_ref[0, chip * 64 : (chip + 1) * 64, b * 128 : (b + 1) * 128] = piece(chip, 12 + b)
    copies[3].start()
    for p in range(DOM):
        for b in range(4):
            part = in_ref[p, 256 + b * 16 : 272 + b * 16, :]
            wide_ref[1, p * 16 : (p + 1) * 16, b * 128 : (b + 1) * 128] = part.astype(F32)
    copies[4].start()
    for copy in copies:
        copy.wait()


def tails_of(ref):
    tails = [ref[p, 320:SPREAD, :].astype(F32) for p in range(DOM)]
    return [tail[0:8] + tail[8:16] for tail in tails]


def first_half_body(mine_ref, out_hbm, tall_ref, wide_ref, sems):
    half_body(position()[1], mine_ref, out_hbm, tall_ref, wide_ref, sems)


def second_half_body(before_hbm, mine_ref, other_ref, gain_in_ref, out_hbm, gain_ref, tall_ref, wide_ref, sems):
    gain = jnp.zeros((8, 128), F32)
    mine, through = tails_of(mine_ref), tails_of(other_ref)
    for p in range(DOM):
        gain = gain + mine[p]
        through[p] = through[p] + mine[p]
    for b in range(4):
        part = (through[b] + through[4 + b] + through[8 + b])[4:5]
        lanes = slice(b * 128, (b + 1) * 128)
        gain_ref[:, lanes] = gain[b : b + 1] + part / gain_in_ref[:, lanes]
    half_body(1 - position()[1], other_ref, out_hbm, tall_ref, wide_ref, sems)


def in_halves(mine, other, gain_row):
    vmem, hbm = pl.BlockSpec(memory_space=pltpu.VMEM), pl.BlockSpec(memory_space=pltpu.HBM)
    scratch = [pltpu.VMEM((3, D, 256), F32), pltpu.VMEM((2, 256, D), F32), pltpu.SemaphoreType.DMA((5,))]
    half = pl.pallas_call(
        first_half_body, out_shape=shape((5, D, D), F32), in_specs=[vmem], out_specs=hbm, scratch_shapes=scratch,
        cost_estimate=pl.CostEstimate(flops=int(3e9), transcendentals=0, bytes_accessed=1 << 20),
    )(mine)
    return pl.pallas_call(
        second_half_body,
        out_shape=(shape((5, D, D), F32), shape((1, D), F32)),
        in_specs=[hbm, vmem, vmem, vmem],
        out_specs=(hbm, vmem),
        input_output_aliases={0: 0},
        scratch_shapes=scratch,
    )(half, mine, other, gain_row)


def chip_shift(step, swap):
    return [(z * 2 + c, ((z + step) % 4) * 2 + (c ^ swap)) for z in range(4) for c in range(2)]


def along_chips(array, step):
    return lax.ppermute(array, "blk", chip_shift(step, 0))


def other_core(array):
    return lax.ppermute(array, "blk", chip_shift(0, 1))


def to_dom_peers(array):
    return lax.all_to_all(array, "dom", split_axis=0, concat_axis=0, tiled=True)


def local(
    x, gain, wq, wk, wv, wo, wm, cluster, pattern, send_rows, send_counts, edge_src, edge_dst, out_grad
):
    gain_row = gain.reshape(1, D)
    pay, outgoing = call(
        norm_body,
        (shape((PAY, D), BF16), shape((DOM, CAP, D), BF16)),
        (pattern, send_counts, x, gain_row, cluster.reshape(1, ROWS), out_grad, send_rows),
        scalars=2,
        micros=4,
    )
    incoming = to_dom_peers(outgoing)
    near, far = along_chips(pay, 1), along_chips(pay, 3)

    counts_t, degree, slot_grads, wqkv, wo_head = call(
        edges_body,
        (
            shape((1024, 512), BF16), shape((ROWS, 128), F32), shape((DOM, CAP, D), BF16),
            shape((192, D), BF16), shape((HEAD, D), BF16),
        ),
        (edge_src.reshape(32, 128), edge_dst.reshape(32, 128), out_grad, wm, wq, wk, wv, wo),
        scratch=[pltpu.VMEM((512, 1024), F32)],
        micros=10,
    )
    near, far, degree = lax.optimization_barrier((near, far, degree))
    pays = [pay, near, along_chips(near[0:ROWS], 1), along_chips(far[ROWS:PAY], 3), far]
    pays = pays + [other_core(part) for part in pays]
    slot_grads = lax.optimization_barrier((incoming, slot_grads))[1]
    back = to_dom_peers(slot_grads)

    base, mine, other = call(
        mean_body,
        (shape((ROWS, D), F32), shape((DOM, 64, 128), BF16), shape((DOM, 64, 128), BF16)),
        (counts_t, degree, incoming, x, out_grad, wm),
        micros=4,
    )

    *results, chunks = call(
        attention_body,
        (*[shape((2, ROWS, 256), BF16)] * 4, shape((DOM, 128, 128), BF16)),
        (*pays, wqkv, wo_head, mine, other_core(other)),
        scratch=[
            pltpu.VMEM((BLK, 128, ROWS), F32),
            pltpu.VMEM((BLK, 8, ROWS), F32),
            pltpu.VMEM((BLK, 128, ROWS), BF16),
            pltpu.VMEM((BLK, HEAD, ROWS), BF16),
            pltpu.VMEM((BLK, ROWS, 128), BF16),
            pltpu.VMEM((BLK, ROWS, 128), BF16),
            pltpu.VMEM((BLK, 80, ROWS), BF16),
            pltpu.VMEM((BLK, BLK, ROWS, ROWS), BF16),
            pltpu.VMEM((BLK, HEAD, ROWS), F32),
            pltpu.VMEM((BLK, HEAD, ROWS), F32),
            pltpu.VMEM((BLK, HEAD, ROWS), F32),
            pltpu.VMEM((BLK, HEAD, ROWS), BF16),
            pltpu.VMEM((BLK, HEAD, ROWS), F32),
            pltpu.VMEM((BLK, BLK, ROWS, ROWS), BF16),
            pltpu.VMEM((BLK, ROWS, 128), BF16),
            pltpu.VMEM((BLK, ROWS, 128), BF16),
        ],
        micros=12,
    )
    chunks = lax.optimization_barrier((chunks, back))[0]
    chunks = to_dom_peers(chunks)
    halo, gain_part = call(
        halo_body,
        (shape((ROWS, D), F32), shape((8, 128), F32)),
        (send_counts, back, send_rows, x),
        scalars=1,
        micros=3,
    )
    *results, gain_part = lax.optimization_barrier((*results, gain_part))
    results = [results[0]] + [along_chips(results[dz], -dz) for dz in (1, 2, 3)]
    chunk = call(
        chunk_sum_body,
        shape((CHUNK, 128), BF16),
        (chunks, gain_part, other_core(gain_part), wqkv),
        scratch=[pltpu.VMEM((8, 128), F32)],
        micros=1,
    )
    chunk_parts = [chunk] + [along_chips(chunk, step) for step in (1, 2, 3)]
    *chunk_parts, r1, r2, r3 = lax.optimization_barrier((*chunk_parts, *results[1:]))
    results = [results[0], r1, r2, r3]
    spread = call(
        spread_body, shape((DOM, SPREAD, 128), BF16), chunk_parts, scratch=[pltpu.VMEM((4, 80, 128), F32)], micros=1
    )
    spread, *results = lax.optimization_barrier((spread, *results))
    gathered = to_dom_peers(spread)
    swapped = [other_core(part[1]) for part in results]
    layer_out, feature_grad = call(
        rows_body,
        (shape((ROWS, D), BF16), shape((ROWS, D), BF16)),
        (*results, *swapped, halo, base, x, gain_row, out_grad, wq, wk, wv, wo),
        scratch=[pltpu.VMEM((4, ROWS, 128), BF16)] * 4 + [pltpu.VMEM((BLK, ROWS, 256), BF16)],
        micros=2,
    )
    gathered, layer_out, feature_grad = lax.optimization_barrier((gathered, layer_out, feature_grad))
    gathered_other = other_core(gathered)
    weight_grads, gain_grad = in_halves(gathered, gathered_other, gain_row)
    return layer_out, feature_grad, weight_grads, gain_grad.reshape(D)


def solution(mesh):
    both = ("dom", "blk")
    placed = (
        P(both, None), P(), P(), P(), P(), P(), P(), P(both), P(both, None), P(both, None), P(both), P(both), P(both),
        P(both, None),
    )
    return jax.shard_map(
        local,
        mesh=mesh,
        in_specs=placed,
        out_specs=(P(both, None), P(both, None), P(), P()),
        check_vma=False,
    )
```

```python
import math

import jax
import jax.numpy as jnp
from jax import lax
from jax.experimental import pallas as pl
from jax.experimental.pallas import tpu as pltpu
from jax.sharding import PartitionSpec as P

F32 = jnp.float32
BF16 = jnp.bfloat16
EPS = 1e-06
D = 512
ROWS = 256
HEAD = 64
BLK = 8
DOM = 16
CAP = 128
EDGES = 4096
PAY = 2 * ROWS + 16
LOG2E = math.log2(math.e)
SCORE_MUL = LOG2E / 8.0
SCORE_SUB = (8.0 + 256.0) * LOG2E
CHUNK = 64 + 64 + 16
SPREAD = 4 * 64 + 64 + 16

NT = (((1,), (1,)), ((), ()))
NN = (((1,), (0,)), ((), ()))


def dot(a, b, dims=NN):
    return lax.dot_general(a, b, dims, preferred_element_type=F32)


def call(body, out_shape, operands, scratch=(), scalars=0, micros=2, left=()):
    specs = [pl.BlockSpec(memory_space=pltpu.SMEM)] * scalars
    specs += [pl.BlockSpec(memory_space=pltpu.VMEM)] * (len(operands) - scalars)
    for at in left:
        specs[at] = pl.BlockSpec(memory_space=pltpu.HBM)
    return pl.pallas_call(
        body,
        out_shape=out_shape,
        in_specs=specs,
        out_specs=jax.tree.map(lambda _: pl.BlockSpec(memory_space=pltpu.VMEM), out_shape),
        scratch_shapes=list(scratch),
        cost_estimate=pl.CostEstimate(flops=int(micros * 1e9), transcendentals=0, bytes_accessed=1 << 20),
    )(*operands)


def shape(dims, dtype):
    return jax.ShapeDtypeStruct(dims, dtype)


def dom_position():
    me = lax.axis_index("dom").astype(jnp.int32)
    return lax.shift_right_logical(me, 2), me & 3


def position():
    me = lax.axis_index("blk").astype(jnp.int32)
    return lax.shift_right_logical(me, 1), me & 1


def norm_body(pattern_ref, counts_ref, x_ref, gain_ref, label_ref, grad_ref, rows_ref, out_ref, slots_ref):
    x = x_ref[...].astype(F32)
    scale = lax.rsqrt(jnp.mean(x * x, axis=-1, keepdims=True) + EPS)
    normed = (x * scale * gain_ref[...]).astype(BF16)
    out_ref[0:ROWS, :] = normed
    out_ref[ROWS : 2 * ROWS, :] = grad_ref[...]
    row = lax.broadcasted_iota(jnp.int32, (16, ROWS), 0)
    lane = lax.broadcasted_iota(jnp.int32, (16, ROWS), 1)
    tail = jnp.where(row == 0, label_ref[...].astype(F32), 0.0)
    for b in range(BLK):
        flag = jnp.where(pattern_ref[0, b] == 1, 1.0, 0.0)
        tail = jnp.where((row == 1 + b) & (lane >= 0), flag, tail)
    out_ref[2 * ROWS : PAY, 0:ROWS] = tail.astype(BF16)
    out_ref[2 * ROWS : PAY, ROWS:D] = jnp.zeros((16, D - ROWS), BF16)
    columns = jnp.transpose(rows_ref[...].astype(F32))
    lane = lax.broadcasted_iota(jnp.int32, (CAP, ROWS), 1).astype(F32)
    slot = lax.broadcasted_iota(jnp.int32, (CAP, ROWS), 0)
    for p in range(DOM):
        hit = (lane == columns[:, p : p + 1]) & (slot < counts_ref[p])
        slots_ref[p] = dot(jnp.where(hit, 1.0, 0.0).astype(BF16), normed).astype(BF16)


E_ROWS = 4


def edges_body(
    src_ref, dst_ref, grad_ref, w_ref, wq_ref, wk_ref, wv_ref, wo_ref,
    counts_t_ref, degree_ref, slots_ref, wqkv_ref, wo_head_ref, acc_ref,
):
    z, core = position()
    head = core * 4 + z
    for m in range(4):
        @pl.when(head >> 1 == m)
        def _():
            for k, ref in enumerate((wq_ref, wk_ref, wv_ref)):
                pair = jnp.transpose(ref[:, m * 128 : (m + 1) * 128].astype(F32))
                picked = jnp.where(head & 1 == 0, pair[0:HEAD], pair[HEAD:128])
                wqkv_ref[k * HEAD : (k + 1) * HEAD, :] = picked.astype(BF16)
            for c in range(2):
                @pl.when(head & 1 == c)
                def _():
                    wo_head_ref[...] = wo_ref[m * 128 + c * HEAD : m * 128 + (c + 1) * HEAD, :]

    low_row = lax.broadcasted_iota(jnp.int32, (512, E_ROWS * 128), 0)
    high_row = lax.broadcasted_iota(jnp.int32, (1024, E_ROWS * 128), 0)
    for step in range(EDGES // (E_ROWS * 128)):
        rows = [step * E_ROWS + k for k in range(E_ROWS)]
        src = jnp.concatenate([src_ref[k : k + 1, :] for k in rows], axis=1)
        dst = jnp.concatenate([dst_ref[k : k + 1, :] for k in rows], axis=1)
        low = jnp.where(low_row == (src & 511), 1.0, 0.0).astype(BF16)
        high = jnp.where(high_row == ((src >> 9) * 256 + dst), 1.0, 0.0).astype(BF16)
        part = dot(low, high, NT)
        if step == 0:
            acc_ref[...] = part
        else:
            acc_ref[...] += part
    counts = acc_ref[...]
    per_row = jnp.sum(counts, axis=0, keepdims=True)
    per_row = per_row[:, 0:256] + per_row[:, 256:512] + per_row[:, 512:768] + per_row[:, 768:1024]
    degree = jnp.transpose(jnp.broadcast_to(jnp.maximum(per_row, 1.0), (128, ROWS)))
    degree_ref[...] = degree
    counts_t_ref[...] = jnp.transpose(counts).astype(BF16)
    counts = counts.astype(BF16)
    inverse = 1.0 / degree[:, 0:1]
    message = (dot(grad_ref[...], w_ref[...], NT) * inverse).astype(BF16)
    for high in range(4):
        part = dot(counts[:, high * 256 : (high + 1) * 256], message).astype(BF16)
        for k in range(4):
            slots_ref[high * 4 + k] = part[k * CAP : (k + 1) * CAP, :]


def mean_body(counts_t_ref, degree_ref, table_ref, x_ref, grad_ref, w_ref, base_ref, mine_ref, other_ref):
    total = jnp.zeros((ROWS, D), F32)
    for high in range(4):
        table = jnp.concatenate([table_ref[high * 4 + k] for k in range(4)], axis=0)
        total = total + dot(counts_t_ref[high * 256 : (high + 1) * 256, :], table)
    mean_rows = (total / degree_ref[:, 0:1]).astype(BF16)
    base_ref[...] = x_ref[...].astype(F32) + dot(mean_rows, w_ref[...])
    dw = dot(jnp.transpose(mean_rows.astype(F32)).astype(BF16), grad_ref[...]).astype(BF16)
    z, core = position()
    for half in range(2):
        def fill(ref):
            for p in range(DOM):
                top = half * 256 + p * 16
                for b in range(4):
                    ref[p, b * 16 : (b + 1) * 16, :] = dw[top : top + 16, b * 128 : (b + 1) * 128]

        @pl.when(core == half)
        def _():
            fill(mine_ref)

        @pl.when(core != half)
        def _():
            fill(other_ref)


def attention_body(
    p0_ref, p1_ref, t2_ref, b2_ref, p3_ref, p4_ref, p5_ref, t6_ref, b6_ref, p7_ref, wqkv_ref, wo_ref, mine_ref, other_ref,
    paya_ref, payb_ref, chunks_ref,
    y_ref, s_ref, qt_ref, kt_ref, k_ref, v_ref, vt_ref, w_ref, dq_ref, dk_ref, dv_ref, at_ref, ga_ref, sl_ref, qr_ref, gr_ref,
):
    pays = (p0_ref, p1_ref, (t2_ref, b2_ref), p3_ref, p4_ref, p5_ref, (t6_ref, b6_ref), p7_ref)

    def normed_of(pay):
        return pay[0][...] if isinstance(pay, tuple) else pay[0:ROWS, :]

    def grads_of(pay):
        return pay[1][0:ROWS, :] if isinstance(pay, tuple) else pay[ROWS : 2 * ROWS, :]

    def tail_of(pay):
        return pay[1][ROWS : PAY - ROWS, 0:ROWS] if isinstance(pay, tuple) else pay[2 * ROWS : PAY, 0:ROWS]

    outs = (paya_ref, payb_ref)
    z, core = position()
    row = lax.broadcasted_iota(jnp.int32, (HEAD, ROWS), 0)
    number = row.astype(F32)

    def head_scale(part):
        return lax.rsqrt(jnp.sum(part * part, axis=0, keepdims=True) * (1.0 / HEAD) + EPS)

    for r in range(BLK):
        pay = pays[r]
        projected = dot(wqkv_ref[...], normed_of(pay), NT)
        query, key, value = projected[0:HEAD], projected[HEAD:128], projected[128:192]
        scale_q, scale_k = head_scale(query), head_scale(key)
        query, key = query * scale_q, key * scale_k
        y_ref[r, 0:HEAD] = query
        y_ref[r, HEAD:128] = key
        s_ref[r, 0:1] = scale_q
        s_ref[r, 1:2] = scale_k
        tail = tail_of(pay).astype(F32)
        same = jnp.where(number == tail[0:1], 32.0, 0.0)
        sender = ((z - (r & 3)) & 3) * 2 + (core ^ (r >> 2))
        wanted = jnp.concatenate([jnp.zeros((16, ROWS), F32), tail[1:9] * 32.0, jnp.zeros((40, ROWS), F32)], axis=0)
        owner = jnp.where(row == 16 + sender, 32.0, 0.0)
        qt_ref[r] = jnp.concatenate([query, same + wanted], axis=0).astype(BF16)
        key = jnp.concatenate([key, same + owner], axis=0)
        kt_ref[r] = key[0:HEAD].astype(BF16)
        k_ref[r] = jnp.transpose(key).astype(BF16)
        value = jnp.concatenate([value, jnp.where(row < 2, 1.0, 0.0)], axis=0)
        vt_ref[r] = value[0:80].astype(BF16)
        v_ref[r] = jnp.transpose(value).astype(BF16)
        ga_ref[r] = dot(wo_ref[...], grads_of(pay), NT)
        qr_ref[r] = jnp.transpose(qt_ref[r].astype(F32)).astype(BF16)

    keys_t = jnp.concatenate([kt_ref[j] for j in range(BLK)], axis=1)
    values_t = jnp.concatenate([vt_ref[j] for j in range(BLK)], axis=1)

    def query_block(i, carry):
        query = qt_ref[i]
        for j in range(BLK):
            scores = dot(k_ref[j], query)
            w_ref[i, j] = jnp.exp2(scores * SCORE_MUL - SCORE_SUB).astype(BF16)
        numer = dot(values_t, w_ref[i].reshape(BLK * ROWS, ROWS))
        inverse = 1.0 / numer[HEAD : HEAD + 1]
        attn = (numer[0:HEAD] * inverse).astype(BF16)
        at_ref[i] = attn
        grad_attn = ga_ref[i]
        minus = jnp.sum(grad_attn * attn.astype(F32), axis=0, keepdims=True) * (-inverse)
        coarse = minus.astype(BF16).astype(F32)
        extra = jnp.where(row == 0, coarse, jnp.where(row == 1, minus - coarse, 0.0))
        grad = jnp.concatenate([grad_attn * inverse, extra], axis=0).astype(BF16)
        gr_ref[i] = jnp.transpose(grad.astype(F32)).astype(BF16)
        for j in range(BLK):
            sl_ref[i, j] = (w_ref[i, j].astype(F32) * dot(v_ref[j], grad)).astype(BF16)
        dq_ref[i] = dot(keys_t, sl_ref[i].reshape(BLK * ROWS, ROWS))
        return carry

    lax.fori_loop(0, BLK, query_block, 0)

    queries = jnp.concatenate([qr_ref[i] for i in range(BLK)], axis=0)
    grads = jnp.concatenate([gr_ref[i] for i in range(BLK)], axis=0)

    def key_block(j, carry):
        slopes = jnp.concatenate([sl_ref[i, j] for i in range(BLK)], axis=1)
        dk_ref[j] = jnp.transpose(dot(slopes, queries))[0:HEAD]
        weights = jnp.concatenate([w_ref[i, j] for i in range(BLK)], axis=1)
        dv_ref[j] = jnp.transpose(dot(weights, grads))[0:HEAD]
        return carry

    lax.fori_loop(0, BLK, key_block, 0)

    dw = jnp.zeros((192, D), F32)
    dwo = jnp.zeros((HEAD, D), F32)
    for r in range(BLK):
        pay = pays[r]

        def pull(grad, y, scale):
            grad = grad * (8.0 / HEAD)
            return scale * (grad - y * (jnp.sum(y * grad, axis=0, keepdims=True) * (1.0 / HEAD)))

        dquery = pull(dq_ref[r], y_ref[r, 0:HEAD], s_ref[r, 0:1])
        dkey = pull(dk_ref[r], y_ref[r, HEAD:128], s_ref[r, 1:2])
        first = jnp.concatenate([dquery, dkey], axis=0)
        second = jnp.concatenate([dv_ref[r], at_ref[r].astype(F32)], axis=0)
        outs[r >> 2][r & 3, :, 0:128] = jnp.transpose(first).astype(BF16)
        outs[r >> 2][r & 3, :, 128:256] = jnp.transpose(second).astype(BF16)
        left = jnp.concatenate([first, second[0:HEAD]], axis=0).astype(BF16)
        dw = dw + dot(left, normed_of(pay))
        dwo = dwo + dot(at_ref[r], grads_of(pay))
    dw = jnp.concatenate([dw, dwo], axis=0).astype(BF16)
    for a in range(4):
        for b in range(4):
            p = a * 4 + b
            chunks_ref[p, 0:64, :] = dw[a * 64 : (a + 1) * 64, b * 128 : (b + 1) * 128]
            chunks_ref[p, 64:128, :] = (mine_ref[p].astype(F32) + other_ref[p].astype(F32)).astype(BF16)


def chunk_sum_body(in_ref, g0_ref, g1_ref, wqkv_ref, out_ref, extra_ref):
    total = in_ref[0].astype(F32)
    for p in range(1, DOM):
        total = total + in_ref[p].astype(F32)
    out_ref[0:128, :] = total.astype(BF16)
    z, core = position()
    kind, lanes = dom_position()
    one, two = g0_ref[...], g1_ref[...]
    extra_ref[...] = jnp.where(core == 0, one, two) + jnp.where(core == 0, two, one)
    for b in range(4):
        @pl.when((kind < 3) & (lanes == b))
        def _():
            start = pl.multiple_of(jnp.minimum(kind, 2) * HEAD, HEAD)
            weights = wqkv_ref[pl.ds(start, HEAD), b * 128 : (b + 1) * 128].astype(F32)
            extra_ref[4:5, :] = jnp.sum(weights * total[0:HEAD], axis=0, keepdims=True)
    extra = extra_ref[...]
    coarse = extra.astype(BF16).astype(F32)
    out_ref[128:CHUNK, :] = jnp.concatenate([coarse, extra - coarse], axis=0).astype(BF16)


def spread_body(c0_ref, c1_ref, c2_ref, c3_ref, out_ref, parts_ref):
    z, core = position()
    for dz, c_ref in enumerate((c0_ref, c1_ref, c2_ref, c3_ref)):
        parts_ref[dz] = c_ref[64:CHUNK, :].astype(F32)
    total = jnp.zeros((80, 128), F32)
    for chip in range(4):
        total = total + parts_ref[(z - chip) & 3]
    gain = total[64:72] + total[72:80]
    coarse = gain.astype(BF16).astype(F32)
    tail = jnp.concatenate([total[0:64], coarse, gain - coarse], axis=0).astype(BF16)
    whole = jnp.concatenate([c_ref[0:64, :] for c_ref in (c0_ref, c1_ref, c2_ref, c3_ref)] + [tail], axis=0)
    for p in range(DOM):
        out_ref[p] = whole


def halo_body(
    counts_ref, back_ref, rows_ref, x_ref, paya_ref, payb_ref,
    out_ref, gain_grad_ref, r0_ref, r1_ref, r2_ref, r3_ref,
):
    for dz, r_ref in enumerate((r0_ref, r1_ref, r2_ref, r3_ref)):
        r_ref[0] = paya_ref[dz]
        r_ref[1] = payb_ref[dz]
    row = lax.broadcasted_iota(jnp.int32, (ROWS, CAP), 0)
    slot = lax.broadcasted_iota(jnp.int32, (ROWS, CAP), 1)
    total = jnp.zeros((ROWS, D), F32)
    for k in range(4):
        hits = []
        for p in range(4 * k, 4 * k + 4):
            hit = (row == rows_ref[p : p + 1, :]) & (slot < counts_ref[p])
            hits.append(jnp.where(hit, 1.0, 0.0).astype(BF16))
        part = jnp.concatenate([back_ref[p] for p in range(4 * k, 4 * k + 4)], axis=0)
        total = total + dot(jnp.concatenate(hits, axis=1), part)
    out_ref[...] = total
    x = x_ref[...].astype(F32)
    scale = lax.rsqrt(jnp.mean(x * x, axis=-1, keepdims=True) + EPS)
    gain_grad = jnp.sum(total * (x * scale), axis=0, keepdims=True)
    gain_grad_ref[...] = jnp.zeros((8, 128), F32)
    for k in range(4):
        gain_grad_ref[k : k + 1, :] = gain_grad[:, k * 128 : (k + 1) * 128]


def rows_body(
    r0_ref, r1_ref, r2_ref, r3_ref, halo_ref, base_ref, x_ref,
    gain_ref, grad_ref, wq_ref, wk_ref, wv_ref, wo_ref,
    out_ref, feature_ref, dq_ref, dk_ref, dv_ref, at_ref, heads_ref,
):
    left = lax.broadcasted_iota(jnp.int32, (ROWS, 128), 1) < HEAD
    z, core = position()
    for dz, r_ref in enumerate((r0_ref, r1_ref, r2_ref, r3_ref)):
        chip = (z + dz) & 3
        heads_ref[core * 4 + chip] = r_ref[0]
        heads_ref[(1 - core) * 4 + chip] = r_ref[1]
    for m in range(4):
        low, high = heads_ref[2 * m].astype(F32), heads_ref[2 * m + 1].astype(F32)
        low0, low1 = low[:, 0:128], low[:, 128:256]
        high0, high1 = high[:, 0:128], high[:, 128:256]
        dq_ref[m] = jnp.where(left, low0, pltpu.roll(high0, HEAD, 1)).astype(BF16)
        dk_ref[m] = jnp.where(left, pltpu.roll(low0, HEAD, 1), high0).astype(BF16)
        dv_ref[m] = jnp.where(left, low1, pltpu.roll(high1, HEAD, 1)).astype(BF16)
        at_ref[m] = jnp.where(left, pltpu.roll(low1, HEAD, 1), high1).astype(BF16)

    def whole(ref):
        return jnp.concatenate([ref[m] for m in range(4)], axis=1)

    out_ref[...] = (base_ref[...] + dot(whole(at_ref), wo_ref[...])).astype(BF16)
    dnormed = dot(whole(dq_ref), wq_ref[...], NT) + dot(whole(dk_ref), wk_ref[...], NT)
    dnormed = dnormed + dot(whole(dv_ref), wv_ref[...], NT) + halo_ref[...]
    x = x_ref[...].astype(F32)
    scale = lax.rsqrt(jnp.mean(x * x, axis=-1, keepdims=True) + EPS)
    scaled = dnormed * gain_ref[...]
    inner = jnp.mean(scaled * x, axis=-1, keepdims=True)
    dx = scale * scaled - x * (scale * scale * scale * inner)
    feature_ref[...] = (grad_ref[...].astype(F32) + dx).astype(BF16)


def half_body(core, in_ref, out_hbm, tall_ref, wide_ref, sems):
    z, _ = position()
    first = pl.multiple_of(core * 256, 256)
    copies = [
        pltpu.make_async_copy(tall_ref.at[t], out_hbm.at[t, :, pl.ds(first, 256)], sems.at[t]) for t in range(3)
    ] + [
        pltpu.make_async_copy(wide_ref.at[t], out_hbm.at[3 + t, pl.ds(first, 256), :], sems.at[3 + t]) for t in range(2)
    ]

    def piece(chip, p):
        start = pl.multiple_of(((z - chip) & 3) * 64, 64)
        return in_ref[p, pl.ds(start, 64), :].astype(F32)

    for t in range(3):
        for b in range(4):
            part = jnp.concatenate([piece(chip, t * 4 + b) for chip in range(4)], axis=0)
            tall_ref[t, b * 128 : (b + 1) * 128, :] = jnp.transpose(part)
        copies[t].start()
    for b in range(4):
        for chip in range(4):
            wide_ref[0, chip * 64 : (chip + 1) * 64, b * 128 : (b + 1) * 128] = piece(chip, 12 + b)
    copies[3].start()
    for p in range(DOM):
        for b in range(4):
            part = in_ref[p, 256 + b * 16 : 272 + b * 16, :]
            wide_ref[1, p * 16 : (p + 1) * 16, b * 128 : (b + 1) * 128] = part.astype(F32)
    copies[4].start()
    for copy in copies:
        copy.wait()


def tails_of(ref):
    tails = [ref[p, 320:SPREAD, :].astype(F32) for p in range(DOM)]
    return [tail[0:8] + tail[8:16] for tail in tails]


def first_half_body(mine_ref, out_hbm, tall_ref, wide_ref, sems):
    half_body(position()[1], mine_ref, out_hbm, tall_ref, wide_ref, sems)


def second_half_body(before_hbm, mine_ref, other_ref, gain_in_ref, out_hbm, gain_ref, tall_ref, wide_ref, sems):
    gain = jnp.zeros((8, 128), F32)
    mine, through = tails_of(mine_ref), tails_of(other_ref)
    for p in range(DOM):
        gain = gain + mine[p]
        through[p] = through[p] + mine[p]
    for b in range(4):
        part = (through[b] + through[4 + b] + through[8 + b])[4:5]
        lanes = slice(b * 128, (b + 1) * 128)
        gain_ref[:, lanes] = gain[b : b + 1] + part / gain_in_ref[:, lanes]
    half_body(1 - position()[1], other_ref, out_hbm, tall_ref, wide_ref, sems)


def in_halves(mine, other, gain_row):
    vmem, hbm = pl.BlockSpec(memory_space=pltpu.VMEM), pl.BlockSpec(memory_space=pltpu.HBM)
    scratch = [pltpu.VMEM((3, D, 256), F32), pltpu.VMEM((2, 256, D), F32), pltpu.SemaphoreType.DMA((5,))]
    half = pl.pallas_call(
        first_half_body, out_shape=shape((5, D, D), F32), in_specs=[vmem], out_specs=hbm, scratch_shapes=scratch,
        cost_estimate=pl.CostEstimate(flops=int(3e9), transcendentals=0, bytes_accessed=1 << 20),
    )(mine)
    return pl.pallas_call(
        second_half_body,
        out_shape=(shape((5, D, D), F32), shape((1, D), F32)),
        in_specs=[hbm, vmem, vmem, vmem],
        out_specs=(hbm, vmem),
        input_output_aliases={0: 0},
        scratch_shapes=scratch,
    )(half, mine, other, gain_row)


def chip_shift(step, swap):
    return [(z * 2 + c, ((z + step) % 4) * 2 + (c ^ swap)) for z in range(4) for c in range(2)]


def along_chips(array, step):
    return lax.ppermute(array, "blk", chip_shift(step, 0))


def other_core(array):
    return lax.ppermute(array, "blk", chip_shift(0, 1))


def to_dom_peers(array):
    return lax.all_to_all(array, "dom", split_axis=0, concat_axis=0, tiled=True)


def local(
    x, gain, wq, wk, wv, wo, wm, cluster, pattern, send_rows, send_counts, edge_src, edge_dst, out_grad
):
    gain_row = gain.reshape(1, D)
    pay, outgoing = call(
        norm_body,
        (shape((PAY, D), BF16), shape((DOM, CAP, D), BF16)),
        (pattern, send_counts, x, gain_row, cluster.reshape(1, ROWS), out_grad, send_rows),
        scalars=2,
        micros=4,
    )
    incoming = to_dom_peers(outgoing)
    near, far = along_chips(pay, 1), along_chips(pay, 3)

    counts_t, degree, slot_grads, wqkv, wo_head = call(
        edges_body,
        (
            shape((1024, 512), BF16), shape((ROWS, 128), F32), shape((DOM, CAP, D), BF16),
            shape((192, D), BF16), shape((HEAD, D), BF16),
        ),
        (edge_src.reshape(32, 128), edge_dst.reshape(32, 128), out_grad, wm, wq, wk, wv, wo),
        scratch=[pltpu.VMEM((512, 1024), F32)],
        micros=10,
    )
    near, far, degree = lax.optimization_barrier((near, far, degree))
    pays = [pay, near, along_chips(near[0:ROWS], 1), along_chips(far[ROWS:PAY], 3), far]
    pays = pays + [other_core(part) for part in pays]
    slot_grads = lax.optimization_barrier((incoming, slot_grads))[1]
    back = to_dom_peers(slot_grads)

    base, mine, other = call(
        mean_body,
        (shape((ROWS, D), F32), shape((DOM, 64, 128), BF16), shape((DOM, 64, 128), BF16)),
        (counts_t, degree, incoming, x, out_grad, wm),
        micros=4,
    )

    pay_a, pay_b, chunks = call(
        attention_body,
        (*[shape((4, ROWS, 256), BF16)] * 2, shape((DOM, 128, 128), BF16)),
        (*pays, wqkv, wo_head, mine, other_core(other)),
        scratch=[
            pltpu.VMEM((BLK, 128, ROWS), F32),
            pltpu.VMEM((BLK, 8, ROWS), F32),
            pltpu.VMEM((BLK, 128, ROWS), BF16),
            pltpu.VMEM((BLK, HEAD, ROWS), BF16),
            pltpu.VMEM((BLK, ROWS, 128), BF16),
            pltpu.VMEM((BLK, ROWS, 128), BF16),
            pltpu.VMEM((BLK, 80, ROWS), BF16),
            pltpu.VMEM((BLK, BLK, ROWS, ROWS), BF16),
            pltpu.VMEM((BLK, HEAD, ROWS), F32),
            pltpu.VMEM((BLK, HEAD, ROWS), F32),
            pltpu.VMEM((BLK, HEAD, ROWS), F32),
            pltpu.VMEM((BLK, HEAD, ROWS), BF16),
            pltpu.VMEM((BLK, HEAD, ROWS), F32),
            pltpu.VMEM((BLK, BLK, ROWS, ROWS), BF16),
            pltpu.VMEM((BLK, ROWS, 128), BF16),
            pltpu.VMEM((BLK, ROWS, 128), BF16),
        ],
        micros=12,
    )
    chunks = lax.optimization_barrier((chunks, back))[0]
    chunks = to_dom_peers(chunks)
    halo, gain_part, *results = call(
        halo_body,
        (shape((ROWS, D), F32), shape((8, 128), F32), *[shape((2, ROWS, 256), BF16)] * 4),
        (send_counts, back, send_rows, x, pay_a, other_core(pay_b)),
        scalars=1,
        micros=3,
    )
    chunk = call(
        chunk_sum_body,
        shape((CHUNK, 128), BF16),
        (chunks, gain_part, other_core(gain_part), wqkv),
        scratch=[pltpu.VMEM((8, 128), F32)],
        micros=1,
    )
    chunk_parts = [chunk] + [along_chips(chunk, step) for step in (1, 2, 3)]
    spread = call(
        spread_body, shape((DOM, SPREAD, 128), BF16), chunk_parts, scratch=[pltpu.VMEM((4, 80, 128), F32)], micros=1
    )
    spread, *results = lax.optimization_barrier((spread, *results))
    gathered = to_dom_peers(spread)
    results = [results[0]] + [along_chips(results[dz], -dz) for dz in (1, 2, 3)]
    layer_out, feature_grad = call(
        rows_body,
        (shape((ROWS, D), BF16), shape((ROWS, D), BF16)),
        (*results, halo, base, x, gain_row, out_grad, wq, wk, wv, wo),
        scratch=[pltpu.VMEM((4, ROWS, 128), BF16)] * 4 + [pltpu.VMEM((BLK, ROWS, 256), BF16)],
        micros=2,
    )
    gathered, layer_out, feature_grad = lax.optimization_barrier((gathered, layer_out, feature_grad))
    gathered_other = other_core(gathered)
    weight_grads, gain_grad = in_halves(gathered, gathered_other, gain_row)
    return layer_out, feature_grad, weight_grads, gain_grad.reshape(D)


def solution(mesh):
    both = ("dom", "blk")
    placed = (
        P(both, None), P(), P(), P(), P(), P(), P(), P(both), P(both, None), P(both, None), P(both), P(both), P(both),
        P(both, None),
    )
    return jax.shard_map(
        local,
        mesh=mesh,
        in_specs=placed,
        out_specs=(P(both, None), P(both, None), P(), P()),
        check_vma=False,
    )
```

```python
import math

import jax
import jax.numpy as jnp
from jax import lax
from jax.experimental import pallas as pl
from jax.experimental.pallas import tpu as pltpu
from jax.sharding import PartitionSpec as P

F32 = jnp.float32
BF16 = jnp.bfloat16
EPS = 1e-06
D = 512
ROWS = 256
HEAD = 64
BLK = 8
DOM = 16
CAP = 128
EDGES = 4096
PAY = 2 * ROWS + 16
LOG2E = math.log2(math.e)
SCORE_MUL = LOG2E / 8.0
SCORE_SUB = (8.0 + 256.0) * LOG2E
CHUNK = 64 + 64 + 16
SPREAD = 4 * 64 + 64 + 16

NT = (((1,), (1,)), ((), ()))
NN = (((1,), (0,)), ((), ()))


def dot(a, b, dims=NN):
    return lax.dot_general(a, b, dims, preferred_element_type=F32)


def call(body, out_shape, operands, scratch=(), scalars=0, micros=2, left=()):
    specs = [pl.BlockSpec(memory_space=pltpu.SMEM)] * scalars
    specs += [pl.BlockSpec(memory_space=pltpu.VMEM)] * (len(operands) - scalars)
    for at in left:
        specs[at] = pl.BlockSpec(memory_space=pltpu.HBM)
    return pl.pallas_call(
        body,
        out_shape=out_shape,
        in_specs=specs,
        out_specs=jax.tree.map(lambda _: pl.BlockSpec(memory_space=pltpu.VMEM), out_shape),
        scratch_shapes=list(scratch),
        cost_estimate=pl.CostEstimate(flops=int(micros * 1e9), transcendentals=0, bytes_accessed=1 << 20),
    )(*operands)


def shape(dims, dtype):
    return jax.ShapeDtypeStruct(dims, dtype)


def dom_position():
    me = lax.axis_index("dom").astype(jnp.int32)
    return lax.shift_right_logical(me, 2), me & 3


def position():
    me = lax.axis_index("blk").astype(jnp.int32)
    return lax.shift_right_logical(me, 1), me & 1


def norm_body(pattern_ref, counts_ref, x_ref, gain_ref, label_ref, grad_ref, rows_ref, out_ref, slots_ref):
    x = x_ref[...].astype(F32)
    scale = lax.rsqrt(jnp.mean(x * x, axis=-1, keepdims=True) + EPS)
    normed = (x * scale * gain_ref[...]).astype(BF16)
    out_ref[0:ROWS, :] = normed
    out_ref[ROWS : 2 * ROWS, :] = grad_ref[...]
    row = lax.broadcasted_iota(jnp.int32, (16, ROWS), 0)
    lane = lax.broadcasted_iota(jnp.int32, (16, ROWS), 1)
    tail = jnp.where(row == 0, label_ref[...].astype(F32), 0.0)
    for b in range(BLK):
        flag = jnp.where(pattern_ref[0, b] == 1, 1.0, 0.0)
        tail = jnp.where((row == 1 + b) & (lane >= 0), flag, tail)
    out_ref[2 * ROWS : PAY, 0:ROWS] = tail.astype(BF16)
    out_ref[2 * ROWS : PAY, ROWS:D] = jnp.zeros((16, D - ROWS), BF16)
    columns = jnp.transpose(rows_ref[...].astype(F32))
    lane = lax.broadcasted_iota(jnp.int32, (CAP, ROWS), 1).astype(F32)
    slot = lax.broadcasted_iota(jnp.int32, (CAP, ROWS), 0)
    for p in range(DOM):
        hit = (lane == columns[:, p : p + 1]) & (slot < counts_ref[p])
        slots_ref[p] = dot(jnp.where(hit, 1.0, 0.0).astype(BF16), normed).astype(BF16)


E_ROWS = 4


def edges_body(
    src_ref, dst_ref, grad_ref, w_ref, wq_ref, wk_ref, wv_ref, wo_ref,
    counts_t_ref, degree_ref, slots_ref, wqkv_ref, wo_head_ref, acc_ref,
):
    z, core = position()
    head = core * 4 + z
    for m in range(4):
        @pl.when(head >> 1 == m)
        def _():
            for k, ref in enumerate((wq_ref, wk_ref, wv_ref)):
                pair = jnp.transpose(ref[:, m * 128 : (m + 1) * 128].astype(F32))
                picked = jnp.where(head & 1 == 0, pair[0:HEAD], pair[HEAD:128])
                wqkv_ref[k * HEAD : (k + 1) * HEAD, :] = picked.astype(BF16)
            for c in range(2):
                @pl.when(head & 1 == c)
                def _():
                    wo_head_ref[...] = wo_ref[m * 128 + c * HEAD : m * 128 + (c + 1) * HEAD, :]

    low_row = lax.broadcasted_iota(jnp.int32, (512, E_ROWS * 128), 0)
    high_row = lax.broadcasted_iota(jnp.int32, (1024, E_ROWS * 128), 0)
    for step in range(EDGES // (E_ROWS * 128)):
        rows = [step * E_ROWS + k for k in range(E_ROWS)]
        src = jnp.concatenate([src_ref[k : k + 1, :] for k in rows], axis=1)
        dst = jnp.concatenate([dst_ref[k : k + 1, :] for k in rows], axis=1)
        low = jnp.where(low_row == (src & 511), 1.0, 0.0).astype(BF16)
        high = jnp.where(high_row == ((src >> 9) * 256 + dst), 1.0, 0.0).astype(BF16)
        part = dot(low, high, NT)
        if step == 0:
            acc_ref[...] = part
        else:
            acc_ref[...] += part
    counts = acc_ref[...]
    per_row = jnp.sum(counts, axis=0, keepdims=True)
    per_row = per_row[:, 0:256] + per_row[:, 256:512] + per_row[:, 512:768] + per_row[:, 768:1024]
    degree = jnp.transpose(jnp.broadcast_to(jnp.maximum(per_row, 1.0), (128, ROWS)))
    degree_ref[...] = degree
    counts_t_ref[...] = jnp.transpose(counts).astype(BF16)
    counts = counts.astype(BF16)
    inverse = 1.0 / degree[:, 0:1]
    message = (dot(grad_ref[...], w_ref[...], NT) * inverse).astype(BF16)
    for high in range(4):
        part = dot(counts[:, high * 256 : (high + 1) * 256], message).astype(BF16)
        for k in range(4):
            slots_ref[high * 4 + k] = part[k * CAP : (k + 1) * CAP, :]


def mean_body(counts_t_ref, degree_ref, table_ref, x_ref, grad_ref, w_ref, base_ref, mine_ref, other_ref):
    total = jnp.zeros((ROWS, D), F32)
    for high in range(4):
        table = jnp.concatenate([table_ref[high * 4 + k] for k in range(4)], axis=0)
        total = total + dot(counts_t_ref[high * 256 : (high + 1) * 256, :], table)
    mean_rows = (total / degree_ref[:, 0:1]).astype(BF16)
    base_ref[...] = x_ref[...].astype(F32) + dot(mean_rows, w_ref[...])
    dw = dot(jnp.transpose(mean_rows.astype(F32)).astype(BF16), grad_ref[...]).astype(BF16)
    z, core = position()
    for half in range(2):
        def fill(ref):
            for p in range(DOM):
                top = half * 256 + p * 16
                for b in range(4):
                    ref[p, b * 16 : (b + 1) * 16, :] = dw[top : top + 16, b * 128 : (b + 1) * 128]

        @pl.when(core == half)
        def _():
            fill(mine_ref)

        @pl.when(core != half)
        def _():
            fill(other_ref)


def attention_body(
    p0_ref, p1_ref, t2_ref, b2_ref, p3_ref, p4_ref, p5_ref, t6_ref, b6_ref, p7_ref, wqkv_ref, wo_ref, mine_ref, other_ref,
    paya_ref, payb_ref, chunks_ref,
    y_ref, s_ref, qt_ref, kt_ref, k_ref, v_ref, vt_ref, w_ref, dq_ref, dk_ref, dv_ref, at_ref, ga_ref, sl_ref, qr_ref, gr_ref,
):
    pays = (p0_ref, p1_ref, (t2_ref, b2_ref), p3_ref, p4_ref, p5_ref, (t6_ref, b6_ref), p7_ref)

    def normed_of(pay):
        return pay[0][...] if isinstance(pay, tuple) else pay[0:ROWS, :]

    def grads_of(pay):
        return pay[1][0:ROWS, :] if isinstance(pay, tuple) else pay[ROWS : 2 * ROWS, :]

    def tail_of(pay):
        return pay[1][ROWS : PAY - ROWS, 0:ROWS] if isinstance(pay, tuple) else pay[2 * ROWS : PAY, 0:ROWS]

    outs = (paya_ref, payb_ref)
    z, core = position()
    row = lax.broadcasted_iota(jnp.int32, (HEAD, ROWS), 0)
    number = row.astype(F32)

    def head_scale(part):
        return lax.rsqrt(jnp.sum(part * part, axis=0, keepdims=True) * (1.0 / HEAD) + EPS)

    for r in range(BLK):
        pay = pays[r]
        projected = dot(wqkv_ref[...], normed_of(pay), NT)
        query, key, value = projected[0:HEAD], projected[HEAD:128], projected[128:192]
        scale_q, scale_k = head_scale(query), head_scale(key)
        query, key = query * scale_q, key * scale_k
        y_ref[r, 0:HEAD] = query
        y_ref[r, HEAD:128] = key
        s_ref[r, 0:1] = scale_q
        s_ref[r, 1:2] = scale_k
        tail = tail_of(pay).astype(F32)
        same = jnp.where(number == tail[0:1], 32.0, 0.0)
        sender = ((z - (r & 3)) & 3) * 2 + (core ^ (r >> 2))
        wanted = jnp.concatenate([jnp.zeros((16, ROWS), F32), tail[1:9] * 32.0, jnp.zeros((40, ROWS), F32)], axis=0)
        owner = jnp.where(row == 16 + sender, 32.0, 0.0)
        qt_ref[r] = jnp.concatenate([query, same + wanted], axis=0).astype(BF16)
        key = jnp.concatenate([key, same + owner], axis=0)
        kt_ref[r] = key[0:HEAD].astype(BF16)
        k_ref[r] = jnp.transpose(key).astype(BF16)
        value = jnp.concatenate([value, jnp.where(row < 2, 1.0, 0.0)], axis=0)
        vt_ref[r] = value[0:80].astype(BF16)
        v_ref[r] = jnp.transpose(value).astype(BF16)
        ga_ref[r] = dot(wo_ref[...], grads_of(pay), NT)
        qr_ref[r] = jnp.transpose(qt_ref[r].astype(F32)).astype(BF16)

    keys_t = jnp.concatenate([kt_ref[j] for j in range(BLK)], axis=1)
    values_t = jnp.concatenate([vt_ref[j] for j in range(BLK)], axis=1)

    def query_block(i, carry):
        query = qt_ref[i]
        for j in range(BLK):
            scores = dot(k_ref[j], query)
            w_ref[i, j] = jnp.exp2(scores * SCORE_MUL - SCORE_SUB).astype(BF16)
        numer = dot(values_t, w_ref[i].reshape(BLK * ROWS, ROWS))
        inverse = 1.0 / numer[HEAD : HEAD + 1]
        attn = (numer[0:HEAD] * inverse).astype(BF16)
        at_ref[i] = attn
        grad_attn = ga_ref[i]
        minus = jnp.sum(grad_attn * attn.astype(F32), axis=0, keepdims=True) * (-inverse)
        coarse = minus.astype(BF16).astype(F32)
        extra = jnp.where(row == 0, coarse, jnp.where(row == 1, minus - coarse, 0.0))
        grad = jnp.concatenate([grad_attn * inverse, extra], axis=0).astype(BF16)
        gr_ref[i] = jnp.transpose(grad.astype(F32)).astype(BF16)
        for j in range(BLK):
            sl_ref[i, j] = (w_ref[i, j].astype(F32) * dot(v_ref[j], grad)).astype(BF16)
        dq_ref[i] = dot(keys_t, sl_ref[i].reshape(BLK * ROWS, ROWS))
        return carry

    lax.fori_loop(0, BLK, query_block, 0)

    queries = jnp.concatenate([qr_ref[i] for i in range(BLK)], axis=0)
    grads = jnp.concatenate([gr_ref[i] for i in range(BLK)], axis=0)

    def key_block(j, carry):
        slopes = jnp.concatenate([sl_ref[i, j] for i in range(BLK)], axis=1)
        dk_ref[j] = jnp.transpose(dot(slopes, queries))[0:HEAD]
        weights = jnp.concatenate([w_ref[i, j] for i in range(BLK)], axis=1)
        dv_ref[j] = jnp.transpose(dot(weights, grads))[0:HEAD]
        return carry

    lax.fori_loop(0, BLK, key_block, 0)

    dw = jnp.zeros((192, D), F32)
    dwo = jnp.zeros((HEAD, D), F32)
    for r in range(BLK):
        pay = pays[r]

        def pull(grad, y, scale):
            grad = grad * (8.0 / HEAD)
            return scale * (grad - y * (jnp.sum(y * grad, axis=0, keepdims=True) * (1.0 / HEAD)))

        dquery = pull(dq_ref[r], y_ref[r, 0:HEAD], s_ref[r, 0:1])
        dkey = pull(dk_ref[r], y_ref[r, HEAD:128], s_ref[r, 1:2])
        first = jnp.concatenate([dquery, dkey], axis=0)
        second = jnp.concatenate([dv_ref[r], at_ref[r].astype(F32)], axis=0)
        outs[r >> 2][r & 3, :, 0:128] = jnp.transpose(first).astype(BF16)
        outs[r >> 2][r & 3, :, 128:256] = jnp.transpose(second).astype(BF16)
        left = jnp.concatenate([first, second[0:HEAD]], axis=0).astype(BF16)
        dw = dw + dot(left, normed_of(pay))
        dwo = dwo + dot(at_ref[r], grads_of(pay))
    dw = jnp.concatenate([dw, dwo], axis=0).astype(BF16)
    for a in range(4):
        for b in range(4):
            p = a * 4 + b
            chunks_ref[p, 0:64, :] = dw[a * 64 : (a + 1) * 64, b * 128 : (b + 1) * 128]
            chunks_ref[p, 64:128, :] = (mine_ref[p].astype(F32) + other_ref[p].astype(F32)).astype(BF16)


def chunk_sum_body(in_ref, g0_ref, g1_ref, wqkv_ref, out_ref, extra_ref):
    total = in_ref[0].astype(F32)
    for p in range(1, DOM):
        total = total + in_ref[p].astype(F32)
    out_ref[0:128, :] = total.astype(BF16)
    z, core = position()
    kind, lanes = dom_position()
    one, two = g0_ref[...], g1_ref[...]
    extra_ref[...] = jnp.where(core == 0, one, two) + jnp.where(core == 0, two, one)
    for b in range(4):
        @pl.when((kind < 3) & (lanes == b))
        def _():
            start = pl.multiple_of(jnp.minimum(kind, 2) * HEAD, HEAD)
            weights = wqkv_ref[pl.ds(start, HEAD), b * 128 : (b + 1) * 128].astype(F32)
            extra_ref[4:5, :] = jnp.sum(weights * total[0:HEAD], axis=0, keepdims=True)
    extra = extra_ref[...]
    coarse = extra.astype(BF16).astype(F32)
    out_ref[128:CHUNK, :] = jnp.concatenate([coarse, extra - coarse], axis=0).astype(BF16)


def spread_body(c0_ref, c1_ref, c2_ref, c3_ref, out_ref, parts_ref):
    z, core = position()
    for dz, c_ref in enumerate((c0_ref, c1_ref, c2_ref, c3_ref)):
        parts_ref[dz] = c_ref[64:CHUNK, :].astype(F32)
    total = jnp.zeros((80, 128), F32)
    for chip in range(4):
        total = total + parts_ref[(z - chip) & 3]
    gain = total[64:72] + total[72:80]
    coarse = gain.astype(BF16).astype(F32)
    tail = jnp.concatenate([total[0:64], coarse, gain - coarse], axis=0).astype(BF16)
    whole = jnp.concatenate([c_ref[0:64, :] for c_ref in (c0_ref, c1_ref, c2_ref, c3_ref)] + [tail], axis=0)
    for p in range(DOM):
        out_ref[p] = whole


def halo_body(
    counts_ref, back_ref, rows_ref, x_ref, paya_ref, payb_ref,
    out_ref, gain_grad_ref, r0_ref, r1_ref, r2_ref, r3_ref,
):
    for dz, r_ref in enumerate((r0_ref, r1_ref, r2_ref, r3_ref)):
        r_ref[0] = paya_ref[dz]
        r_ref[1] = payb_ref[dz]
    row = lax.broadcasted_iota(jnp.int32, (ROWS, CAP), 0)
    slot = lax.broadcasted_iota(jnp.int32, (ROWS, CAP), 1)
    total = jnp.zeros((ROWS, D), F32)
    for k in range(4):
        hits = []
        for p in range(4 * k, 4 * k + 4):
            hit = (row == rows_ref[p : p + 1, :]) & (slot < counts_ref[p])
            hits.append(jnp.where(hit, 1.0, 0.0).astype(BF16))
        part = jnp.concatenate([back_ref[p] for p in range(4 * k, 4 * k + 4)], axis=0)
        total = total + dot(jnp.concatenate(hits, axis=1), part)
    out_ref[...] = total
    x = x_ref[...].astype(F32)
    scale = lax.rsqrt(jnp.mean(x * x, axis=-1, keepdims=True) + EPS)
    gain_grad = jnp.sum(total * (x * scale), axis=0, keepdims=True)
    gain_grad_ref[...] = jnp.zeros((8, 128), F32)
    for k in range(4):
        gain_grad_ref[k : k + 1, :] = gain_grad[:, k * 128 : (k + 1) * 128]


def rows_body(
    r0_ref, r1_ref, r2_ref, r3_ref, halo_ref, base_ref, x_ref,
    gain_ref, grad_ref, wq_ref, wk_ref, wv_ref, wo_ref,
    out_ref, feature_ref, dq_ref, dk_ref, dv_ref, at_ref, heads_ref,
):
    left = lax.broadcasted_iota(jnp.int32, (ROWS, 128), 1) < HEAD
    z, core = position()
    for dz, r_ref in enumerate((r0_ref, r1_ref, r2_ref, r3_ref)):
        chip = (z + dz) & 3
        heads_ref[core * 4 + chip] = r_ref[0]
        heads_ref[(1 - core) * 4 + chip] = r_ref[1]
    for m in range(4):
        low, high = heads_ref[2 * m].astype(F32), heads_ref[2 * m + 1].astype(F32)
        low0, low1 = low[:, 0:128], low[:, 128:256]
        high0, high1 = high[:, 0:128], high[:, 128:256]
        dq_ref[m] = jnp.where(left, low0, pltpu.roll(high0, HEAD, 1)).astype(BF16)
        dk_ref[m] = jnp.where(left, pltpu.roll(low0, HEAD, 1), high0).astype(BF16)
        dv_ref[m] = jnp.where(left, low1, pltpu.roll(high1, HEAD, 1)).astype(BF16)
        at_ref[m] = jnp.where(left, pltpu.roll(low1, HEAD, 1), high1).astype(BF16)

    def whole(ref):
        return jnp.concatenate([ref[m] for m in range(4)], axis=1)

    out_ref[...] = (base_ref[...] + dot(whole(at_ref), wo_ref[...])).astype(BF16)
    dnormed = dot(whole(dq_ref), wq_ref[...], NT) + dot(whole(dk_ref), wk_ref[...], NT)
    dnormed = dnormed + dot(whole(dv_ref), wv_ref[...], NT) + halo_ref[...]
    x = x_ref[...].astype(F32)
    scale = lax.rsqrt(jnp.mean(x * x, axis=-1, keepdims=True) + EPS)
    scaled = dnormed * gain_ref[...]
    inner = jnp.mean(scaled * x, axis=-1, keepdims=True)
    dx = scale * scaled - x * (scale * scale * scale * inner)
    feature_ref[...] = (grad_ref[...].astype(F32) + dx).astype(BF16)


def half_body(core, in_ref, out_hbm, tall_ref, wide_ref, sems):
    z, _ = position()
    first = pl.multiple_of(core * 256, 256)
    copies = [
        pltpu.make_async_copy(tall_ref.at[t], out_hbm.at[t, :, pl.ds(first, 256)], sems.at[t]) for t in range(3)
    ] + [
        pltpu.make_async_copy(wide_ref.at[t], out_hbm.at[3 + t, pl.ds(first, 256), :], sems.at[3 + t]) for t in range(2)
    ]

    def piece(chip, p):
        start = pl.multiple_of(((z - chip) & 3) * 64, 64)
        return in_ref[p, pl.ds(start, 64), :].astype(F32)

    for t in range(3):
        for b in range(4):
            part = jnp.concatenate([piece(chip, t * 4 + b) for chip in range(4)], axis=0)
            tall_ref[t, b * 128 : (b + 1) * 128, :] = jnp.transpose(part)
        copies[t].start()
    for b in range(4):
        for chip in range(4):
            wide_ref[0, chip * 64 : (chip + 1) * 64, b * 128 : (b + 1) * 128] = piece(chip, 12 + b)
    copies[3].start()
    for p in range(DOM):
        for b in range(4):
            part = in_ref[p, 256 + b * 16 : 272 + b * 16, :]
            wide_ref[1, p * 16 : (p + 1) * 16, b * 128 : (b + 1) * 128] = part.astype(F32)
    copies[4].start()
    for copy in copies:
        copy.wait()


def tails_of(ref):
    tails = [ref[p, 320:SPREAD, :].astype(F32) for p in range(DOM)]
    return [tail[0:8] + tail[8:16] for tail in tails]


def through_of(tails):
    return [(tails[b] + tails[4 + b] + tails[8 + b])[4:5] for b in range(4)]


def first_half_body(mine_ref, out_hbm, gain_ref, tall_ref, wide_ref, sems):
    tails = tails_of(mine_ref)
    total = tails[0]
    for p in range(1, DOM):
        total = total + tails[p]
    gain_ref[0:4, :] = total[0:4]
    for b, part in enumerate(through_of(tails)):
        gain_ref[4 + b : 5 + b, :] = part
    half_body(position()[1], mine_ref, out_hbm, tall_ref, wide_ref, sems)


def second_half_body(before_hbm, mine_gain_ref, other_ref, gain_in_ref, out_hbm, gain_ref, tall_ref, wide_ref, sems):
    for b, part in enumerate(through_of(tails_of(other_ref))):
        lanes = slice(b * 128, (b + 1) * 128)
        part = (part + mine_gain_ref[4 + b : 5 + b, :]) / gain_in_ref[:, lanes]
        gain_ref[:, lanes] = mine_gain_ref[b : b + 1, :] + part
    half_body(1 - position()[1], other_ref, out_hbm, tall_ref, wide_ref, sems)


def in_halves(mine, other, gain_row):
    vmem, hbm = pl.BlockSpec(memory_space=pltpu.VMEM), pl.BlockSpec(memory_space=pltpu.HBM)
    scratch = [pltpu.VMEM((3, D, 256), F32), pltpu.VMEM((2, 256, D), F32), pltpu.SemaphoreType.DMA((5,))]
    half, mine_gain = pl.pallas_call(
        first_half_body,
        out_shape=(shape((5, D, D), F32), shape((8, 128), F32)),
        in_specs=[vmem],
        out_specs=(hbm, vmem),
        scratch_shapes=scratch,
        cost_estimate=pl.CostEstimate(flops=int(3e9), transcendentals=0, bytes_accessed=1 << 20),
    )(mine)
    return pl.pallas_call(
        second_half_body,
        out_shape=(shape((5, D, D), F32), shape((1, D), F32)),
        in_specs=[hbm, vmem, vmem, vmem],
        out_specs=(hbm, vmem),
        input_output_aliases={0: 0},
        scratch_shapes=scratch,
    )(half, mine_gain, other, gain_row)


def chip_shift(step, swap):
    return [(z * 2 + c, ((z + step) % 4) * 2 + (c ^ swap)) for z in range(4) for c in range(2)]


def along_chips(array, step):
    return lax.ppermute(array, "blk", chip_shift(step, 0))


def other_core(array):
    return lax.ppermute(array, "blk", chip_shift(0, 1))


def to_dom_peers(array):
    return lax.all_to_all(array, "dom", split_axis=0, concat_axis=0, tiled=True)


def local(
    x, gain, wq, wk, wv, wo, wm, cluster, pattern, send_rows, send_counts, edge_src, edge_dst, out_grad
):
    gain_row = gain.reshape(1, D)
    pay, outgoing = call(
        norm_body,
        (shape((PAY, D), BF16), shape((DOM, CAP, D), BF16)),
        (pattern, send_counts, x, gain_row, cluster.reshape(1, ROWS), out_grad, send_rows),
        scalars=2,
        micros=4,
    )
    incoming = to_dom_peers(outgoing)
    near, far = along_chips(pay, 1), along_chips(pay, 3)

    counts_t, degree, slot_grads, wqkv, wo_head = call(
        edges_body,
        (
            shape((1024, 512), BF16), shape((ROWS, 128), F32), shape((DOM, CAP, D), BF16),
            shape((192, D), BF16), shape((HEAD, D), BF16),
        ),
        (edge_src.reshape(32, 128), edge_dst.reshape(32, 128), out_grad, wm, wq, wk, wv, wo),
        scratch=[pltpu.VMEM((512, 1024), F32)],
        micros=10,
    )
    near, far, degree = lax.optimization_barrier((near, far, degree))
    pays = [pay, near, along_chips(near[0:ROWS], 1), along_chips(far[ROWS:PAY], 3), far]
    pays = pays + [other_core(part) for part in pays]
    slot_grads = lax.optimization_barrier((incoming, slot_grads))[1]
    back = to_dom_peers(slot_grads)

    base, mine, other = call(
        mean_body,
        (shape((ROWS, D), F32), shape((DOM, 64, 128), BF16), shape((DOM, 64, 128), BF16)),
        (counts_t, degree, incoming, x, out_grad, wm),
        micros=4,
    )

    pay_a, pay_b, chunks = call(
        attention_body,
        (*[shape((4, ROWS, 256), BF16)] * 2, shape((DOM, 128, 128), BF16)),
        (*pays, wqkv, wo_head, mine, other_core(other)),
        scratch=[
            pltpu.VMEM((BLK, 128, ROWS), F32),
            pltpu.VMEM((BLK, 8, ROWS), F32),
            pltpu.VMEM((BLK, 128, ROWS), BF16),
            pltpu.VMEM((BLK, HEAD, ROWS), BF16),
            pltpu.VMEM((BLK, ROWS, 128), BF16),
            pltpu.VMEM((BLK, ROWS, 128), BF16),
            pltpu.VMEM((BLK, 80, ROWS), BF16),
            pltpu.VMEM((BLK, BLK, ROWS, ROWS), BF16),
            pltpu.VMEM((BLK, HEAD, ROWS), F32),
            pltpu.VMEM((BLK, HEAD, ROWS), F32),
            pltpu.VMEM((BLK, HEAD, ROWS), F32),
            pltpu.VMEM((BLK, HEAD, ROWS), BF16),
            pltpu.VMEM((BLK, HEAD, ROWS), F32),
            pltpu.VMEM((BLK, BLK, ROWS, ROWS), BF16),
            pltpu.VMEM((BLK, ROWS, 128), BF16),
            pltpu.VMEM((BLK, ROWS, 128), BF16),
        ],
        micros=12,
    )
    chunks = lax.optimization_barrier((chunks, back))[0]
    chunks = to_dom_peers(chunks)
    halo, gain_part, *results = call(
        halo_body,
        (shape((ROWS, D), F32), shape((8, 128), F32), *[shape((2, ROWS, 256), BF16)] * 4),
        (send_counts, back, send_rows, x, pay_a, other_core(pay_b)),
        scalars=1,
        micros=3,
    )
    chunk = call(
        chunk_sum_body,
        shape((CHUNK, 128), BF16),
        (chunks, gain_part, other_core(gain_part), wqkv),
        scratch=[pltpu.VMEM((8, 128), F32)],
        micros=1,
    )
    chunk_parts = [chunk] + [along_chips(chunk, step) for step in (1, 2, 3)]
    spread = call(
        spread_body, shape((DOM, SPREAD, 128), BF16), chunk_parts, scratch=[pltpu.VMEM((4, 80, 128), F32)], micros=1
    )
    spread, *results = lax.optimization_barrier((spread, *results))
    gathered = to_dom_peers(spread)
    results = [results[0]] + [along_chips(results[dz], -dz) for dz in (1, 2, 3)]
    layer_out, feature_grad = call(
        rows_body,
        (shape((ROWS, D), BF16), shape((ROWS, D), BF16)),
        (*results, halo, base, x, gain_row, out_grad, wq, wk, wv, wo),
        scratch=[pltpu.VMEM((4, ROWS, 128), BF16)] * 4 + [pltpu.VMEM((BLK, ROWS, 256), BF16)],
        micros=2,
    )
    gathered, layer_out, feature_grad = lax.optimization_barrier((gathered, layer_out, feature_grad))
    gathered_other = other_core(gathered)
    weight_grads, gain_grad = in_halves(gathered, gathered_other, gain_row)
    return layer_out, feature_grad, weight_grads, gain_grad.reshape(D)


def solution(mesh):
    both = ("dom", "blk")
    placed = (
        P(both, None), P(), P(), P(), P(), P(), P(), P(both), P(both, None), P(both, None), P(both), P(both), P(both),
        P(both, None),
    )
    return jax.shard_map(
        local,
        mesh=mesh,
        in_specs=placed,
        out_specs=(P(both, None), P(both, None), P(), P()),
        check_vma=False,
    )
```

```python
import math

import jax
import jax.numpy as jnp
from jax import lax
from jax.experimental import pallas as pl
from jax.experimental.pallas import tpu as pltpu
from jax.sharding import PartitionSpec as P

F32 = jnp.float32
BF16 = jnp.bfloat16
EPS = 1e-06
D = 512
ROWS = 256
HEAD = 64
BLK = 8
DOM = 16
CAP = 128
EDGES = 4096
PAY = 2 * ROWS + 16
LOG2E = math.log2(math.e)
SCORE_MUL = LOG2E / 8.0
SCORE_SUB = (8.0 + 256.0) * LOG2E
CHUNK = 64 + 64 + 16
SPREAD = 4 * 64 + 64 + 16

NT = (((1,), (1,)), ((), ()))
NN = (((1,), (0,)), ((), ()))


def dot(a, b, dims=NN):
    return lax.dot_general(a, b, dims, preferred_element_type=F32)


def call(body, out_shape, operands, scratch=(), scalars=0, micros=2, left=()):
    specs = [pl.BlockSpec(memory_space=pltpu.SMEM)] * scalars
    specs += [pl.BlockSpec(memory_space=pltpu.VMEM)] * (len(operands) - scalars)
    for at in left:
        specs[at] = pl.BlockSpec(memory_space=pltpu.HBM)
    return pl.pallas_call(
        body,
        out_shape=out_shape,
        in_specs=specs,
        out_specs=jax.tree.map(lambda _: pl.BlockSpec(memory_space=pltpu.VMEM), out_shape),
        scratch_shapes=list(scratch),
        cost_estimate=pl.CostEstimate(flops=int(micros * 1e9), transcendentals=0, bytes_accessed=1 << 20),
    )(*operands)


def shape(dims, dtype):
    return jax.ShapeDtypeStruct(dims, dtype)


def dom_position():
    me = lax.axis_index("dom").astype(jnp.int32)
    return lax.shift_right_logical(me, 2), me & 3


def position():
    me = lax.axis_index("blk").astype(jnp.int32)
    return lax.shift_right_logical(me, 1), me & 1


def norm_body(pattern_ref, counts_ref, x_ref, gain_ref, label_ref, grad_ref, rows_ref, out_ref, slots_ref):
    x = x_ref[...].astype(F32)
    scale = lax.rsqrt(jnp.mean(x * x, axis=-1, keepdims=True) + EPS)
    normed = (x * scale * gain_ref[...]).astype(BF16)
    out_ref[0:ROWS, :] = normed
    out_ref[ROWS : 2 * ROWS, :] = grad_ref[...]
    row = lax.broadcasted_iota(jnp.int32, (16, ROWS), 0)
    lane = lax.broadcasted_iota(jnp.int32, (16, ROWS), 1)
    tail = jnp.where(row == 0, label_ref[...].astype(F32), 0.0)
    for b in range(BLK):
        flag = jnp.where(pattern_ref[0, b] == 1, 1.0, 0.0)
        tail = jnp.where((row == 1 + b) & (lane >= 0), flag, tail)
    out_ref[2 * ROWS : PAY, 0:ROWS] = tail.astype(BF16)
    out_ref[2 * ROWS : PAY, ROWS:D] = jnp.zeros((16, D - ROWS), BF16)
    columns = jnp.transpose(rows_ref[...].astype(F32))
    lane = lax.broadcasted_iota(jnp.int32, (CAP, ROWS), 1).astype(F32)
    slot = lax.broadcasted_iota(jnp.int32, (CAP, ROWS), 0)
    for p in range(DOM):
        hit = (lane == columns[:, p : p + 1]) & (slot < counts_ref[p])
        slots_ref[p] = dot(jnp.where(hit, 1.0, 0.0).astype(BF16), normed).astype(BF16)


E_ROWS = 4


def edges_body(
    src_ref, dst_ref, grad_ref, w_ref, wq_ref, wk_ref, wv_ref, wo_ref,
    counts_t_ref, degree_ref, slots_ref, wqkv_ref, wo_head_ref, acc_ref,
):
    z, core = position()
    head = core * 4 + z
    for m in range(4):
        @pl.when(head >> 1 == m)
        def _():
            for k, ref in enumerate((wq_ref, wk_ref, wv_ref)):
                pair = jnp.transpose(ref[:, m * 128 : (m + 1) * 128].astype(F32))
                picked = jnp.where(head & 1 == 0, pair[0:HEAD], pair[HEAD:128])
                wqkv_ref[k * HEAD : (k + 1) * HEAD, :] = picked.astype(BF16)
            for c in range(2):
                @pl.when(head & 1 == c)
                def _():
                    wo_head_ref[...] = wo_ref[m * 128 + c * HEAD : m * 128 + (c + 1) * HEAD, :]

    low_row = lax.broadcasted_iota(jnp.int32, (512, E_ROWS * 128), 0)
    high_row = lax.broadcasted_iota(jnp.int32, (1024, E_ROWS * 128), 0)
    for step in range(EDGES // (E_ROWS * 128)):
        rows = [step * E_ROWS + k for k in range(E_ROWS)]
        src = jnp.concatenate([src_ref[k : k + 1, :] for k in rows], axis=1)
        dst = jnp.concatenate([dst_ref[k : k + 1, :] for k in rows], axis=1)
        low = jnp.where(low_row == (src & 511), 1.0, 0.0).astype(BF16)
        high = jnp.where(high_row == ((src >> 9) * 256 + dst), 1.0, 0.0).astype(BF16)
        part = dot(low, high, NT)
        if step == 0:
            acc_ref[...] = part
        else:
            acc_ref[...] += part
    counts = acc_ref[...]
    per_row = jnp.sum(counts, axis=0, keepdims=True)
    per_row = per_row[:, 0:256] + per_row[:, 256:512] + per_row[:, 512:768] + per_row[:, 768:1024]
    degree = jnp.transpose(jnp.broadcast_to(jnp.maximum(per_row, 1.0), (128, ROWS)))
    degree_ref[...] = degree
    counts_t_ref[...] = jnp.transpose(counts).astype(BF16)
    counts = counts.astype(BF16)
    inverse = 1.0 / degree[:, 0:1]
    message = (dot(grad_ref[...], w_ref[...], NT) * inverse).astype(BF16)
    for high in range(4):
        part = dot(counts[:, high * 256 : (high + 1) * 256], message).astype(BF16)
        for k in range(4):
            slots_ref[high * 4 + k] = part[k * CAP : (k + 1) * CAP, :]


def mean_body(counts_t_ref, degree_ref, table_ref, x_ref, grad_ref, w_ref, base_ref, mine_ref, other_ref):
    total = jnp.zeros((ROWS, D), F32)
    for high in range(4):
        table = jnp.concatenate([table_ref[high * 4 + k] for k in range(4)], axis=0)
        total = total + dot(counts_t_ref[high * 256 : (high + 1) * 256, :], table)
    mean_rows = (total / degree_ref[:, 0:1]).astype(BF16)
    base_ref[...] = x_ref[...].astype(F32) + dot(mean_rows, w_ref[...])
    dw = dot(jnp.transpose(mean_rows.astype(F32)).astype(BF16), grad_ref[...]).astype(BF16)
    z, core = position()
    for half in range(2):
        def fill(ref):
            for p in range(DOM):
                top = half * 256 + p * 16
                for b in range(4):
                    ref[p, b * 16 : (b + 1) * 16, :] = dw[top : top + 16, b * 128 : (b + 1) * 128]

        @pl.when(core == half)
        def _():
            fill(mine_ref)

        @pl.when(core != half)
        def _():
            fill(other_ref)


def attention_body(
    p0_ref, p1_ref, t2_ref, b2_ref, p3_ref, p4_ref, p5_ref, t6_ref, b6_ref, p7_ref, wqkv_ref, wo_ref, mine_ref, other_ref,
    paya_ref, payb_ref, chunks_ref,
    y_ref, s_ref, qt_ref, kt_ref, k_ref, v_ref, vt_ref, w_ref, dq_ref, dk_ref, dv_ref, at_ref, ga_ref, sl_ref, qr_ref, gr_ref,
):
    pays = (p0_ref, p1_ref, (t2_ref, b2_ref), p3_ref, p4_ref, p5_ref, (t6_ref, b6_ref), p7_ref)

    def normed_of(pay):
        return pay[0][...] if isinstance(pay, tuple) else pay[0:ROWS, :]

    def grads_of(pay):
        return pay[1][0:ROWS, :] if isinstance(pay, tuple) else pay[ROWS : 2 * ROWS, :]

    def tail_of(pay):
        return pay[1][ROWS : PAY - ROWS, 0:ROWS] if isinstance(pay, tuple) else pay[2 * ROWS : PAY, 0:ROWS]

    outs = (paya_ref, payb_ref)
    z, core = position()
    row = lax.broadcasted_iota(jnp.int32, (HEAD, ROWS), 0)
    number = row.astype(F32)

    def head_scale(part):
        return lax.rsqrt(jnp.sum(part * part, axis=0, keepdims=True) * (1.0 / HEAD) + EPS)

    for r in range(BLK):
        pay = pays[r]
        projected = dot(wqkv_ref[...], normed_of(pay), NT)
        query, key, value = projected[0:HEAD], projected[HEAD:128], projected[128:192]
        scale_q, scale_k = head_scale(query), head_scale(key)
        query, key = query * scale_q, key * scale_k
        y_ref[r, 0:HEAD] = query
        y_ref[r, HEAD:128] = key
        s_ref[r, 0:1] = scale_q
        s_ref[r, 1:2] = scale_k
        tail = tail_of(pay).astype(F32)
        same = jnp.where(number == tail[0:1], 32.0, 0.0)
        sender = ((z - (r & 3)) & 3) * 2 + (core ^ (r >> 2))
        wanted = jnp.concatenate([jnp.zeros((16, ROWS), F32), tail[1:9] * 32.0, jnp.zeros((40, ROWS), F32)], axis=0)
        owner = jnp.where(row == 16 + sender, 32.0, 0.0)
        qt_ref[r] = jnp.concatenate([query, same + wanted], axis=0).astype(BF16)
        key = jnp.concatenate([key, same + owner], axis=0)
        kt_ref[r] = key[0:HEAD].astype(BF16)
        k_ref[r] = jnp.transpose(key).astype(BF16)
        value = jnp.concatenate([value, jnp.where(row < 2, 1.0, 0.0)], axis=0)
        vt_ref[r] = value[0:80].astype(BF16)
        v_ref[r] = jnp.transpose(value).astype(BF16)
        ga_ref[r] = dot(wo_ref[...], grads_of(pay), NT)
        qr_ref[r] = jnp.transpose(qt_ref[r].astype(F32)).astype(BF16)

    keys_t = jnp.concatenate([kt_ref[j] for j in range(BLK)], axis=1)
    values_t = jnp.concatenate([vt_ref[j] for j in range(BLK)], axis=1)

    def query_block(i, carry):
        query = qt_ref[i]
        for j in range(BLK):
            scores = dot(k_ref[j], query)
            w_ref[i, j] = jnp.exp2(scores * SCORE_MUL - SCORE_SUB).astype(BF16)
        numer = dot(values_t, w_ref[i].reshape(BLK * ROWS, ROWS))
        inverse = 1.0 / numer[HEAD : HEAD + 1]
        attn = (numer[0:HEAD] * inverse).astype(BF16)
        at_ref[i] = attn
        grad_attn = ga_ref[i]
        minus = jnp.sum(grad_attn * attn.astype(F32), axis=0, keepdims=True) * (-inverse)
        coarse = minus.astype(BF16).astype(F32)
        extra = jnp.where(row == 0, coarse, jnp.where(row == 1, minus - coarse, 0.0))
        grad = jnp.concatenate([grad_attn * inverse, extra], axis=0).astype(BF16)
        gr_ref[i] = jnp.transpose(grad.astype(F32)).astype(BF16)
        for j in range(BLK):
            sl_ref[i, j] = (w_ref[i, j].astype(F32) * dot(v_ref[j], grad)).astype(BF16)
        dq_ref[i] = dot(keys_t, sl_ref[i].reshape(BLK * ROWS, ROWS))
        return carry

    lax.fori_loop(0, BLK, query_block, 0)

    queries = jnp.concatenate([qr_ref[i] for i in range(BLK)], axis=0)
    grads = jnp.concatenate([gr_ref[i] for i in range(BLK)], axis=0)

    def key_block(j, carry):
        slopes = jnp.concatenate([sl_ref[i, j] for i in range(BLK)], axis=1)
        dk_ref[j] = jnp.transpose(dot(slopes, queries))[0:HEAD]
        weights = jnp.concatenate([w_ref[i, j] for i in range(BLK)], axis=1)
        dv_ref[j] = jnp.transpose(dot(weights, grads))[0:HEAD]
        return carry

    lax.fori_loop(0, BLK, key_block, 0)

    dw = jnp.zeros((192, D), F32)
    dwo = jnp.zeros((HEAD, D), F32)
    for r in range(BLK):
        pay = pays[r]

        def pull(grad, y, scale):
            grad = grad * (8.0 / HEAD)
            return scale * (grad - y * (jnp.sum(y * grad, axis=0, keepdims=True) * (1.0 / HEAD)))

        dquery = pull(dq_ref[r], y_ref[r, 0:HEAD], s_ref[r, 0:1])
        dkey = pull(dk_ref[r], y_ref[r, HEAD:128], s_ref[r, 1:2])
        first = jnp.concatenate([dquery, dkey], axis=0)
        second = jnp.concatenate([dv_ref[r], at_ref[r].astype(F32)], axis=0)
        outs[r >> 2][r & 3, :, 0:128] = jnp.transpose(first).astype(BF16)
        outs[r >> 2][r & 3, :, 128:256] = jnp.transpose(second).astype(BF16)
        left = jnp.concatenate([first, second[0:HEAD]], axis=0).astype(BF16)
        dw = dw + dot(left, normed_of(pay))
        dwo = dwo + dot(at_ref[r], grads_of(pay))
    dw = jnp.concatenate([dw, dwo], axis=0).astype(BF16)
    for a in range(4):
        for b in range(4):
            p = a * 4 + b
            chunks_ref[p, 0:64, :] = dw[a * 64 : (a + 1) * 64, b * 128 : (b + 1) * 128]
            chunks_ref[p, 64:128, :] = (mine_ref[p].astype(F32) + other_ref[p].astype(F32)).astype(BF16)


def chunk_sum_body(in_ref, g0_ref, g1_ref, wqkv_ref, out_ref, extra_ref):
    total = in_ref[0].astype(F32)
    for p in range(1, DOM):
        total = total + in_ref[p].astype(F32)
    out_ref[0:128, :] = total.astype(BF16)
    z, core = position()
    kind, lanes = dom_position()
    one, two = g0_ref[...], g1_ref[...]
    extra_ref[...] = jnp.where(core == 0, one, two) + jnp.where(core == 0, two, one)
    for b in range(4):
        @pl.when((kind < 3) & (lanes == b))
        def _():
            start = pl.multiple_of(jnp.minimum(kind, 2) * HEAD, HEAD)
            weights = wqkv_ref[pl.ds(start, HEAD), b * 128 : (b + 1) * 128].astype(F32)
            extra_ref[4:5, :] = jnp.sum(weights * total[0:HEAD], axis=0, keepdims=True)
    extra = extra_ref[...]
    coarse = extra.astype(BF16).astype(F32)
    out_ref[128:CHUNK, :] = jnp.concatenate([coarse, extra - coarse], axis=0).astype(BF16)


def spread_body(c0_ref, c1_ref, c2_ref, c3_ref, out_ref, parts_ref):
    z, core = position()
    for dz, c_ref in enumerate((c0_ref, c1_ref, c2_ref, c3_ref)):
        parts_ref[dz] = c_ref[64:CHUNK, :].astype(F32)
    total = jnp.zeros((80, 128), F32)
    for chip in range(4):
        total = total + parts_ref[(z - chip) & 3]
    gain = total[64:72] + total[72:80]
    coarse = gain.astype(BF16).astype(F32)
    tail = jnp.concatenate([total[0:64], coarse, gain - coarse], axis=0).astype(BF16)
    whole = jnp.concatenate([c_ref[0:64, :] for c_ref in (c0_ref, c1_ref, c2_ref, c3_ref)] + [tail], axis=0)
    for p in range(DOM):
        out_ref[p] = whole


def halo_body(
    counts_ref, back_ref, rows_ref, x_ref, paya_ref, payb_ref,
    out_ref, gain_grad_ref, r0_ref, r1_ref, r2_ref, r3_ref,
):
    for dz, r_ref in enumerate((r0_ref, r1_ref, r2_ref, r3_ref)):
        r_ref[0] = paya_ref[dz]
        r_ref[1] = payb_ref[dz]
    row = lax.broadcasted_iota(jnp.int32, (ROWS, CAP), 0)
    slot = lax.broadcasted_iota(jnp.int32, (ROWS, CAP), 1)
    total = jnp.zeros((ROWS, D), F32)
    for k in range(4):
        hits = []
        for p in range(4 * k, 4 * k + 4):
            hit = (row == rows_ref[p : p + 1, :]) & (slot < counts_ref[p])
            hits.append(jnp.where(hit, 1.0, 0.0).astype(BF16))
        part = jnp.concatenate([back_ref[p] for p in range(4 * k, 4 * k + 4)], axis=0)
        total = total + dot(jnp.concatenate(hits, axis=1), part)
    out_ref[...] = total
    x = x_ref[...].astype(F32)
    scale = lax.rsqrt(jnp.mean(x * x, axis=-1, keepdims=True) + EPS)
    gain_grad = jnp.sum(total * (x * scale), axis=0, keepdims=True)
    gain_grad_ref[...] = jnp.zeros((8, 128), F32)
    for k in range(4):
        gain_grad_ref[k : k + 1, :] = gain_grad[:, k * 128 : (k + 1) * 128]


def rows_body(
    r0_ref, r1_ref, r2_ref, r3_ref, halo_ref, base_ref, x_ref,
    gain_ref, grad_ref, wq_ref, wk_ref, wv_ref, wo_ref,
    out_ref, feature_ref, dq_ref, dk_ref, dv_ref, at_ref, heads_ref,
):
    left = lax.broadcasted_iota(jnp.int32, (ROWS, 128), 1) < HEAD
    z, core = position()
    for dz, r_ref in enumerate((r0_ref, r1_ref, r2_ref, r3_ref)):
        chip = (z + dz) & 3
        heads_ref[core * 4 + chip] = r_ref[0]
        heads_ref[(1 - core) * 4 + chip] = r_ref[1]
    for m in range(4):
        low, high = heads_ref[2 * m].astype(F32), heads_ref[2 * m + 1].astype(F32)
        low0, low1 = low[:, 0:128], low[:, 128:256]
        high0, high1 = high[:, 0:128], high[:, 128:256]
        dq_ref[m] = jnp.where(left, low0, pltpu.roll(high0, HEAD, 1)).astype(BF16)
        dk_ref[m] = jnp.where(left, pltpu.roll(low0, HEAD, 1), high0).astype(BF16)
        dv_ref[m] = jnp.where(left, low1, pltpu.roll(high1, HEAD, 1)).astype(BF16)
        at_ref[m] = jnp.where(left, pltpu.roll(low1, HEAD, 1), high1).astype(BF16)

    def whole(ref):
        return jnp.concatenate([ref[m] for m in range(4)], axis=1)

    out_ref[...] = (base_ref[...] + dot(whole(at_ref), wo_ref[...])).astype(BF16)
    dnormed = dot(whole(dq_ref), wq_ref[...], NT) + dot(whole(dk_ref), wk_ref[...], NT)
    dnormed = dnormed + dot(whole(dv_ref), wv_ref[...], NT) + halo_ref[...]
    x = x_ref[...].astype(F32)
    scale = lax.rsqrt(jnp.mean(x * x, axis=-1, keepdims=True) + EPS)
    scaled = dnormed * gain_ref[...]
    inner = jnp.mean(scaled * x, axis=-1, keepdims=True)
    dx = scale * scaled - x * (scale * scale * scale * inner)
    feature_ref[...] = (grad_ref[...].astype(F32) + dx).astype(BF16)


def half_body(core, in_ref, out_hbm, tall_ref, wide_ref, sems):
    z, _ = position()
    first = pl.multiple_of(core * 256, 256)
    copies = [
        pltpu.make_async_copy(tall_ref.at[t], out_hbm.at[t, :, pl.ds(first, 256)], sems.at[t]) for t in range(3)
    ] + [
        pltpu.make_async_copy(wide_ref.at[t], out_hbm.at[3 + t, pl.ds(first, 256), :], sems.at[3 + t]) for t in range(2)
    ]

    def piece(chip, p):
        start = pl.multiple_of(((z - chip) & 3) * 64, 64)
        return in_ref[p, pl.ds(start, 64), :].astype(F32)

    for t in range(3):
        for b in range(4):
            part = jnp.concatenate([piece(chip, t * 4 + b) for chip in range(4)], axis=0)
            tall_ref[t, b * 128 : (b + 1) * 128, :] = jnp.transpose(part)
        copies[t].start()
    for b in range(4):
        for chip in range(4):
            wide_ref[0, chip * 64 : (chip + 1) * 64, b * 128 : (b + 1) * 128] = piece(chip, 12 + b)
    copies[3].start()
    for p in range(DOM):
        for b in range(4):
            part = in_ref[p, 256 + b * 16 : 272 + b * 16, :]
            wide_ref[1, p * 16 : (p + 1) * 16, b * 128 : (b + 1) * 128] = part.astype(F32)
    copies[4].start()
    for copy in copies:
        copy.wait()


def tails_of(ref):
    tails = [ref[p, 320:SPREAD, :].astype(F32) for p in range(DOM)]
    return [tail[0:8] + tail[8:16] for tail in tails]


def first_half_body(mine_ref, out_hbm, tall_ref, wide_ref, sems):
    half_body(position()[1], mine_ref, out_hbm, tall_ref, wide_ref, sems)


def second_half_body(before_hbm, mine_ref, other_ref, gain_in_ref, out_hbm, gain_ref, tall_ref, wide_ref, sems):
    gain = jnp.zeros((8, 128), F32)
    mine, through = tails_of(mine_ref), tails_of(other_ref)
    for p in range(DOM):
        gain = gain + mine[p]
        through[p] = through[p] + mine[p]
    for b in range(4):
        part = (through[b] + through[4 + b] + through[8 + b])[4:5]
        lanes = slice(b * 128, (b + 1) * 128)
        gain_ref[:, lanes] = gain[b : b + 1] + part / gain_in_ref[:, lanes]
    half_body(1 - position()[1], other_ref, out_hbm, tall_ref, wide_ref, sems)


def in_halves(mine, other, gain_row):
    vmem, hbm = pl.BlockSpec(memory_space=pltpu.VMEM), pl.BlockSpec(memory_space=pltpu.HBM)
    scratch = [pltpu.VMEM((3, D, 256), F32), pltpu.VMEM((2, 256, D), F32), pltpu.SemaphoreType.DMA((5,))]
    half = pl.pallas_call(
        first_half_body, out_shape=shape((5, D, D), F32), in_specs=[vmem], out_specs=hbm, scratch_shapes=scratch,
        cost_estimate=pl.CostEstimate(flops=int(3e9), transcendentals=0, bytes_accessed=1 << 20),
    )(mine)
    return pl.pallas_call(
        second_half_body,
        out_shape=(shape((5, D, D), F32), shape((1, D), F32)),
        in_specs=[hbm, vmem, vmem, vmem],
        out_specs=(hbm, vmem),
        input_output_aliases={0: 0},
        scratch_shapes=scratch,
    )(half, mine, other, gain_row)


def chip_shift(step, swap):
    return [(z * 2 + c, ((z + step) % 4) * 2 + (c ^ swap)) for z in range(4) for c in range(2)]


def along_chips(array, step):
    return lax.ppermute(array, "blk", chip_shift(step, 0))


def other_core(array):
    return lax.ppermute(array, "blk", chip_shift(0, 1))


def to_dom_peers(array):
    return lax.all_to_all(array, "dom", split_axis=0, concat_axis=0, tiled=True)


def local(
    x, gain, wq, wk, wv, wo, wm, cluster, pattern, send_rows, send_counts, edge_src, edge_dst, out_grad
):
    gain_row = gain.reshape(1, D)
    pay, outgoing = call(
        norm_body,
        (shape((PAY, D), BF16), shape((DOM, CAP, D), BF16)),
        (pattern, send_counts, x, gain_row, cluster.reshape(1, ROWS), out_grad, send_rows),
        scalars=2,
        micros=4,
    )
    incoming = to_dom_peers(outgoing)
    near, far = along_chips(pay, 1), along_chips(pay, 3)

    counts_t, degree, slot_grads, wqkv, wo_head = call(
        edges_body,
        (
            shape((1024, 512), BF16), shape((ROWS, 128), F32), shape((DOM, CAP, D), BF16),
            shape((192, D), BF16), shape((HEAD, D), BF16),
        ),
        (edge_src.reshape(32, 128), edge_dst.reshape(32, 128), out_grad, wm, wq, wk, wv, wo),
        scratch=[pltpu.VMEM((512, 1024), F32)],
        micros=10,
    )
    near, far, degree = lax.optimization_barrier((near, far, degree))
    pays = [pay, near, along_chips(near[0:ROWS], 1), along_chips(far[ROWS:PAY], 3), far]
    pays = pays + [other_core(part) for part in pays]
    slot_grads = lax.optimization_barrier((incoming, slot_grads))[1]
    back = to_dom_peers(slot_grads)

    base, mine, other = call(
        mean_body,
        (shape((ROWS, D), F32), shape((DOM, 64, 128), BF16), shape((DOM, 64, 128), BF16)),
        (counts_t, degree, incoming, x, out_grad, wm),
        micros=4,
    )

    pay_a, pay_b, chunks = call(
        attention_body,
        (*[shape((4, ROWS, 256), BF16)] * 2, shape((DOM, 128, 128), BF16)),
        (*pays, wqkv, wo_head, mine, other_core(other)),
        scratch=[
            pltpu.VMEM((BLK, 128, ROWS), F32),
            pltpu.VMEM((BLK, 8, ROWS), F32),
            pltpu.VMEM((BLK, 128, ROWS), BF16),
            pltpu.VMEM((BLK, HEAD, ROWS), BF16),
            pltpu.VMEM((BLK, ROWS, 128), BF16),
            pltpu.VMEM((BLK, ROWS, 128), BF16),
            pltpu.VMEM((BLK, 80, ROWS), BF16),
            pltpu.VMEM((BLK, BLK, ROWS, ROWS), BF16),
            pltpu.VMEM((BLK, HEAD, ROWS), F32),
            pltpu.VMEM((BLK, HEAD, ROWS), F32),
            pltpu.VMEM((BLK, HEAD, ROWS), F32),
            pltpu.VMEM((BLK, HEAD, ROWS), BF16),
            pltpu.VMEM((BLK, HEAD, ROWS), F32),
            pltpu.VMEM((BLK, BLK, ROWS, ROWS), BF16),
            pltpu.VMEM((BLK, ROWS, 128), BF16),
            pltpu.VMEM((BLK, ROWS, 128), BF16),
        ],
        micros=8,
    )
    chunks = lax.optimization_barrier((chunks, back))[0]
    chunks = to_dom_peers(chunks)
    halo, gain_part, *results = call(
        halo_body,
        (shape((ROWS, D), F32), shape((8, 128), F32), *[shape((2, ROWS, 256), BF16)] * 4),
        (send_counts, back, send_rows, x, pay_a, other_core(pay_b)),
        scalars=1,
        micros=3,
    )
    chunk = call(
        chunk_sum_body,
        shape((CHUNK, 128), BF16),
        (chunks, gain_part, other_core(gain_part), wqkv),
        scratch=[pltpu.VMEM((8, 128), F32)],
        micros=1,
    )
    chunk_parts = [chunk] + [along_chips(chunk, step) for step in (1, 2, 3)]
    spread = call(
        spread_body, shape((DOM, SPREAD, 128), BF16), chunk_parts, scratch=[pltpu.VMEM((4, 80, 128), F32)], micros=1
    )
    spread, *results = lax.optimization_barrier((spread, *results))
    gathered = to_dom_peers(spread)
    results = [results[0]] + [along_chips(results[dz], -dz) for dz in (1, 2, 3)]
    layer_out, feature_grad = call(
        rows_body,
        (shape((ROWS, D), BF16), shape((ROWS, D), BF16)),
        (*results, halo, base, x, gain_row, out_grad, wq, wk, wv, wo),
        scratch=[pltpu.VMEM((4, ROWS, 128), BF16)] * 4 + [pltpu.VMEM((BLK, ROWS, 256), BF16)],
        micros=2,
    )
    gathered, layer_out, feature_grad = lax.optimization_barrier((gathered, layer_out, feature_grad))
    gathered_other = other_core(gathered)
    weight_grads, gain_grad = in_halves(gathered, gathered_other, gain_row)
    return layer_out, feature_grad, weight_grads, gain_grad.reshape(D)


def solution(mesh):
    both = ("dom", "blk")
    placed = (
        P(both, None), P(), P(), P(), P(), P(), P(), P(both), P(both, None), P(both, None), P(both), P(both), P(both),
        P(both, None),
    )
    return jax.shard_map(
        local,
        mesh=mesh,
        in_specs=placed,
        out_specs=(P(both, None), P(both, None), P(), P()),
        check_vma=False,
    )
```
